128 devices in a mesh: rows: 32 (over x, y, core), cols: 4 (over z).
Axes of the slice: x: 4, y: 4, z: 4, core: 2. Of those that a mesh axis runs over, the one named last changes fastest.
Arguments:
- local_weights: bfloat16 [32, 4, 48, 256, 256], P('rows', 'cols'), may hold values from -6 to 6
- local_gains: float32 [32, 4, 48, 2, 256], P('rows', 'cols'), may hold values from 1 to 48
- local_coords: int32 [32, 4, 48, 2], P('rows', 'cols'), may hold values from 0 to 15, as said below
- remote_weights: bfloat16 [32, 4, 32, 256, 256], P('rows', 'cols'), may hold values from -6 to 6
- remote_gains: float32 [32, 4, 32, 2, 256], P('rows', 'cols'), may hold values from 1 to 48
- remote_groups: int32 [32, 4, 32], P('rows', 'cols'), may hold values from 0 to 31, as said below
- remote_coords: int32 [32, 4, 32, 2], P('rows', 'cols'), may hold values from 0 to 15
- start_block: float32 [16, 131072], P(None, 'rows'), may hold values from -20 to 20
Outputs:
- embedding: float32 [16, 131072], P(None, ('rows', 'cols'))
The draws below stay inside these ranges and needn't reach their ends.
Inputs may be any that keep to these rules, and one draw needn't show every extreme that they name: For each [r, c], the row tiles local_coords[r, c, :, 0] take every value 0 to 15. For each [r, c], every group named in remote_groups[r, c, :] is named exactly 2 times; one group is named 2 times in every [r, c].
All inputs are finite; a program needn't handle non-finite values.
Results may differ from the reference program's by a relative error of at most 0.0046.
Values may be sent and summed in bfloat16 or wider, within the bound.
A program may use at most 128 MiB of HBM per device.

```python
import math
import jax
import jax.numpy as jnp
from jax import lax

TILE = 256
WIDTH = 16
BR = 16
LOC = 48
MOST = 2
ITERS = 2
LT = 32
N_ROWS = 32
N_COLS = 4


def draw_remote_groups(key, part):
    hub_group = jax.random.randint(jax.random.fold_in(key, 7), (), 0, N_ROWS)
    sender_keys = jax.random.split(jax.random.fold_in(key, 11), N_ROWS * N_COLS)

    def draw_sender(sender_key):
        key_first, key_second = jax.random.split(sender_key)
        shuffled = jax.random.permutation(key_first, N_ROWS)
        position = jnp.argsort(shuffled)
        position = jnp.where(jnp.arange(N_ROWS) == hub_group, -1, position)
        ordered = jnp.argsort(position)
        slot_order = jax.random.permutation(key_second, LT)
        return ordered[slot_order // MOST]
    return jax.vmap(draw_sender)(sender_keys).reshape(N_ROWS, N_COLS, LT).astype(jnp.int32)


def draw_local_coords(key, part):
    sender_keys = jax.random.split(jax.random.fold_in(key, 13), N_ROWS * N_COLS)

    def draw_sender(sender_key):
        key_first, key_second, key_third, key_fourth = jax.random.split(sender_key, 4)
        covered = jax.random.permutation(key_first, BR).astype(jnp.int32)
        extra_rows = jax.random.randint(key_second, (LOC - BR,), 0, BR).astype(jnp.int32)
        row_tiles = jnp.concatenate([covered, extra_rows])[jax.random.permutation(key_third, LOC)]
        col_tiles = jax.random.randint(key_fourth, (LOC,), 0, BR).astype(jnp.int32)
        return jnp.stack([row_tiles, col_tiles], axis=1)
    return jax.vmap(draw_sender)(sender_keys).reshape(N_ROWS, N_COLS, LOC, 2).astype(jnp.int32)


def gain_draw(key, tile_count):
    shape_full = (N_ROWS, N_COLS, tile_count, 2, TILE)
    uniform_part = jax.random.uniform(key, shape_full, jnp.float32)
    spread = jnp.exp(math.log(10.0) * uniform_part)
    rising = 1.0 + 2.0 * jnp.arange(N_COLS, dtype=jnp.float32) / max(N_COLS - 1, 1)
    row_gain = jnp.arange(2) == 0
    factor = jnp.where(row_gain[None, None, None, :, None], rising[None, :, None, None, None], 1.0)
    return (spread * factor).astype(jnp.float32)


def draw_local_gains(key, part):
    return gain_draw(jax.random.fold_in(key, 17), LOC)


def draw_remote_gains(key, part):
    return gain_draw(jax.random.fold_in(key, 19), LT)


def draw_start_block(key, part):
    vertex_total = N_ROWS * BR * TILE
    group_of = (jnp.arange(vertex_total) // (BR * TILE)).astype(jnp.float32)
    rising = 1.0 + 4.0 * group_of / max(N_ROWS - 1, 1)
    values = jax.random.truncated_normal(jax.random.fold_in(key, 23), -4.0, 4.0, (WIDTH, vertex_total), jnp.float32)
    return (values * rising[None, :]).astype(jnp.float32)


def plant(entries, own_key, least, largest):
    longest = entries.shape.index(max(entries.shape))
    spots = []
    for shift in (0, 1):
        where = [jax.random.randint(jax.random.fold_in(own_key, axis), (), 0, length) for axis, length in enumerate(entries.shape)]
        where[longest] = (where[longest] + shift) % entries.shape[longest]
        spots.append(tuple(where))
    return entries.at[spots[0]].set(least).at[spots[1]].set(largest)


def block_levels(stream_key, shape, cuts, smallest, top_value):
    level = 1.0
    for dim, shards_of in cuts:
        draws = jax.random.uniform(jax.random.fold_in(jax.random.fold_in(stream_key, 6), dim), (shards_of,), jnp.float32, smallest / len(cuts), top_value / len(cuts))
        level = level * jnp.repeat(jnp.exp(draws), shape[dim] // shards_of).reshape((-1,) + (1,) * (len(shape) - 1 - dim))
    return level


def noise(rng, shape, deviation, reach, cuts=(), kind=jnp.bfloat16):
    factor_of = block_levels(rng, shape, cuts, -0.22, 0.18) if cuts else 1.0
    array = jax.random.normal(rng, shape, jnp.float32) * deviation * factor_of
    return jnp.minimum(jnp.maximum(array, -reach), reach).astype(kind)


def setup_inputs(seed: int = 0) -> dict:
    seeds = jax.random.split(jax.random.key(seed), 9)
    local_weights = noise(seeds[0], (N_ROWS, N_COLS, LOC, TILE, TILE), 1.0, 6.0, ((0, 32), (1, 4)))
    local_gains = draw_local_gains(jax.random.fold_in(seeds[8], 71), 0)
    local_coords = draw_local_coords(jax.random.fold_in(seeds[8], 71), 0)
    remote_weights = noise(seeds[3], (N_ROWS, N_COLS, LT, TILE, TILE), 1.0, 6.0, ((0, 32), (1, 4)))
    remote_gains = draw_remote_gains(jax.random.fold_in(seeds[8], 71), 0)
    remote_groups = draw_remote_groups(jax.random.fold_in(seeds[8], 71), 0)
    remote_coords = plant(jax.random.randint(seeds[6], (N_ROWS, N_COLS, LT, 2), 0, BR), jax.random.fold_in(seeds[6], 1), 0, BR - 1).astype(jnp.int32)
    start_block = draw_start_block(jax.random.fold_in(seeds[8], 71), 0)
    return dict(local_weights=local_weights, local_gains=local_gains, local_coords=local_coords, remote_weights=remote_weights, remote_gains=remote_gains, remote_groups=remote_groups, remote_coords=remote_coords, start_block=start_block)


def dequantize(weights, gain_pair):
    return (gain_pair[:, 0, :, None] * weights.astype(jnp.float32) * gain_pair[:, 1, None, :]).astype(jnp.bfloat16)

def reference(local_weights, local_gains, local_coords, remote_weights, remote_gains, remote_groups, remote_coords, start_block):
    devices = N_ROWS * N_COLS
    tile_total = N_ROWS * BR
    vertices = tile_total * TILE
    dev_row = (jnp.arange(devices, dtype=jnp.int32) // N_COLS).astype(jnp.int32)
    local_pairs = local_coords.reshape(devices, LOC, 2).astype(jnp.int32)
    remote_pairs = remote_coords.reshape(devices, LT, 2).astype(jnp.int32)
    local_set = (local_weights.reshape(devices, LOC, TILE, TILE), local_gains.reshape(devices, LOC, 2, TILE), (dev_row[:, None] * BR + local_pairs[:, :, 0]).astype(jnp.int32), (dev_row[:, None] * BR + local_pairs[:, :, 1]).astype(jnp.int32))
    remote_set = (remote_weights.reshape(devices, LT, TILE, TILE), remote_gains.reshape(devices, LT, 2, TILE), (dev_row[:, None] * BR + remote_pairs[:, :, 0]).astype(jnp.int32), (remote_groups.reshape(devices, LT).astype(jnp.int32) * BR + remote_pairs[:, :, 1]).astype(jnp.int32))
    both_sets = (local_set, remote_set)

    def degree_step(summed, pieces):
        weights, gain_pair, row_tiles, col_tiles = pieces
        magnitude = jnp.abs(dequantize(weights, gain_pair).astype(jnp.float32))
        summed = summed.at[row_tiles].add(lax.optimization_barrier(jnp.sum(magnitude, axis=2)))
        summed = summed.at[col_tiles].add(lax.optimization_barrier(jnp.sum(magnitude, axis=1)))
        return (summed, None)
    degree = jnp.zeros((tile_total, TILE), jnp.float32)
    for tile_set in both_sets:
        degree = lax.scan(degree_step, degree, tile_set)[0]
    inv_root = 1.0 / jnp.sqrt(degree)
    vectors = start_block.reshape(WIDTH, tile_total, TILE).transpose(1, 0, 2)
    for iteration in range(ITERS):
        scaled_block = (vectors * inv_root[:, None, :]).astype(jnp.bfloat16)

        def product_step(summed, pieces):
            weights, gain_pair, row_tiles, col_tiles = pieces
            tile_full = dequantize(weights, gain_pair).astype(jnp.float32)
            forward = jnp.einsum('tij,tkj->tki', tile_full, scaled_block[col_tiles].astype(jnp.float32))
            backward = jnp.einsum('tij,tki->tkj', tile_full, scaled_block[row_tiles].astype(jnp.float32))
            summed = summed.at[row_tiles].add(forward)
            summed = summed.at[col_tiles].add(backward)
            return (summed, None)
        image = jnp.zeros((tile_total, WIDTH, TILE), jnp.float32)
        for tile_set in both_sets:
            image = lax.scan(product_step, image, tile_set)[0]
        image = image * inv_root[:, None, :]
        gram = jnp.einsum('bki,bli->kl', image, image, precision=lax.Precision.HIGHEST) / vertices
        factor = jnp.linalg.cholesky(gram)
        inverse = jax.scipy.linalg.solve_triangular(factor, jnp.eye(WIDTH, dtype=jnp.float32), lower=True)
        vectors = jnp.einsum('kl,bli->bki', inverse, image, precision=lax.Precision.HIGHEST)
    return vectors.transpose(1, 0, 2).reshape(WIDTH, vertices)
```

```python
import functools

import jax
import jax.numpy as jnp
from jax import lax
from jax.experimental import pallas as pl
from jax.experimental.pallas import tpu as pltpu
from jax.sharding import PartitionSpec as P

TILE = 256
HALF = 128
WIDTH = 16
BR = 16
MOST = 2
ITERS = 2
LOC = 48
LT = 32
GROUPS = 32
SPLITS = 4
QUARTER = BR // SPLITS
NX, NY, NCORE = 4, 4, 2
CHUNK = 8
VERTICES = GROUPS * BR * TILE
MESH = pl.DeviceIdType.MESH
VMEM = pl.BlockSpec(memory_space=pltpu.VMEM)
SMEM = pl.BlockSpec(memory_space=pltpu.SMEM)
HIGHEST = lax.Precision.HIGHEST


def plane_partner(me, offset):
    core, y, x = me % NCORE, (me // NCORE) % NY, me // (NCORE * NY)
    dc, dy, dx = offset % NCORE, (offset // NCORE) % NY, offset // (NCORE * NY)
    ahead = (((x + dx) % NX) * NY + (y + dy) % NY) * NCORE + (core + dc) % NCORE
    behind = (((x + NX - dx) % NX) * NY + (y + NY - dy) % NY) * NCORE + (core + NCORE - dc) % NCORE
    return ahead, behind


def greet(me, my_split, plane, splits):
    barrier = pltpu.get_barrier_semaphore()
    total = 0
    if plane:

        def signal(offset, carry):
            ahead, _ = plane_partner(me, offset)
            pl.semaphore_signal(barrier, inc=1, device_id=(ahead, my_split), device_id_type=MESH)
            return carry

        lax.fori_loop(1, GROUPS, signal, 0)
        total += GROUPS - 1
    if splits:
        for dz in range(1, SPLITS):
            other = (my_split + dz) % SPLITS
            pl.semaphore_signal(barrier, inc=1, device_id=(me, other), device_id_type=MESH)
        total += SPLITS - 1
    pl.semaphore_wait(barrier, total)


def plane_copy(me, my_split, offset, source, target, send_sem, recv_sem, waiting):
    ahead, behind = plane_partner(me, offset)
    return pltpu.make_async_remote_copy(
        src_ref=source(ahead),
        dst_ref=target(behind if waiting else me),
        send_sem=send_sem.at[offset],
        recv_sem=recv_sem.at[offset],
        device_id=(ahead, my_split),
        device_id_type=MESH,
    )


def plane_exchange(me, my_split, source, target, send_sem, recv_sem):
    def start(offset, carry):
        plane_copy(me, my_split, offset, source, target, send_sem, recv_sem, False).start()
        return carry

    lax.fori_loop(1, GROUPS, start, 0)


def plane_wait(me, my_split, source, target, send_sem, recv_sem):
    def wait(offset, carry):
        plane_copy(me, my_split, offset, source, target, send_sem, recv_sem, True).wait()
        return carry

    lax.fori_loop(1, GROUPS, wait, 0)


def dequantize_kernel(
    local_rows, local_cols, groups, remote_rows, remote_cols,
    local_w, local_g, remote_w, remote_g,
    local_eff, remote_eff, degree_out, message, slots,
    degree, count,
):
    step = pl.program_id(0)
    ones = jnp.ones((8, TILE), jnp.bfloat16)

    @pl.when(step == 0)
    def _():
        degree[...] = jnp.zeros_like(degree)
        message[:, 0:8, :] = jnp.zeros((GROUPS, 8, HALF), jnp.float32)
        message[:, 8:16, :] = jnp.full((GROUPS, 8, HALF), -1.0, jnp.float32)

        def clear(i, carry):
            count[i] = 0
            return carry

        lax.fori_loop(0, GROUPS, clear, 0)

    def scale(weights, gains, out):
        row_gains = jnp.concatenate([gains[t, 0:1, :] for t in range(CHUNK)], axis=0).T
        sums = []
        for t in range(CHUNK):
            eff = (
                row_gains[:, t : t + 1] * weights[t].astype(jnp.float32) * gains[t, 1:2, :]
            ).astype(jnp.bfloat16)
            out[t] = eff
            size = jnp.abs(eff)
            row_sum = lax.dot_general(
                ones, size, (((1,), (1,)), ((), ())), preferred_element_type=jnp.float32
            )
            col_sum = jnp.dot(ones, size, preferred_element_type=jnp.float32)
            sums.append((row_sum, col_sum))
        return sums

    @pl.when(step < LOC // CHUNK)
    def _():
        sums = scale(local_w, local_g, local_eff)
        for t, (row_sum, col_sum) in enumerate(sums):
            tile = step * CHUNK + t
            degree[local_rows[tile]] += row_sum
            degree[local_cols[tile]] += col_sum

    @pl.when(step >= LOC // CHUNK)
    def _():
        sums = scale(remote_w, remote_g, remote_eff)
        for t, (row_sum, col_sum) in enumerate(sums):
            tile = (step - LOC // CHUNK) * CHUNK + t
            degree[remote_rows[tile]] += row_sum
            group = groups[tile]
            rank = count[group]
            count[group] = rank + 1
            slots[tile] = group * MOST + rank
            column = jnp.full((1, HALF), remote_cols[tile].astype(jnp.float32))
            for half in range(2):
                message[group, pl.ds(2 * rank + half, 1), :] = col_sum[
                    0:1, half * HALF : (half + 1) * HALF
                ]
                message[group, pl.ds(8 + 2 * rank + half, 1), :] = column

    @pl.when(step == pl.num_programs(0) - 1)
    def _():
        for j in range(BR):
            for half in range(2):
                degree_out[2 * j + half : 2 * j + half + 1, :] = degree[
                    j, 0:1, half * HALF : (half + 1) * HALF
                ]


def dequantize(local_coords, groups, remote_coords, local_w, local_g, remote_w, remote_g):
    first = LOC // CHUNK
    steps = (LOC + LT) // CHUNK
    local_block = lambda i, *_: (jnp.minimum(i, first - 1), 0, 0)
    remote_block = lambda i, *_: (jnp.maximum(i - first, 0), 0, 0)
    whole = lambda rank: (lambda i, *_: (0,) * rank)
    return pl.pallas_call(
        dequantize_kernel,
        out_shape=(
            jax.ShapeDtypeStruct((LOC, TILE, TILE), jnp.bfloat16),
            jax.ShapeDtypeStruct((LT, TILE, TILE), jnp.bfloat16),
            jax.ShapeDtypeStruct((2 * BR, HALF), jnp.float32),
            jax.ShapeDtypeStruct((GROUPS, 16, HALF), jnp.float32),
            jax.ShapeDtypeStruct((LT,), jnp.int32),
        ),
        grid_spec=pltpu.PrefetchScalarGridSpec(
            num_scalar_prefetch=5,
            grid=(steps,),
            in_specs=[
                pl.BlockSpec((CHUNK, TILE, TILE), local_block),
                pl.BlockSpec((CHUNK, 2, TILE), local_block),
                pl.BlockSpec((CHUNK, TILE, TILE), remote_block),
                pl.BlockSpec((CHUNK, 2, TILE), remote_block),
            ],
            out_specs=(
                pl.BlockSpec((CHUNK, TILE, TILE), local_block),
                pl.BlockSpec((CHUNK, TILE, TILE), remote_block),
                pl.BlockSpec((2 * BR, HALF), whole(2)),
                pl.BlockSpec((GROUPS, 16, HALF), whole(3)),
                SMEM,
            ),
            scratch_shapes=[
                pltpu.VMEM((BR, 8, TILE), jnp.float32),
                pltpu.SMEM((GROUPS,), jnp.int32),
            ],
        ),
        compiler_params=pltpu.CompilerParams(vmem_limit_bytes=40 << 20),
        name="dequantize",
    )(
        local_coords[:, 0], local_coords[:, 1], groups, remote_coords[:, 0], remote_coords[:, 1],
        local_w, local_g, remote_w, remote_g,
    )


def degree_kernel(
    message, degree_in, start, inv_out, column_out, block_out,
    arrived, split_part, send_sem, recv_sem, zsend_sem, zrecv_sem, own_sem,
):
    me, my_split = lax.axis_index("rows"), lax.axis_index("cols")
    greet(me, my_split, True, True)
    source, target = (lambda p: message.at[p]), (lambda p: arrived.at[p])
    own = pltpu.make_async_copy(message.at[me], arrived.at[me], own_sem)
    own.start()
    plane_exchange(me, my_split, source, target, send_sem, recv_sem)
    own.wait()
    plane_wait(me, my_split, source, target, send_sem, recv_sem)
    columns = arrived[:, 8:16, :].reshape(GROUPS * 8, HALF)
    column_out[...] = columns
    sums = arrived[:, 0:8, :].reshape(GROUPS * 8, HALF)
    row = lax.broadcasted_iota(jnp.int32, (GROUPS * 8, HALF), 0)
    lane = lax.broadcasted_iota(jnp.int32, (GROUPS * 8, HALF), 1)
    chosen = (columns == (lane // 2).astype(jnp.float32)) & (row % 2 == lane % 2)
    added = lax.dot_general(
        jnp.where(chosen, 1.0, 0.0).astype(jnp.float32),
        sums,
        (((0,), (0,)), ((), ())),
        precision=HIGHEST,
        preferred_element_type=jnp.float32,
    )
    split_part[my_split] = degree_in[...] + added[0 : 2 * BR, :]
    copies = []
    for dz in range(1, SPLITS):
        other = (my_split + dz) % SPLITS
        copy = pltpu.make_async_remote_copy(
            src_ref=split_part.at[my_split],
            dst_ref=split_part.at[my_split],
            send_sem=zsend_sem.at[dz],
            recv_sem=zrecv_sem.at[dz],
            device_id=(me, other),
            device_id_type=MESH,
        )
        copy.start()
        copies.append(copy)
    for dz, copy in enumerate(copies, 1):
        copy.wait_send()
        before = (my_split + SPLITS - dz) % SPLITS
        pltpu.make_async_remote_copy(
            src_ref=split_part.at[my_split],
            dst_ref=split_part.at[before],
            send_sem=zsend_sem.at[dz],
            recv_sem=zrecv_sem.at[dz],
            device_id=(me, before),
            device_id_type=MESH,
        ).wait_recv()
    degree = split_part[0] + split_part[1] + split_part[2] + split_part[3]
    inv_root = 1.0 / jnp.sqrt(degree)
    inv_out[...] = inv_root
    for k in range(2 * BR):
        block_out[k // 2, :, (k % 2) * HALF : (k % 2 + 1) * HALF] = (
            start[:, k * HALF : (k + 1) * HALF] * inv_root[k : k + 1, :]
        ).astype(jnp.bfloat16)


def degree_exchange(message, degree, start):
    return pl.pallas_call(
        degree_kernel,
        out_shape=(
            jax.ShapeDtypeStruct((2 * BR, HALF), jnp.float32),
            jax.ShapeDtypeStruct((GROUPS * 8, HALF), jnp.float32),
            jax.ShapeDtypeStruct((BR, WIDTH, TILE), jnp.bfloat16),
        ),
        in_specs=[VMEM] * 3,
        out_specs=(VMEM,) * 3,
        scratch_shapes=[
            pltpu.VMEM((GROUPS, 16, HALF), jnp.float32),
            pltpu.VMEM((SPLITS, 2 * BR, HALF), jnp.float32),
            pltpu.SemaphoreType.DMA((GROUPS,)),
            pltpu.SemaphoreType.DMA((GROUPS,)),
            pltpu.SemaphoreType.DMA((SPLITS,)),
            pltpu.SemaphoreType.DMA((SPLITS,)),
            pltpu.SemaphoreType.DMA,
        ],
        compiler_params=pltpu.CompilerParams(
            collective_id=0, has_side_effects=True, vmem_limit_bytes=32 << 20
        ),
        name="degree_exchange",
    )(message, degree, start)


def message_kernel(slots, remote_rows, columns, block, remote_eff, message):
    step = pl.program_id(0)

    @pl.when(step == 0)
    def _():
        def answer(slot, carry):
            column = columns[slot]

            @pl.when(column >= 0)
            def _():
                message[slot // MOST, slot % MOST] = block[column]

            return carry

        lax.fori_loop(0, GROUPS * MOST, answer, 0, unroll=8)

    for t in range(CHUNK):
        tile = step * CHUNK + t
        product = jnp.dot(
            block[remote_rows[tile]], remote_eff[t], preferred_element_type=jnp.float32
        )
        slot = slots[tile]
        message[slot // MOST, MOST + slot % MOST] = product.astype(jnp.bfloat16)


def make_message(slots, remote_rows, columns, block, remote_eff):
    return pl.pallas_call(
        message_kernel,
        out_shape=jax.ShapeDtypeStruct((GROUPS, 2 * MOST, WIDTH, TILE), jnp.bfloat16),
        grid_spec=pltpu.PrefetchScalarGridSpec(
            num_scalar_prefetch=3,
            grid=(LT // CHUNK,),
            in_specs=[
                pl.BlockSpec((BR, WIDTH, TILE), lambda i, *_: (0, 0, 0)),
                pl.BlockSpec((CHUNK, TILE, TILE), lambda i, *_: (i, 0, 0)),
            ],
            out_specs=pl.BlockSpec((GROUPS, 2 * MOST, WIDTH, TILE), lambda i, *_: (0, 0, 0, 0)),
        ),
        compiler_params=pltpu.CompilerParams(vmem_limit_bytes=32 << 20),
        name="make_message",
    )(slots, remote_rows, columns, block, remote_eff)


def exchange_kernel(message, arrived, send_sem, recv_sem, own_sem):
    me, my_split = lax.axis_index("rows"), lax.axis_index("cols")
    greet(me, my_split, True, False)
    source, target = (lambda p: message.at[p]), (lambda p: arrived.at[p])
    plane_exchange(me, my_split, source, target, send_sem, recv_sem)
    own = pltpu.make_async_copy(message.at[me], arrived.at[me], own_sem)
    own.start()
    own.wait()
    plane_wait(me, my_split, source, target, send_sem, recv_sem)


def exchange(message):
    return pl.pallas_call(
        exchange_kernel,
        out_shape=jax.ShapeDtypeStruct(message.shape, message.dtype),
        in_specs=[VMEM],
        out_specs=VMEM,
        scratch_shapes=[
            pltpu.SemaphoreType.DMA((GROUPS,)),
            pltpu.SemaphoreType.DMA((GROUPS,)),
            pltpu.SemaphoreType.DMA,
        ],
        compiler_params=pltpu.CompilerParams(
            collective_id=1, has_side_effects=True, vmem_limit_bytes=32 << 20
        ),
        name="exchange",
    )(message)


def product_kernel(
    local_rows, local_cols, slots, remote_rows, columns, block, local_eff, remote_eff, arrived, total
):
    step = pl.program_id(0)

    @pl.when(step == 0)
    def _():
        total[...] = jnp.zeros_like(total)

    @pl.when(step < LOC // CHUNK)
    def _():
        products = []
        for t in range(CHUNK):
            tile = step * CHUNK + t
            row, col = local_rows[tile], local_cols[tile]
            forward = lax.dot_general(
                block[col], local_eff[t], (((1,), (1,)), ((), ())), preferred_element_type=jnp.float32
            )
            backward = jnp.dot(block[row], local_eff[t], preferred_element_type=jnp.float32)
            products.append((row, forward))
            products.append((col, backward))
        for where, product in products:
            total[where] += product

    @pl.when(step >= LOC // CHUNK)
    def _():
        products = []
        for t in range(CHUNK):
            tile = (step - LOC // CHUNK) * CHUNK + t
            slot = slots[tile]
            forward = lax.dot_general(
                arrived[slot // MOST, slot % MOST],
                remote_eff[t],
                (((1,), (1,)), ((), ())),
                preferred_element_type=jnp.float32,
            )
            products.append((remote_rows[tile], forward))
        for where, product in products:
            total[where] += product

    @pl.when(step == pl.num_programs(0) - 1)
    def _():
        def add(slot, carry):
            column = columns[slot]

            @pl.when(column >= 0)
            def _():
                total[column] += arrived[slot // MOST, MOST + slot % MOST].astype(jnp.float32)

            return carry

        lax.fori_loop(0, GROUPS * MOST, add, 0, unroll=8)


def products(local_coords, slots, remote_rows, columns, block, local_eff, remote_eff, arrived):
    first = LOC // CHUNK
    return pl.pallas_call(
        product_kernel,
        out_shape=jax.ShapeDtypeStruct((BR, WIDTH, TILE), jnp.float32),
        grid_spec=pltpu.PrefetchScalarGridSpec(
            num_scalar_prefetch=5,
            grid=((LOC + LT) // CHUNK,),
            in_specs=[
                pl.BlockSpec((BR, WIDTH, TILE), lambda i, *_: (0, 0, 0)),
                pl.BlockSpec((CHUNK, TILE, TILE), lambda i, *_: (jnp.minimum(i, first - 1), 0, 0)),
                pl.BlockSpec((CHUNK, TILE, TILE), lambda i, *_: (jnp.maximum(i - first, 0), 0, 0)),
                pl.BlockSpec((GROUPS, 2 * MOST, WIDTH, TILE), lambda i, *_: (0, 0, 0, 0)),
            ],
            out_specs=pl.BlockSpec((BR, WIDTH, TILE), lambda i, *_: (0, 0, 0)),
        ),
        compiler_params=pltpu.CompilerParams(vmem_limit_bytes=40 << 20),
        name="products",
    )(
        local_coords[:, 0], local_coords[:, 1], slots, remote_rows, columns,
        block, local_eff, remote_eff, arrived,
    )


def factor_inverse(gram):
    row = lax.broadcasted_iota(jnp.int32, (WIDTH, HALF), 0)
    lane = lax.broadcasted_iota(jnp.int32, (WIDTH, HALF), 1)
    work = jnp.where(lane == row + WIDTH, 1.0, jnp.where(lane < WIDTH, gram, 0.0))
    roots = jnp.zeros((WIDTH, HALF), jnp.float32)
    for k in range(WIDTH):
        pivot_row = jnp.broadcast_to(work[k : k + 1, :], (WIDTH, HALF))
        column = jnp.broadcast_to(work[:, k : k + 1], (WIDTH, HALF))
        pivot = jnp.broadcast_to(work[k : k + 1, k : k + 1], (WIDTH, HALF))
        roots = jnp.where(row == k, 1.0 / jnp.sqrt(pivot), roots)
        work = work - jnp.where(row > k, column / pivot, 0.0) * pivot_row
    return (work * roots)[:, WIDTH : 2 * WIDTH]


def split_copy(me, my_split, dz, source, target, send_sem, recv_sem):
    other = (my_split + dz) % SPLITS
    return pltpu.make_async_remote_copy(
        src_ref=source,
        dst_ref=target,
        send_sem=send_sem.at[dz],
        recv_sem=recv_sem.at[dz],
        device_id=(me, other),
        device_id_type=MESH,
    )


def normalize_kernel(
    last, total, inv, out,
    parts, image, split_gram, plane_gram,
    send_sem, recv_sem, rsend_sem, rrecv_sem, gsend_sem, grecv_sem,
):
    me, my_split = lax.axis_index("rows"), lax.axis_index("cols")
    greet(me, my_split, True, True)
    for dz in range(1, SPLITS):
        other = (my_split + dz) % SPLITS
        split_copy(
            me, my_split, dz, total.at[pl.ds(other * QUARTER, QUARTER)], parts.at[dz], rsend_sem, rrecv_sem
        ).start()
    mine = pl.ds(my_split * QUARTER, QUARTER)
    summed = total[mine]
    for dz in range(1, SPLITS):
        other = (my_split + dz) % SPLITS
        split_copy(
            me, my_split, dz, total.at[pl.ds(other * QUARTER, QUARTER)], parts.at[dz], rsend_sem, rrecv_sem
        ).wait()
        summed = summed + parts[dz]
    my_inv = inv[pl.ds(my_split * (2 * QUARTER), 2 * QUARTER), :]
    for k in range(2 * QUARTER):
        half = slice((k % 2) * HALF, (k % 2 + 1) * HALF)
        image[my_split * QUARTER + k // 2, :, half] = summed[k // 2, :, half] * my_inv[k : k + 1, :]

    def gram_of(tile):
        return lax.dot_general(
            tile, tile, (((1,), (1,)), ((), ())), precision=HIGHEST, preferred_element_type=jnp.float32
        )

    if last:
        gram = jnp.zeros((WIDTH, WIDTH), jnp.float32)
        for j in range(QUARTER):
            gram = gram + gram_of(image[my_split * QUARTER + j])
        split_gram[my_split, :, 0:WIDTH] = gram
        for dz in range(1, SPLITS):
            split_copy(
                me, my_split, dz, split_gram.at[my_split], split_gram.at[my_split], gsend_sem, grecv_sem
            ).start()
        for dz in range(1, SPLITS):
            before = (my_split + SPLITS - dz) % SPLITS
            split_copy(
                me, my_split, dz, split_gram.at[my_split], split_gram.at[before], gsend_sem, grecv_sem
            ).wait()
        gram = split_gram[0] + split_gram[1] + split_gram[2] + split_gram[3]
        plane_gram[me] = gram
    else:
        for dz in range(1, SPLITS):
            split_copy(
                me, my_split, dz, image.at[mine], image.at[mine], gsend_sem, grecv_sem
            ).start()
        for dz in range(1, SPLITS):
            before = (my_split + SPLITS - dz) % SPLITS
            split_copy(
                me, my_split, dz, image.at[mine], image.at[pl.ds(before * QUARTER, QUARTER)], gsend_sem, grecv_sem
            ).wait()
        gram = jnp.zeros((WIDTH, WIDTH), jnp.float32)
        for j in range(BR):
            gram = gram + gram_of(image[j])
        plane_gram[me, :, 0:WIDTH] = gram
    source, target = (lambda p: plane_gram.at[me]), (lambda p: plane_gram.at[p])
    plane_exchange(me, my_split, source, target, send_sem, recv_sem)
    plane_wait(me, my_split, source, target, send_sem, recv_sem)
    gram = plane_gram[0]
    for p in range(1, GROUPS):
        gram = gram + plane_gram[p]
    inverse = factor_inverse(gram / VERTICES)
    if last:
        for j in range(QUARTER):
            out[:, j * TILE : (j + 1) * TILE] = jnp.dot(
                inverse, image[my_split * QUARTER + j], precision=HIGHEST, preferred_element_type=jnp.float32
            )
    else:
        for j in range(BR):
            vectors = jnp.dot(inverse, image[j], precision=HIGHEST, preferred_element_type=jnp.float32)
            for half in range(2):
                lanes = slice(half * HALF, (half + 1) * HALF)
                out[j, :, lanes] = (vectors[:, lanes] * inv[2 * j + half : 2 * j + half + 1, :]).astype(
                    jnp.bfloat16
                )


def normalize(total, inv, last):
    if last:
        out = jax.ShapeDtypeStruct((WIDTH, QUARTER * TILE), jnp.float32)
    else:
        out = jax.ShapeDtypeStruct((BR, WIDTH, TILE), jnp.bfloat16)
    return pl.pallas_call(
        functools.partial(normalize_kernel, last),
        out_shape=out,
        in_specs=[VMEM] * 2,
        out_specs=VMEM,
        scratch_shapes=[
            pltpu.VMEM((SPLITS, QUARTER, WIDTH, TILE), jnp.float32),
            pltpu.VMEM((BR, WIDTH, TILE), jnp.float32),
            pltpu.VMEM((SPLITS, WIDTH, HALF), jnp.float32),
            pltpu.VMEM((GROUPS, WIDTH, HALF), jnp.float32),
        ]
        + [pltpu.SemaphoreType.DMA((GROUPS,))] * 2
        + [pltpu.SemaphoreType.DMA((SPLITS,))] * 4,
        compiler_params=pltpu.CompilerParams(
            collective_id=3 if last else 2, has_side_effects=True, vmem_limit_bytes=32 << 20
        ),
        name="normalize_last" if last else "normalize",
    )(total, inv)


def per_device(
    local_weights, local_gains, local_coords, remote_weights, remote_gains, remote_groups, remote_coords, start_block
):
    local_coords = local_coords[0, 0]
    remote_coords = remote_coords[0, 0]
    local_eff, remote_eff, degree, message, slots = dequantize(
        local_coords, remote_groups[0, 0], remote_coords,
        local_weights[0, 0], local_gains[0, 0], remote_weights[0, 0], remote_gains[0, 0],
    )
    inv, columns, block = degree_exchange(message, degree, start_block)
    columns = columns.reshape(GROUPS, 8, HALF)[:, 0 : 2 * MOST : 2, 0].reshape(GROUPS * MOST).astype(jnp.int32)
    remote_rows = remote_coords[:, 0]
    for iteration in range(ITERS):
        outgoing = make_message(slots, remote_rows, columns, block, remote_eff)
        arrived = exchange(outgoing)
        total = products(local_coords, slots, remote_rows, columns, block, local_eff, remote_eff, arrived)
        block = normalize(total, inv, iteration == ITERS - 1)
    return block


def solution(mesh):
    in_specs = (
        P("rows", "cols", None, None, None),
        P("rows", "cols", None, None, None),
        P("rows", "cols", None, None),
        P("rows", "cols", None, None, None),
        P("rows", "cols", None, None, None),
        P("rows", "cols", None),
        P("rows", "cols", None, None),
        P(None, "rows"),
    )
    out_specs = P(None, ("rows", "cols"))
    return jax.shard_map(
        per_device, mesh=mesh, in_specs=in_specs, out_specs=out_specs, check_vma=False
    )
```

```python
import jax
import jax.numpy as jnp
from jax import lax
from jax.experimental import pallas as pl
from jax.experimental.pallas import tpu as pltpu
from jax.sharding import PartitionSpec as P

TILE = 256
HALF = 128
WIDTH = 16
BR = 16
MOST = 2
ITERS = 2
LOC = 48
LT = 32
GROUPS = 32
SPLITS = 4
QROWS = BR // SPLITS * WIDTH
NX, NY, NCORE = 4, 4, 2
CHUNK = 8
STEP = 4
VERTICES = GROUPS * BR * TILE
PAD = BR - 1
MESH = pl.DeviceIdType.MESH
VMEM = pl.BlockSpec(memory_space=pltpu.VMEM)
ANY = pl.BlockSpec(memory_space=pl.ANY)
HIGHEST = lax.Precision.HIGHEST
F32 = jnp.float32
BF16 = jnp.bfloat16

T_REMOTE, T_LOCAL, T_SLOT, T_TILE = 0, LT, LT + LOC, LT + LOC + GROUPS
TABLE = LT + LOC + GROUPS + 8


def dot(a, b, dims=((1,), (0,)), precision=None):
    return lax.dot_general(a, b, (dims, ((), ())), precision=precision, preferred_element_type=F32)


def iota(shape, dim):
    return lax.broadcasted_iota(jnp.int32, shape, dim)


def factor_inverse(gram):
    row, lane = iota((WIDTH, HALF), 0), iota((WIDTH, HALF), 1)
    gram = jnp.concatenate([gram, jnp.zeros((WIDTH, HALF - WIDTH), F32)], axis=1)
    work = jnp.where(lane == row + WIDTH, 1.0, gram)
    roots = jnp.zeros((WIDTH, HALF), F32)
    for k in range(WIDTH):
        pivot_row = jnp.broadcast_to(work[k : k + 1, :], (WIDTH, HALF))
        column = jnp.broadcast_to(work[:, k : k + 1], (WIDTH, HALF))
        pivot = jnp.broadcast_to(work[k : k + 1, k : k + 1], (WIDTH, HALF))
        roots = jnp.where(row == k, 1.0 / jnp.sqrt(pivot), roots)
        work = work - jnp.where(row > k, column / pivot, 0.0) * pivot_row
    return (work * roots)[:, WIDTH : 2 * WIDTH]


class Place:
    def __init__(self):
        self.me, self.z = lax.axis_index("rows"), lax.axis_index("cols")
        self.core = self.me % NCORE
        self.y = (self.me // NCORE) % NY
        self.x = self.me // (NCORE * NY)

    def plane(self, offset, sign=1):
        dc, dy, dx = offset % NCORE, (offset // NCORE) % NY, offset // (NCORE * NY)
        x = (self.x + NX + sign * dx) % NX
        y = (self.y + NY + sign * dy) % NY
        return (x * NY + y) * NCORE + (self.core + NCORE + sign * dc) % NCORE

    def split(self, dz, sign=1):
        return (self.z + SPLITS + sign * dz) % SPLITS

    def near(self, offset, sign=1):
        core = (self.core + NCORE + sign * (offset % NCORE)) % NCORE
        z = self.split(offset // NCORE, sign)
        return self.me - self.core + core, z, z * NCORE + core

    def far(self, offset, sign=1):
        x = (self.x + NX + sign * (offset // NY)) % NX
        y = (self.y + NY + sign * (offset % NY)) % NY
        return (x * NY + y) * NCORE + self.core, self.z, x * NY + y


def copy_to(source, target, send_sem, recv_sem, row, split):
    return pltpu.make_async_remote_copy(
        src_ref=source, dst_ref=target, send_sem=send_sem, recv_sem=recv_sem,
        device_id=(row, split), device_id_type=MESH,
    )


def loop(start, stop, body):
    def step(i, carry):
        body(i)
        return carry

    lax.fori_loop(start, stop, step, 0)


def whole_kernel(
    groups, local_coords, remote_coords, local_gains, remote_gains, start, local_w, remote_w,
    out,
    eff, table_v, table, column_sums, column_of, live, sums, deg_out, deg_in, split_part, inv, spread, gather, row_blocks,
    padded, answer_out, answer_in, product, product_out, product_in, fetched, total,
    parts, image, near_gram, far_gram,
    load_sem, table_sem, deg_send, deg_recv, zdeg_send, zdeg_recv,
    answer_send, answer_recv, product_send, product_recv,
    part_send, part_recv, image_send, image_recv, near_send, near_recv, far_send, far_recv,
):
    at = Place()
    me, z = at.me, at.z
    first = LT // CHUNK
    chunks = (LT + LOC) // CHUNK

    def load(c):
        chunk = pl.ds(c * CHUNK, CHUNK)
        source = remote_w.at[chunk] if c < first else local_w.at[pl.ds((c - first) * CHUNK, CHUNK)]
        return pltpu.make_async_copy(source, eff.at[chunk], load_sem.at[c])

    for c in range(chunks):
        load(c).start()

    barrier = pltpu.get_barrier_semaphore()

    def signal(row, split):
        pl.semaphore_signal(barrier, inc=1, device_id=(row, split), device_id_type=MESH)

    loop(1, GROUPS, lambda o: signal(at.plane(o), z))
    for offset in range(2, NCORE * SPLITS):
        row, split, _ = at.near(offset)
        signal(row, split)

    group = jnp.broadcast_to(groups[...], (GROUPS, LT))
    slot_group, tile_id = iota((GROUPS, LT), 0), iota((GROUPS, LT), 1)
    named = group == slot_group
    lowest = jnp.min(jnp.where(named, tile_id, LT - 1), axis=1, keepdims=True)
    highest = jnp.max(jnp.where(named, tile_id, -1), axis=1, keepdims=True)
    slot = MOST * slot_group + jnp.where(tile_id == highest, 1, 0)
    tile_slot = jnp.sum(jnp.where(named, slot, 0), axis=0, keepdims=True)
    lane = iota((GROUPS, HALF), 1)
    by_slot = jnp.where(lane == 0, lowest, jnp.where(lane == 1, jnp.maximum(highest, 0), highest))
    table_v[...] = jnp.zeros_like(table_v)
    table_v[T_REMOTE : T_REMOTE + LT, 0:2] = remote_coords[...]
    table_v[T_LOCAL : T_LOCAL + LOC, 0:2] = local_coords[...]
    table_v[T_SLOT : T_SLOT + GROUPS, :] = by_slot
    table_v[T_TILE : T_TILE + 1, 0:LT] = tile_slot
    table_copy = pltpu.make_async_copy(table_v, table, table_sem.at[0])
    table_copy.start()
    live[...] = jnp.broadcast_to(highest.astype(F32), (GROUPS, HALF))
    columns = jnp.broadcast_to(remote_coords[:, 1:2].astype(F32), (LT, HALF))
    for t in range(LT):
        column_of[t] = jnp.broadcast_to(columns[t : t + 1, :], (8, HALF))
    padded[...] = jnp.zeros_like(padded)
    fetched[...] = jnp.zeros_like(fetched)
    table_copy.wait()

    def pair(p):
        return pl.ds(MOST * p, MOST)

    ones = jnp.ones((8, TILE), BF16)

    def scale(tile0, gains, gain0, row_at, keep, col_at):
        row_gains = jnp.concatenate([gains[gain0 + t, 0:1, :] for t in range(CHUNK)], axis=0).T
        for t in range(CHUNK):
            scaled = (
                row_gains[:, t : t + 1] * eff[tile0 + t].astype(F32) * gains[gain0 + t, 1:2, :]
            ).astype(BF16)
            eff[tile0 + t] = scaled
            size = jnp.abs(scaled)
            sums[pl.ds(row_at + t, 1), :] = dot(ones, size, ((1,), (1,)))[0:1, :]
            keep(col_at + t, dot(ones, size))

    def remote_chunk(c):
        chunk = pl.ds(c * CHUNK, CHUNK)
        pltpu.make_async_copy(remote_w.at[chunk], eff.at[chunk], load_sem.at[c]).wait()

        def keep(t, value):
            column_sums[t] = value

        scale(c * CHUNK, remote_gains, c * CHUNK, c * CHUNK, keep, c * CHUNK)

    def local_chunk(c):
        pltpu.make_async_copy(
            local_w.at[pl.ds(c * CHUNK, CHUNK)],
            eff.at[pl.ds(LT + c * CHUNK, CHUNK)],
            load_sem.at[first + c],
        ).wait()

        def keep(t, value):
            sums[pl.ds(t, 1), :] = value[0:1, :]

        scale(LT + c * CHUNK, local_gains, c * CHUNK, LT + c * CHUNK, keep, LT + LOC + c * CHUNK)

    loop(0, first, remote_chunk)
    pl.semaphore_wait(barrier, GROUPS - 1 + NCORE * SPLITS - 2)

    def fill_degree(p, ref):
        alive = live[pl.ds(p, 1), :]
        for s in range(MOST):
            tile = table[T_SLOT + p, s]
            row = column_sums[tile]
            for half in range(2):
                ref[p, 2 * s + half : 2 * s + half + 1, :] = row[0:1, half * HALF : (half + 1) * HALF]
            ref[p, 4 + 2 * s : 6 + 2 * s, :] = jnp.where(alive >= 0.0, column_of[tile][0:2, :], -1.0)

    def send_degree(o):
        to = at.plane(o)
        fill_degree(to, deg_out)
        copy_to(deg_out.at[to], deg_in.at[me], deg_send.at[o], deg_recv.at[o], to, z).start()

    loop(1, GROUPS, send_degree)
    fill_degree(me, deg_in)
    loop(0, LOC // CHUNK, local_chunk)

    def wait_degree(o):
        copy_to(
            deg_out.at[at.plane(o)], deg_in.at[at.plane(o, -1)], deg_send.at[o], deg_recv.at[o], at.plane(o), z
        ).wait()

    loop(1, GROUPS, wait_degree)

    lane = iota((HALF, HALF), 1)
    targets = jnp.concatenate(
        [
            jnp.broadcast_to(remote_coords[:, 0:1], (LT, HALF)),
            jnp.broadcast_to(local_coords[:, 0:1], (LOC, HALF)),
            jnp.broadcast_to(local_coords[:, 1:2], (LOC, HALF)),
        ],
        axis=0,
    )
    hot = jnp.where(targets == lane, 1.0, 0.0)
    split_part[z] = dot(hot, sums[...], ((0,), (0,)), HIGHEST)[0:BR, :]
    came = deg_in[...].reshape(GROUPS * 8, HALF)
    column = pltpu.roll(came, GROUPS * 8 - 4, 0)
    row8 = iota((GROUPS * 8, HALF), 0) % 8
    lane_f = iota((GROUPS * 8, HALF), 1).astype(F32)
    for half in range(2):
        chosen = (column == lane_f) & ((row8 == half) | (row8 == 2 + half))
        hot = jnp.where(chosen, 1.0, 0.0)
        split_part[z, :, half * HALF : (half + 1) * HALF] += dot(hot, came, ((0,), (0,)), HIGHEST)[0:BR, :]

    def degree_copy(dz, sign):
        other = at.split(dz, sign)
        return copy_to(
            split_part.at[z], split_part.at[z if sign > 0 else other], zdeg_send.at[dz], zdeg_recv.at[dz], me, other
        )

    for dz in range(1, SPLITS):
        degree_copy(dz, 1).start()

    row = iota((BR * WIDTH, HALF), 0)
    lane = iota((BR * WIDTH, HALF), 1)
    row_tile = (row // WIDTH).astype(F32)
    lanes = iota((1, HALF), 1)
    per = HALF // WIDTH
    for q in range(GROUPS * MOST // per):
        column = jnp.zeros((1, HALF), F32)
        for i in range(per):
            at_slot = deg_in[q * (per // MOST) + i // MOST, 4 + 2 * (i % MOST) : 5 + 2 * (i % MOST), :]
            column = jnp.where(lanes // WIDTH == i, at_slot, column)
        chosen = (jnp.broadcast_to(column, row.shape) == row_tile) & (lane % WIDTH == row % WIDTH)
        spread[:, q * HALF : (q + 1) * HALF] = jnp.where(chosen, 1.0, 0.0).astype(BF16)

    lane = iota((WIDTH, TILE), 1)
    diagonal = lane % WIDTH == iota((WIDTH, TILE), 0)
    lane_tile = (lane // WIDTH).astype(F32)
    for slot in range(GROUPS * MOST):
        own = deg_in[slot // MOST, 4 + 2 * (slot % MOST) : 5 + 2 * (slot % MOST), :]
        own = jnp.broadcast_to(jnp.concatenate([own, own], axis=1), (WIDTH, TILE))
        gather[slot * WIDTH : (slot + 1) * WIDTH, :] = jnp.where(diagonal & (own == lane_tile), 1.0, 0.0).astype(BF16)

    for dz in range(1, SPLITS):
        degree_copy(dz, 1).wait_send()
        degree_copy(dz, -1).wait_recv()
    inv[...] = 1.0 / jnp.sqrt((split_part[0] + split_part[1]) + (split_part[2] + split_part[3]))

    def set_rows(j, vectors):
        scaled = (vectors * inv[j : j + 1, :]).astype(BF16)
        padded[j, PAD] = scaled
        row_blocks[j] = scaled

    for j in range(BR):
        set_rows(j, start[:, j * TILE : (j + 1) * TILE])

    for it in range(ITERS):
        last = it == ITERS - 1
        a_in, p_in = answer_in.at[it], product_in.at[it]

        answer_out[...] = (
            dot(gather[...], row_blocks[...].reshape(BR * WIDTH, TILE)).astype(BF16).reshape(answer_out.shape)
        )

        def send_answer(o):
            to = at.plane(o)
            copy_to(answer_out.at[pair(to)], a_in.at[pair(me)], answer_send.at[it, o], answer_recv.at[it, o], to, z).start()

        loop(1, GROUPS, send_answer)
        a_in[pair(me)] = answer_out[pair(me)]

        def backward(i):
            for u in range(STEP):
                tile = i * STEP + u
                x = row_blocks[table[T_REMOTE + tile, 0]]
                product[tile] = dot(x, eff[tile]).astype(BF16)

        loop(0, LT // STEP, backward)

        def fill_product(p, ref):
            for s in range(MOST):
                ref[MOST * p + s] = product[table[T_SLOT + p, s]]

        def send_product(o):
            to = at.plane(o)
            fill_product(to, product_out)
            copy_to(product_out.at[pair(to)], p_in.at[pair(me)], product_send.at[it, o], product_recv.at[it, o], to, z).start()

        loop(1, GROUPS, send_product)
        fill_product(me, p_in)

        total[...] = jnp.zeros_like(total)

        def window(ref, index, row_tile):
            return ref[index, pl.ds(PAD - row_tile, BR)].reshape(BR * WIDTH, TILE)

        def local(i):
            value = total[...]
            for u in range(STEP):
                tile = i * STEP + u
                r, c = table[T_LOCAL + tile, 0], table[T_LOCAL + tile, 1]
                value += dot(window(padded, c, r), eff[LT + tile], ((1,), (1,)))
                value += dot(window(padded, r, c), eff[LT + tile])
            total[...] = value

        loop(0, LOC // STEP, local)

        def wait_answer(o):
            copy_to(
                answer_out.at[pair(at.plane(o))], a_in.at[pair(at.plane(o, -1))],
                answer_send.at[it, o], answer_recv.at[it, o], at.plane(o), z,
            ).wait()

        loop(1, GROUPS, wait_answer)

        def forward(i):
            value = total[...]
            for u in range(STEP):
                tile = i * STEP + u
                slot = table[T_TILE, tile]
                fetched[u, PAD] = a_in[slot]
                value += dot(window(fetched, u, table[T_REMOTE + tile, 0]), eff[tile], ((1,), (1,)))
            total[...] = value

        loop(0, LT // STEP, forward)

        def wait_product(o):
            copy_to(
                product_out.at[pair(at.plane(o))], p_in.at[pair(at.plane(o, -1))],
                product_send.at[it, o], product_recv.at[it, o], at.plane(o), z,
            ).wait()

        loop(1, GROUPS, wait_product)
        total[...] += dot(spread[...], p_in[...].reshape(GROUPS * MOST * WIDTH, TILE))

        def part_copy(dz):
            other = at.split(dz)
            return copy_to(
                total.at[pl.ds(other * QROWS, QROWS)], parts.at[it, dz],
                part_send.at[it, dz], part_recv.at[it, dz], me, other,
            )

        for dz in range(1, SPLITS):
            part_copy(dz).start()
        mine = pl.ds(z * QROWS, QROWS)
        for dz in range(1, SPLITS):
            part_copy(dz).wait()
        summed = total[mine, :] + ((parts[it, 1] + parts[it, 2]) + parts[it, 3])
        tiles = [
            summed[j * WIDTH : (j + 1) * WIDTH, :] * inv[pl.ds(z * (BR // SPLITS) + j, 1), :]
            for j in range(BR // SPLITS)
        ]
        wide = jnp.concatenate(tiles, axis=1)
        gram = dot(wide, wide, ((1,), (1,)), HIGHEST)
        packed = jnp.concatenate([gram[0:8], gram[8:16], jnp.zeros((8, HALF - 2 * WIDTH), F32)], axis=1)

        def near_copy(offset, sign):
            row, split, slot = at.near(offset, sign)
            own = z * NCORE + at.core
            return copy_to(
                near_gram.at[it, own], near_gram.at[it, own if sign > 0 else slot],
                near_send.at[it, offset], near_recv.at[it, offset], row, split,
            )

        near_gram[it, z * NCORE + at.core] = packed
        for offset in range(1, NCORE * SPLITS):
            near_copy(offset, 1).start()

        def image_copy(dz, sign):
            other = at.split(dz, sign)
            return copy_to(
                image.at[mine], image.at[mine if sign > 0 else pl.ds(other * QROWS, QROWS)],
                image_send.at[dz], image_recv.at[dz], me, other,
            )

        if not last:
            image[mine, :] = jnp.concatenate(tiles, axis=0)
            for dz in range(1, SPLITS):
                image_copy(dz, 1).start()
        for offset in range(1, NCORE * SPLITS):
            near_copy(offset, 1).wait_send()
            near_copy(offset, -1).wait_recv()
        near_sum = near_gram[it, 0]
        for i in range(1, NCORE * SPLITS):
            near_sum = near_sum + near_gram[it, i]

        def far_copy(offset, sign):
            row, split, slot = at.far(offset, sign)
            own = at.x * NY + at.y
            return copy_to(
                far_gram.at[it, own], far_gram.at[it, own if sign > 0 else slot],
                far_send.at[it, offset], far_recv.at[it, offset], row, split,
            )

        far_gram[it, at.x * NY + at.y] = near_sum
        loop(1, NX * NY, lambda o: far_copy(o, 1).start())

        def wait_far(o):
            far_copy(o, 1).wait_send()
            far_copy(o, -1).wait_recv()

        loop(1, NX * NY, wait_far)
        packed = far_gram[it, 0]
        for i in range(1, NX * NY):
            packed = packed + far_gram[it, i]
        gram = jnp.concatenate([packed[:, 0:WIDTH], packed[:, WIDTH : 2 * WIDTH]], axis=0)
        inverse = factor_inverse(gram / VERTICES)
        if last:
            out[...] = dot(inverse, wide, precision=HIGHEST)
        else:
            for dz in range(1, SPLITS):
                image_copy(dz, 1).wait_send()
                image_copy(dz, -1).wait_recv()
            for j in range(BR):
                vectors = dot(inverse, image[j * WIDTH : (j + 1) * WIDTH, :], precision=HIGHEST)
                set_rows(j, vectors)


def per_device(
    local_weights, local_gains, local_coords, remote_weights, remote_gains, remote_groups, remote_coords, start_block
):
    dma = pltpu.SemaphoreType.DMA
    return pl.pallas_call(
        whole_kernel,
        out_shape=jax.ShapeDtypeStruct((WIDTH, QROWS // WIDTH * TILE), F32),
        in_specs=[VMEM] * 6 + [ANY] * 2,
        out_specs=VMEM,
        scratch_shapes=[
            pltpu.VMEM((LT + LOC, TILE, TILE), BF16),
            pltpu.VMEM((TABLE, HALF), jnp.int32),
            pltpu.SMEM((TABLE, HALF), jnp.int32),
            pltpu.VMEM((LT, 8, TILE), F32),
            pltpu.VMEM((LT, 8, HALF), F32),
            pltpu.VMEM((GROUPS, HALF), F32),
            pltpu.VMEM((LT + 2 * LOC, TILE), F32),
            pltpu.VMEM((GROUPS, 8, HALF), F32),
            pltpu.VMEM((GROUPS, 8, HALF), F32),
            pltpu.VMEM((SPLITS, BR, TILE), F32),
            pltpu.VMEM((BR, TILE), F32),
            pltpu.VMEM((BR * WIDTH, GROUPS * MOST * WIDTH), BF16),
            pltpu.VMEM((GROUPS * MOST * WIDTH, BR * WIDTH), BF16),
            pltpu.VMEM((BR, WIDTH, TILE), BF16),
            pltpu.VMEM((BR, 2 * PAD + 1, WIDTH, TILE), BF16),
            pltpu.VMEM((GROUPS * MOST, WIDTH, TILE), BF16),
            pltpu.VMEM((ITERS, GROUPS * MOST, WIDTH, TILE), BF16),
            pltpu.VMEM((LT, WIDTH, TILE), BF16),
            pltpu.VMEM((GROUPS * MOST, WIDTH, TILE), BF16),
            pltpu.VMEM((ITERS, GROUPS * MOST, WIDTH, TILE), BF16),
            pltpu.VMEM((STEP, 2 * PAD + 1, WIDTH, TILE), BF16),
            pltpu.VMEM((BR * WIDTH, TILE), F32),
            pltpu.VMEM((ITERS, SPLITS, QROWS, TILE), F32),
            pltpu.VMEM((BR * WIDTH, TILE), F32),
            pltpu.VMEM((ITERS, NCORE * SPLITS, 8, HALF), F32),
            pltpu.VMEM((ITERS, NX * NY, 8, HALF), F32),
            dma(((LT + LOC) // CHUNK,)),
            dma((1,)),
            dma((GROUPS,)),
            dma((GROUPS,)),
            dma((SPLITS,)),
            dma((SPLITS,)),
            dma((ITERS, GROUPS)),
            dma((ITERS, GROUPS)),
            dma((ITERS, GROUPS)),
            dma((ITERS, GROUPS)),
            dma((ITERS, SPLITS)),
            dma((ITERS, SPLITS)),
            dma((SPLITS,)),
            dma((SPLITS,)),
            dma((ITERS, NCORE * SPLITS)),
            dma((ITERS, NCORE * SPLITS)),
            dma((ITERS, NX * NY)),
            dma((ITERS, NX * NY)),
        ],
        compiler_params=pltpu.CompilerParams(
            collective_id=0, has_side_effects=True, vmem_limit_bytes=48 << 20
        ),
        name="iterate",
    )(
        remote_groups[0], local_coords[0, 0], remote_coords[0, 0], local_gains[0, 0], remote_gains[0, 0],
        start_block, local_weights[0, 0], remote_weights[0, 0],
    )


def solution(mesh):
    in_specs = (
        P("rows", "cols", None, None, None),
        P("rows", "cols", None, None, None),
        P("rows", "cols", None, None),
        P("rows", "cols", None, None, None),
        P("rows", "cols", None, None, None),
        P("rows", "cols", None),
        P("rows", "cols", None, None),
        P(None, "rows"),
    )
    out_specs = P(None, ("rows", "cols"))
    return jax.shard_map(
        per_device, mesh=mesh, in_specs=in_specs, out_specs=out_specs, check_vma=False
    )
```

```python
import jax
import jax.numpy as jnp
from jax import lax
from jax.experimental import pallas as pl
from jax.experimental.pallas import tpu as pltpu
from jax.sharding import PartitionSpec as P

TILE = 256
HALF = 128
WIDTH = 16
BR = 16
MOST = 2
ITERS = 2
LOC = 48
LT = 32
GROUPS = 32
SPLITS = 4
QROWS = BR // SPLITS * WIDTH
NX, NY, NCORE = 4, 4, 2
CHUNK = 8
STEP = 4
VERTICES = GROUPS * BR * TILE
PAD = BR - 1
MESH = pl.DeviceIdType.MESH
VMEM = pl.BlockSpec(memory_space=pltpu.VMEM)
F32 = jnp.float32
BF16 = jnp.bfloat16

HBM = pl.BlockSpec(memory_space=pltpu.HBM)
T_REMOTE_ROW, T_REMOTE_COL, T_LOCAL_ROW, T_LOCAL_COL, T_SLOT, T_FIRST = range(6)
LEFT, RIGHT = (0, 0, 1, 0, 1, 2), (0, 1, 0, 2, 1, 0)


def dot(a, b, dims=((1,), (0,))):
    return lax.dot_general(a, b, (dims, ((), ())), preferred_element_type=F32)


def split3(value):
    high = value.astype(BF16)
    rest = value - high.astype(F32)
    middle = rest.astype(BF16)
    return high, middle, (rest - middle.astype(F32)).astype(BF16)


def select_sum(hot, value, dims=((1,), (0,))):
    high, middle, low = split3(value)
    return dot(hot, high, dims) + (dot(hot, middle, dims) + dot(hot, low, dims))


def iota(shape, dim):
    return lax.broadcasted_iota(jnp.int32, shape, dim)


def factor_inverse(gram):
    copies = len(LEFT) * WIDTH
    row, lane = iota((WIDTH, HALF), 0), iota((WIDTH, HALF), 1)
    gram = jnp.concatenate([jnp.zeros((WIDTH, copies), F32), gram, jnp.zeros((WIDTH, HALF - copies - WIDTH), F32)], axis=1)
    work = jnp.where((lane % WIDTH == row) & (lane < copies), 1.0, gram)
    roots = jnp.zeros((WIDTH, HALF), F32)
    for k in range(WIDTH):
        at = copies + k
        pivot_row = jnp.broadcast_to(work[k : k + 1, :], (WIDTH, HALF))
        column = jnp.broadcast_to(work[:, at : at + 1], (WIDTH, HALF))
        pivot = jnp.broadcast_to(work[k : k + 1, at : at + 1], (WIDTH, HALF))
        roots = jnp.where(row == k, 1.0 / jnp.sqrt(pivot), roots)
        work = work - jnp.where(row > k, column / pivot, 0.0) * pivot_row
    inverse = work * roots
    high, middle, low = (part.astype(F32) for part in split3(inverse))
    part = lane // WIDTH
    chosen = jnp.where((part == 2) | (part == 4), middle, jnp.where(part == 5, low, high))
    return chosen.astype(BF16)[:, 0:copies]


class Place:
    def __init__(self):
        self.me, self.z = lax.axis_index("rows"), lax.axis_index("cols")
        self.core = self.me % NCORE
        self.y = (self.me // NCORE) % NY
        self.x = self.me // (NCORE * NY)

    def plane(self, offset, sign=1):
        dc, dy, dx = offset % NCORE, (offset // NCORE) % NY, offset // (NCORE * NY)
        x = (self.x + NX + sign * dx) % NX
        y = (self.y + NY + sign * dy) % NY
        return (x * NY + y) * NCORE + (self.core + NCORE + sign * dc) % NCORE

    def split(self, dz, sign=1):
        return (self.z + SPLITS + sign * dz) % SPLITS

    def near(self, offset, sign=1):
        core = (self.core + NCORE + sign * (offset % NCORE)) % NCORE
        z = self.split(offset // NCORE, sign)
        return self.me - self.core + core, z, z * NCORE + core

    def far(self, offset, sign=1):
        x = (self.x + NX + sign * (offset // NY)) % NX
        y = (self.y + NY + sign * (offset % NY)) % NY
        return (x * NY + y) * NCORE + self.core, self.z, x * NY + y


def copy_to(source, target, send_sem, recv_sem, row, split):
    return pltpu.make_async_remote_copy(
        src_ref=source, dst_ref=target, send_sem=send_sem, recv_sem=recv_sem,
        device_id=(row, split), device_id_type=MESH,
    )


def wait_all(ref, send_sem, recv_sem, place):
    copy_to(ref, ref, send_sem, recv_sem, place.me, place.z).wait()


def loop(start, stop, body):
    def step(i, carry):
        body(i)
        return carry

    lax.fori_loop(start, stop, step, 0)


def whole_kernel(
    groups_h, local_coords_h, remote_coords_h, local_gains_h, remote_gains_h, start_h, local_w, remote_w,
    out,
    groups, local_coords, remote_coords, local_gains, remote_gains, start,
    eff, table_v, table, column_sums, sums, deg_out, deg_in, split_part, inv, spread, gather, row_blocks,
    padded, answer_out, answer_in, product, product_out, product_in, fetched, total,
    parts, image, image_parts, near_gram, far_gram,
    load_sem, small_sem, table_sem, deg_sem, zdeg_sem, answer_sem, product_sem,
    part_sem, image_sem, near_sem, far_sem,
):
    at = Place()
    me, z = at.me, at.z
    first = LT // CHUNK
    chunks = (LT + LOC) // CHUNK

    def load(c):
        chunk = pl.ds(c * CHUNK, CHUNK)
        source = remote_w.at[chunk] if c < first else local_w.at[pl.ds((c - first) * CHUNK, CHUNK)]
        return pltpu.make_async_copy(source, eff.at[chunk], load_sem.at[c])

    small = [
        pltpu.make_async_copy(source, target, small_sem.at[i])
        for i, (source, target) in enumerate(
            [
                (groups_h, groups), (remote_coords_h, remote_coords), (local_coords_h, local_coords),
                (remote_gains_h, remote_gains), (local_gains_h, local_gains), (start_h, start),
            ]
        )
    ]
    for copy in small[:4]:
        copy.start()
    for c in range(chunks):
        load(c).start()
    for copy in small[4:]:
        copy.start()

    barrier = pltpu.get_barrier_semaphore()

    def signal(row, split):
        pl.semaphore_signal(barrier, inc=1, device_id=(row, split), device_id_type=MESH)

    for o in range(1, GROUPS):
        signal(at.plane(o), z)
    for offset in range(2, NCORE * SPLITS):
        row, split, _ = at.near(offset)
        signal(row, split)

    for copy in small[:3]:
        copy.wait()
    padded[...] = jnp.zeros_like(padded)
    fetched[...] = jnp.zeros_like(fetched)
    group = jnp.broadcast_to(groups[...], (GROUPS, LT))
    slot_group, tile_id = iota((GROUPS, LT), 0), iota((GROUPS, LT), 1)
    named = group == slot_group
    lowest = jnp.min(jnp.where(named, tile_id, LT - 1), axis=1, keepdims=True)
    highest = jnp.max(jnp.where(named, tile_id, -1), axis=1, keepdims=True)
    is_first, is_second = named & (tile_id == lowest), named & (tile_id == highest)
    slot = MOST * slot_group + jnp.where(is_second, 1, 0)
    named_t = jnp.transpose(group) == iota((LT, GROUPS), 1)
    tile_t = iota((LT, GROUPS), 0)
    table_v[...] = jnp.zeros_like(table_v)
    table_v[T_REMOTE_ROW : T_REMOTE_ROW + 2, 0:LT] = remote_coords[...]
    table_v[T_LOCAL_ROW : T_LOCAL_ROW + 2, 0:LOC] = local_coords[...]
    table_v[T_SLOT : T_SLOT + 1, 0:LT] = jnp.sum(jnp.where(named, slot, 0), axis=0, keepdims=True)
    table_v[T_FIRST : T_FIRST + 1, 0:GROUPS] = jnp.min(jnp.where(named_t, tile_t, LT - 1), axis=0, keepdims=True)
    table_v[T_FIRST + 1 : T_FIRST + 2, 0:GROUPS] = jnp.max(jnp.where(named_t, tile_t, 0), axis=0, keepdims=True)
    table_copy = pltpu.make_async_copy(table_v, table, table_sem.at[0])
    table_copy.start()
    hot_slots = jnp.concatenate([jnp.where(hot, 1.0, 0.0) for hot in (is_first, is_second)], axis=0)
    target = jnp.broadcast_to(remote_coords[1:2, :].astype(F32) + 1.0, (MOST * GROUPS, LT))
    slot_column = jnp.sum(hot_slots * target, axis=1, keepdims=True) - 1.0
    slot_column = jnp.broadcast_to(slot_column, (MOST * GROUPS, HALF))
    hot_slots = hot_slots.astype(BF16)
    small[3].wait()

    def pair(p):
        return pl.ds(MOST * p, MOST)

    ones = jnp.ones((8, TILE), BF16)

    def scale(tile0, gains, gain0, row_at, keep, col_at):
        row_gains = jnp.concatenate([gains[gain0 + t, 0:1, :] for t in range(CHUNK)], axis=0).T
        for t in range(CHUNK):
            scaled = (
                row_gains[:, t : t + 1] * eff[tile0 + t].astype(F32) * gains[gain0 + t, 1:2, :]
            ).astype(BF16)
            eff[tile0 + t] = scaled
            size = jnp.abs(scaled)
            sums[pl.ds(row_at + t, 1), :] = dot(ones, size, ((1,), (1,)))[0:1, :]
            keep(col_at + t, dot(ones, size))

    def remote_chunk(c):
        chunk = pl.ds(c * CHUNK, CHUNK)
        pltpu.make_async_copy(remote_w.at[chunk], eff.at[chunk], load_sem.at[c]).wait()

        def keep(t, value):
            column_sums[pl.ds(t, 1), :] = value[0:1, :]

        scale(c * CHUNK, remote_gains, c * CHUNK, c * CHUNK, keep, c * CHUNK)

    def local_chunk(c):
        pltpu.make_async_copy(
            local_w.at[pl.ds(c * CHUNK, CHUNK)],
            eff.at[pl.ds(LT + c * CHUNK, CHUNK)],
            load_sem.at[first + c],
        ).wait()

        def keep(t, value):
            sums[pl.ds(t, 1), :] = value[0:1, :]

        scale(LT + c * CHUNK, local_gains, c * CHUNK, LT + c * CHUNK, keep, LT + LOC + c * CHUNK)

    loop(0, first, remote_chunk)
    pl.semaphore_wait(barrier, GROUPS - 1 + NCORE * SPLITS - 2)

    slot_sums = select_sum(hot_slots, column_sums[...])
    for p in range(GROUPS):
        pieces = []
        for s in range(MOST):
            row = slot_sums[s * GROUPS + p : s * GROUPS + p + 1, :]
            pieces += [row[:, 0:HALF], row[:, HALF:TILE]]
        for s in range(MOST):
            pieces += [slot_column[s * GROUPS + p : s * GROUPS + p + 1, :]] * 2
        deg_out[p] = jnp.concatenate(pieces, axis=0)
    for o in range(1, GROUPS):
        to = at.plane(o)
        copy_to(deg_out.at[to], deg_in.at[me], deg_sem.at[0], deg_sem.at[1], to, z).start()
    deg_in[me] = deg_out[me]
    small[4].wait()
    loop(0, LOC // CHUNK, local_chunk)
    small[5].wait()
    table_copy.wait()

    def hot_rows(row):
        return jnp.where(jnp.broadcast_to(row, (BR, row.shape[1])) == iota((BR, row.shape[1]), 0), 1.0, 0.0).astype(BF16)

    own = select_sum(hot_rows(remote_coords[0:1, :]), sums[0:LT, :])
    own += select_sum(hot_rows(local_coords[0:1, :]), sums[LT : LT + LOC, :])
    own += select_sum(hot_rows(local_coords[1:2, :]), sums[LT + LOC : LT + 2 * LOC, :])
    wait_all(deg_in.at[pl.ds(0, GROUPS - 1)], deg_sem.at[0], deg_sem.at[1], at)
    came = deg_in[...].reshape(GROUPS * 8, HALF)
    column = pltpu.roll(came, GROUPS * 8 - 4, 0)
    row8 = iota((GROUPS * 8, HALF), 0) % 8
    lane_f = iota((GROUPS * 8, HALF), 1).astype(F32)
    added = []
    for half in range(2):
        chosen = (column == lane_f) & ((row8 == half) | (row8 == 2 + half))
        hot = jnp.where(chosen, 1.0, 0.0).astype(BF16)
        added.append(select_sum(hot, came, ((0,), (0,)))[0:BR, :])
    split_part[z] = own + jnp.concatenate(added, axis=1)

    for dz in range(1, SPLITS):
        copy_to(split_part.at[z], split_part.at[z], zdeg_sem.at[0], zdeg_sem.at[1], me, at.split(dz)).start()

    row = iota((BR * WIDTH, HALF), 0)
    lane = iota((BR * WIDTH, HALF), 1)
    row_tile = (row // WIDTH).astype(F32)
    lanes = iota((1, HALF), 1)
    per = HALF // WIDTH
    for q in range(GROUPS * MOST // per):
        column = jnp.zeros((1, HALF), F32)
        for i in range(per):
            at_slot = deg_in[q * (per // MOST) + i // MOST, 4 + 2 * (i % MOST) : 5 + 2 * (i % MOST), :]
            column = jnp.where(lanes // WIDTH == i, at_slot, column)
        chosen = (jnp.broadcast_to(column, row.shape) == row_tile) & (lane % WIDTH == row % WIDTH)
        spread[:, q * HALF : (q + 1) * HALF] = jnp.where(chosen, 1.0, 0.0).astype(BF16)

    lane = iota((WIDTH, TILE), 1)
    diagonal = lane % WIDTH == iota((WIDTH, TILE), 0)
    lane_tile = (lane // WIDTH).astype(F32)
    for slot in range(GROUPS * MOST):
        own = deg_in[slot // MOST, 4 + 2 * (slot % MOST) : 5 + 2 * (slot % MOST), :]
        own = jnp.broadcast_to(jnp.concatenate([own, own], axis=1), (WIDTH, TILE))
        gather[slot * WIDTH : (slot + 1) * WIDTH, :] = jnp.where(diagonal & (own == lane_tile), 1.0, 0.0).astype(BF16)

    wait_all(split_part.at[pl.ds(0, SPLITS - 1)], zdeg_sem.at[0], zdeg_sem.at[1], at)
    inv[...] = 1.0 / jnp.sqrt((split_part[0] + split_part[1]) + (split_part[2] + split_part[3]))

    def set_rows(j, vectors):
        scaled = (vectors * inv[j : j + 1, :]).astype(BF16)
        padded[j, PAD] = scaled
        row_blocks[j] = scaled

    for j in range(BR):
        set_rows(j, start[:, j * TILE : (j + 1) * TILE])

    for it in range(ITERS):
        last = it == ITERS - 1
        a_in, p_in = answer_in.at[it], product_in.at[it]

        answer_out[...] = (
            dot(gather[...], row_blocks[...].reshape(BR * WIDTH, TILE)).astype(BF16).reshape(answer_out.shape)
        )

        for o in range(1, GROUPS):
            to = at.plane(o)
            copy_to(
                answer_out.at[pair(to)], a_in.at[pair(me)], answer_sem.at[it, 0], answer_sem.at[it, 1], to, z
            ).start()
        a_in[pair(me)] = answer_out[pair(me)]

        def backward(i):
            for u in range(STEP):
                tile = i * STEP + u
                x = row_blocks[table[T_REMOTE_ROW, tile]]
                product[tile] = dot(x, eff[tile]).astype(BF16)

        loop(0, LT // STEP, backward)

        def fill_product(p, ref):
            for s in range(MOST):
                ref[MOST * p + s] = product[table[T_FIRST + s, p]]

        for o in range(1, GROUPS):
            to = at.plane(o)
            fill_product(to, product_out)
            copy_to(
                product_out.at[pair(to)], p_in.at[pair(me)], product_sem.at[it, 0], product_sem.at[it, 1], to, z
            ).start()
        fill_product(me, p_in)

        total[...] = jnp.zeros_like(total)

        def window(ref, index, row_tile):
            return ref[index, pl.ds(PAD - row_tile, BR)].reshape(BR * WIDTH, TILE)

        def local(i):
            value = total[...]
            for u in range(STEP):
                tile = i * STEP + u
                r, c = table[T_LOCAL_ROW, tile], table[T_LOCAL_COL, tile]
                value += dot(window(padded, c, r), eff[LT + tile], ((1,), (1,)))
                value += dot(window(padded, r, c), eff[LT + tile])
            total[...] = value

        loop(0, LOC // STEP, local)

        others = pl.ds(0, MOST * (GROUPS - 1))
        wait_all(a_in.at[others], answer_sem.at[it, 0], answer_sem.at[it, 1], at)

        def forward(i):
            value = total[...]
            for u in range(STEP):
                tile = i * STEP + u
                slot = table[T_SLOT, tile]
                fetched[u, PAD] = a_in[slot]
                value += dot(window(fetched, u, table[T_REMOTE_ROW, tile]), eff[tile], ((1,), (1,)))
            total[...] = value

        loop(0, LT // STEP, forward)

        wait_all(p_in.at[others], product_sem.at[it, 0], product_sem.at[it, 1], at)
        total[...] += dot(spread[...], p_in[...].reshape(GROUPS * MOST * WIDTH, TILE))

        for dz in range(1, SPLITS):
            other = at.split(dz)
            copy_to(
                total.at[pl.ds(other * QROWS, QROWS)], parts.at[it, dz], part_sem.at[it, 0], part_sem.at[it, 1], me, other
            ).start()
        mine = pl.ds(z * QROWS, QROWS)
        wait_all(parts.at[it, pl.ds(1, SPLITS - 1)], part_sem.at[it, 0], part_sem.at[it, 1], at)
        summed = total[mine, :] + ((parts[it, 1] + parts[it, 2]) + parts[it, 3])
        tiles = [
            summed[j * WIDTH : (j + 1) * WIDTH, :] * inv[pl.ds(z * (BR // SPLITS) + j, 1), :]
            for j in range(BR // SPLITS)
        ]
        wide = jnp.concatenate(tiles, axis=1)
        wide_parts = split3(wide)
        stacked = jnp.concatenate(wide_parts, axis=0)
        crossed = dot(stacked, stacked, ((1,), (1,)))

        def cross(i, j):
            return crossed[i * WIDTH : (i + 1) * WIDTH, j * WIDTH : (j + 1) * WIDTH]

        gram = cross(0, 0) + ((cross(0, 1) + cross(1, 0)) + ((cross(0, 2) + cross(2, 0)) + cross(1, 1)))
        packed = jnp.concatenate([gram[0:8], gram[8:16], jnp.zeros((8, HALF - 2 * WIDTH), F32)], axis=1)

        own = z * NCORE + at.core
        near_gram[it, own] = packed
        for offset in range(1, NCORE * SPLITS):
            row, split, _ = at.near(offset)
            copy_to(
                near_gram.at[it, own], near_gram.at[it, own], near_sem.at[it, 0], near_sem.at[it, 1], row, split
            ).start()
        if not last:
            image[mine, :] = jnp.concatenate(tiles, axis=0)
            for dz in range(1, SPLITS):
                copy_to(image.at[mine], image.at[mine], image_sem.at[0], image_sem.at[1], me, at.split(dz)).start()
        wait_all(near_gram.at[it, pl.ds(0, NCORE * SPLITS - 1)], near_sem.at[it, 0], near_sem.at[it, 1], at)
        near_sum = near_gram[it, 0]
        for i in range(1, NCORE * SPLITS):
            near_sum = near_sum + near_gram[it, i]

        own = at.x * NY + at.y
        far_gram[it, own] = near_sum
        for offset in range(1, NX * NY):
            row, split, _ = at.far(offset)
            copy_to(
                far_gram.at[it, own], far_gram.at[it, own], far_sem.at[it, 0], far_sem.at[it, 1], row, split
            ).start()
        if not last:
            wait_all(image.at[pl.ds(0, (SPLITS - 1) * QROWS)], image_sem.at[0], image_sem.at[1], at)
            for j in range(BR):
                pieces = split3(image[j * WIDTH : (j + 1) * WIDTH, :])
                image_parts[j] = jnp.concatenate([pieces[i] for i in RIGHT], axis=0)
        wait_all(far_gram.at[it, pl.ds(0, NX * NY - 1)], far_sem.at[it, 0], far_sem.at[it, 1], at)
        packed = far_gram[it, 0]
        for i in range(1, NX * NY):
            packed = packed + far_gram[it, i]
        gram = jnp.concatenate([packed[:, 0:WIDTH], packed[:, WIDTH : 2 * WIDTH]], axis=0)
        inverse = factor_inverse(gram / VERTICES)
        if last:
            out[...] = dot(inverse, jnp.concatenate([wide_parts[i] for i in RIGHT], axis=0))
        else:
            for j in range(BR):
                set_rows(j, dot(inverse, image_parts[j]))


def per_device(
    local_weights, local_gains, local_coords, remote_weights, remote_gains, remote_groups, remote_coords, start_block
):
    dma = pltpu.SemaphoreType.DMA
    return pl.pallas_call(
        whole_kernel,
        out_shape=jax.ShapeDtypeStruct((WIDTH, QROWS // WIDTH * TILE), F32),
        in_specs=[HBM] * 8,
        out_specs=VMEM,
        scratch_shapes=[
            pltpu.VMEM((1, LT), jnp.int32),
            pltpu.VMEM((2, LOC), jnp.int32),
            pltpu.VMEM((2, LT), jnp.int32),
            pltpu.VMEM((LOC, 2, TILE), F32),
            pltpu.VMEM((LT, 2, TILE), F32),
            pltpu.VMEM((WIDTH, BR * TILE), F32),
            pltpu.VMEM((LT + LOC, TILE, TILE), BF16),
            pltpu.VMEM((8, HALF), jnp.int32),
            pltpu.SMEM((8, HALF), jnp.int32),
            pltpu.VMEM((LT, TILE), F32),
            pltpu.VMEM((LT + 2 * LOC, TILE), F32),
            pltpu.VMEM((GROUPS, 8, HALF), F32),
            pltpu.VMEM((GROUPS, 8, HALF), F32),
            pltpu.VMEM((SPLITS, BR, TILE), F32),
            pltpu.VMEM((BR, TILE), F32),
            pltpu.VMEM((BR * WIDTH, GROUPS * MOST * WIDTH), BF16),
            pltpu.VMEM((GROUPS * MOST * WIDTH, BR * WIDTH), BF16),
            pltpu.VMEM((BR, WIDTH, TILE), BF16),
            pltpu.VMEM((BR, 2 * PAD + 1, WIDTH, TILE), BF16),
            pltpu.VMEM((GROUPS * MOST, WIDTH, TILE), BF16),
            pltpu.VMEM((ITERS, GROUPS * MOST, WIDTH, TILE), BF16),
            pltpu.VMEM((LT, WIDTH, TILE), BF16),
            pltpu.VMEM((GROUPS * MOST, WIDTH, TILE), BF16),
            pltpu.VMEM((ITERS, GROUPS * MOST, WIDTH, TILE), BF16),
            pltpu.VMEM((STEP, 2 * PAD + 1, WIDTH, TILE), BF16),
            pltpu.VMEM((BR * WIDTH, TILE), F32),
            pltpu.VMEM((ITERS, SPLITS, QROWS, TILE), F32),
            pltpu.VMEM((BR * WIDTH, TILE), F32),
            pltpu.VMEM((BR, len(RIGHT) * WIDTH, TILE), BF16),
            pltpu.VMEM((ITERS, NCORE * SPLITS, 8, HALF), F32),
            pltpu.VMEM((ITERS, NX * NY, 8, HALF), F32),
            dma(((LT + LOC) // CHUNK,)),
            dma((6,)),
            dma((1,)),
            dma((2,)),
            dma((2,)),
            dma((ITERS, 2)),
            dma((ITERS, 2)),
            dma((ITERS, 2)),
            dma((2,)),
            dma((ITERS, 2)),
            dma((ITERS, 2)),
        ],
        compiler_params=pltpu.CompilerParams(
            collective_id=0, has_side_effects=True, vmem_limit_bytes=60 << 20
        ),
        name="iterate",
    )(
        remote_groups[0], local_coords[0, 0].T, remote_coords[0, 0].T, local_gains[0, 0], remote_gains[0, 0],
        start_block, local_weights[0, 0], remote_weights[0, 0],
    )


def solution(mesh):
    in_specs = (
        P("rows", "cols", None, None, None),
        P("rows", "cols", None, None, None),
        P("rows", "cols", None, None),
        P("rows", "cols", None, None, None),
        P("rows", "cols", None, None, None),
        P("rows", "cols", None),
        P("rows", "cols", None, None),
        P(None, "rows"),
    )
    out_specs = P(None, ("rows", "cols"))
    return jax.shard_map(
        per_device, mesh=mesh, in_specs=in_specs, out_specs=out_specs, check_vma=False
    )
```

```python
import jax
import jax.numpy as jnp
from jax import lax
from jax.experimental import pallas as pl
from jax.experimental.pallas import tpu as pltpu
from jax.sharding import PartitionSpec as P

TILE = 256
HALF = 128
WIDTH = 16
BR = 16
MOST = 2
ITERS = 2
LOC = 48
LT = 32
GROUPS = 32
SPLITS = 4
QROWS = BR // SPLITS * WIDTH
NX, NY, NCORE = 4, 4, 2
CHUNK = 8
STEP = 4
VERTICES = GROUPS * BR * TILE
PAD = BR - 1
MESH = pl.DeviceIdType.MESH
VMEM = pl.BlockSpec(memory_space=pltpu.VMEM)
F32 = jnp.float32
BF16 = jnp.bfloat16

HBM = pl.BlockSpec(memory_space=pltpu.HBM)
T_REMOTE_ROW, T_REMOTE_COL, T_LOCAL_ROW, T_LOCAL_COL, T_SLOT, T_FIRST = range(6)
LEFT, RIGHT = (0, 0, 1, 0, 1, 2), (0, 1, 0, 2, 1, 0)


def ring(distance, size):
    return min(distance, size - distance)


PLANE = sorted(
    range(1, NX * NY * NCORE), key=lambda o: -ring(o // (NCORE * NY), NX) - ring(o // NCORE % NY, NY)
)
NEAR = sorted(range(1, NCORE * SPLITS), key=lambda o: -ring(o // NCORE, SPLITS))
FAR = sorted(range(1, NX * NY), key=lambda o: -ring(o // NY, NX) - ring(o % NY, NY))
DZ = (2, 1, 3)


def dot(a, b, dims=((1,), (0,))):
    return lax.dot_general(a, b, (dims, ((), ())), preferred_element_type=F32)


def split3(value):
    high = value.astype(BF16)
    rest = value - high.astype(F32)
    middle = rest.astype(BF16)
    return high, middle, (rest - middle.astype(F32)).astype(BF16)


def select_sum(hot, value, dims=((1,), (0,))):
    high, middle, low = split3(value)
    return dot(hot, high, dims) + (dot(hot, middle, dims) + dot(hot, low, dims))


def iota(shape, dim):
    return lax.broadcasted_iota(jnp.int32, shape, dim)


def factor_inverse(gram):
    copies = len(LEFT) * WIDTH
    shape = (WIDTH, HALF)
    row, lane = iota(shape, 0), iota(shape, 1)
    work = jnp.where((lane % WIDTH == row) & (lane < copies), 1.0, 0.0)
    columns = [jnp.broadcast_to(gram[:, k : k + 1], shape) for k in range(WIDTH)]
    roots = jnp.zeros(shape, F32)
    for k in range(WIDTH):
        pivot = jnp.broadcast_to(columns[k][k : k + 1, :], shape)
        roots = jnp.where(row == k, 1.0 / jnp.sqrt(pivot), roots)
        if k == WIDTH - 1:
            break
        factor = jnp.where(row > k, columns[k] * (1.0 / pivot), 0.0)
        for j in range(k + 1, WIDTH):
            columns[j] = columns[j] - factor * jnp.broadcast_to(columns[j][k : k + 1, :], shape)
        work = work - factor * jnp.broadcast_to(work[k : k + 1, :], shape)
    inverse = work * roots
    high, middle, low = (part.astype(F32) for part in split3(inverse))
    part = lane // WIDTH
    chosen = jnp.where((part == 2) | (part == 4), middle, jnp.where(part == 5, low, high))
    return chosen.astype(BF16)[:, 0:copies]


class Place:
    def __init__(self):
        self.me, self.z = lax.axis_index("rows"), lax.axis_index("cols")
        self.core = self.me % NCORE
        self.y = (self.me // NCORE) % NY
        self.x = self.me // (NCORE * NY)

    def plane(self, offset, sign=1):
        dc, dy, dx = offset % NCORE, (offset // NCORE) % NY, offset // (NCORE * NY)
        x = (self.x + NX + sign * dx) % NX
        y = (self.y + NY + sign * dy) % NY
        return (x * NY + y) * NCORE + (self.core + NCORE + sign * dc) % NCORE

    def split(self, dz, sign=1):
        return (self.z + SPLITS + sign * dz) % SPLITS

    def near(self, offset, sign=1):
        core = (self.core + NCORE + sign * (offset % NCORE)) % NCORE
        z = self.split(offset // NCORE, sign)
        return self.me - self.core + core, z, z * NCORE + core

    def far(self, offset, sign=1):
        x = (self.x + NX + sign * (offset // NY)) % NX
        y = (self.y + NY + sign * (offset % NY)) % NY
        return (x * NY + y) * NCORE + self.core, self.z, x * NY + y


def copy_to(source, target, send_sem, recv_sem, row, split):
    return pltpu.make_async_remote_copy(
        src_ref=source, dst_ref=target, send_sem=send_sem, recv_sem=recv_sem,
        device_id=(row, split), device_id_type=MESH,
    )


def wait_all(ref, send_sem, recv_sem, place):
    copy_to(ref, ref, send_sem, recv_sem, place.me, place.z).wait()


def loop(start, stop, body):
    def step(i, carry):
        body(i)
        return carry

    lax.fori_loop(start, stop, step, 0)


def whole_kernel(
    groups_h, local_coords_h, remote_coords_h, local_gains_h, remote_gains_h, start_h, local_w, remote_w,
    out,
    groups, local_coords, remote_coords, local_gains, remote_gains, start,
    eff, table_v, table, column_sums, sums, deg_out, deg_in, split_part, inv, spread, gather, row_blocks,
    padded, answer_out, answer_in, product, product_out, product_in, fetched, total,
    parts, late, late_out, late_in, image, image_parts, near_gram, far_gram,
    load_sem, small_sem, table_sem, deg_sem, zdeg_sem, answer_sem, product_sem,
    part_sem, late_sem, image_sem, near_sem, far_sem,
):
    at = Place()
    me, z = at.me, at.z
    first = LT // CHUNK
    chunks = (LT + LOC) // CHUNK

    def load(c):
        chunk = pl.ds(c * CHUNK, CHUNK)
        source = remote_w.at[chunk] if c < first else local_w.at[pl.ds((c - first) * CHUNK, CHUNK)]
        return pltpu.make_async_copy(source, eff.at[chunk], load_sem.at[c])

    small = [
        pltpu.make_async_copy(source, target, small_sem.at[i])
        for i, (source, target) in enumerate(
            [
                (groups_h, groups), (remote_coords_h, remote_coords), (local_coords_h, local_coords),
                (remote_gains_h, remote_gains), (local_gains_h, local_gains), (start_h, start),
            ]
        )
    ]
    for copy in small[:4]:
        copy.start()
    for c in range(chunks):
        load(c).start()
    for copy in small[4:]:
        copy.start()

    barrier = pltpu.get_barrier_semaphore()

    def signal(row, split):
        pl.semaphore_signal(barrier, inc=1, device_id=(row, split), device_id_type=MESH)

    for o in PLANE:
        signal(at.plane(o), z)
    for offset in range(2, NCORE * SPLITS):
        row, split, _ = at.near(offset)
        signal(row, split)

    for copy in small[:3]:
        copy.wait()
    group = jnp.broadcast_to(groups[...], (GROUPS, LT))
    slot_group, tile_id = iota((GROUPS, LT), 0), iota((GROUPS, LT), 1)
    named = group == slot_group
    lowest = jnp.min(jnp.where(named, tile_id, LT - 1), axis=1, keepdims=True)
    highest = jnp.max(jnp.where(named, tile_id, -1), axis=1, keepdims=True)
    is_first, is_second = named & (tile_id == lowest), named & (tile_id == highest)
    slot = MOST * slot_group + jnp.where(is_second, 1, 0)
    named_t = jnp.transpose(group) == iota((LT, GROUPS), 1)
    tile_t = iota((LT, GROUPS), 0)
    table_v[...] = jnp.zeros_like(table_v)
    table_v[T_REMOTE_ROW : T_REMOTE_ROW + 2, 0:LT] = remote_coords[...]
    table_v[T_LOCAL_ROW : T_LOCAL_ROW + 2, 0:LOC] = local_coords[...]
    table_v[T_SLOT : T_SLOT + 1, 0:LT] = jnp.sum(jnp.where(named, slot, 0), axis=0, keepdims=True)
    table_v[T_FIRST : T_FIRST + 1, 0:GROUPS] = jnp.min(jnp.where(named_t, tile_t, LT - 1), axis=0, keepdims=True)
    table_v[T_FIRST + 1 : T_FIRST + 2, 0:GROUPS] = jnp.max(jnp.where(named_t, tile_t, 0), axis=0, keepdims=True)
    table_copy = pltpu.make_async_copy(table_v, table, table_sem.at[0])
    table_copy.start()
    hot_slots = jnp.concatenate([jnp.where(hot, 1.0, 0.0) for hot in (is_first, is_second)], axis=0)
    target = jnp.broadcast_to(remote_coords[1:2, :].astype(F32) + 1.0, (MOST * GROUPS, LT))
    slot_column = jnp.sum(hot_slots * target, axis=1, keepdims=True) - 1.0
    slot_column = jnp.broadcast_to(slot_column, (MOST * GROUPS, HALF))
    hot_slots = hot_slots.astype(BF16)
    small[3].wait()

    def pair(p):
        return pl.ds(MOST * p, MOST)

    ones = jnp.ones((8, TILE), BF16)

    def scale(tile0, gains, gain0, row_at, keep, col_at):
        row_gains = jnp.concatenate([gains[gain0 + t, 0:1, :] for t in range(CHUNK)], axis=0).T
        for t in range(CHUNK):
            scaled = (
                row_gains[:, t : t + 1] * eff[tile0 + t].astype(F32) * gains[gain0 + t, 1:2, :]
            ).astype(BF16)
            eff[tile0 + t] = scaled
            size = jnp.abs(scaled)
            sums[pl.ds(row_at + t, 1), :] = dot(ones, size, ((1,), (1,)))[0:1, :]
            keep(col_at + t, dot(ones, size))

    def remote_chunk(c):
        chunk = pl.ds(c * CHUNK, CHUNK)
        pltpu.make_async_copy(remote_w.at[chunk], eff.at[chunk], load_sem.at[c]).wait()

        def keep(t, value):
            column_sums[pl.ds(t, 1), :] = value[0:1, :]

        scale(c * CHUNK, remote_gains, c * CHUNK, c * CHUNK, keep, c * CHUNK)

    def local_chunk(c):
        pltpu.make_async_copy(
            local_w.at[pl.ds(c * CHUNK, CHUNK)],
            eff.at[pl.ds(LT + c * CHUNK, CHUNK)],
            load_sem.at[first + c],
        ).wait()

        def keep(t, value):
            sums[pl.ds(t, 1), :] = value[0:1, :]

        scale(LT + c * CHUNK, local_gains, c * CHUNK, LT + c * CHUNK, keep, LT + LOC + c * CHUNK)

    loop(0, first, remote_chunk)
    pl.semaphore_wait(barrier, GROUPS - 1 + NCORE * SPLITS - 2)

    slot_sums = select_sum(hot_slots, column_sums[...])
    for p in range(GROUPS):
        pieces = []
        for s in range(MOST):
            row = slot_sums[s * GROUPS + p : s * GROUPS + p + 1, :]
            pieces += [row[:, 0:HALF], row[:, HALF:TILE]]
        for s in range(MOST):
            pieces += [slot_column[s * GROUPS + p : s * GROUPS + p + 1, :]] * 2
        deg_out[p] = jnp.concatenate(pieces, axis=0)
    for o in PLANE:
        to = at.plane(o)
        copy_to(deg_out.at[to], deg_in.at[me], deg_sem.at[0], deg_sem.at[1], to, z).start()
    deg_in[me] = deg_out[me]
    small[4].wait()
    loop(0, LOC // CHUNK, local_chunk)
    small[5].wait()
    table_copy.wait()

    def hot_rows(row):
        return jnp.where(jnp.broadcast_to(row, (BR, row.shape[1])) == iota((BR, row.shape[1]), 0), 1.0, 0.0).astype(BF16)

    own = select_sum(hot_rows(remote_coords[0:1, :]), sums[0:LT, :])
    own += select_sum(hot_rows(local_coords[0:1, :]), sums[LT : LT + LOC, :])
    own += select_sum(hot_rows(local_coords[1:2, :]), sums[LT + LOC : LT + 2 * LOC, :])
    wait_all(deg_in.at[pl.ds(0, GROUPS - 1)], deg_sem.at[0], deg_sem.at[1], at)
    came = deg_in[...].reshape(GROUPS * 8, HALF)
    column = pltpu.roll(came, GROUPS * 8 - 4, 0)
    row8 = iota((GROUPS * 8, HALF), 0) % 8
    lane_f = iota((GROUPS * 8, HALF), 1).astype(F32)
    added = []
    for half in range(2):
        chosen = (column == lane_f) & ((row8 == half) | (row8 == 2 + half))
        hot = jnp.where(chosen, 1.0, 0.0).astype(BF16)
        added.append(select_sum(hot, came, ((0,), (0,)))[0:BR, :])
    split_part[z] = own + jnp.concatenate(added, axis=1)

    for dz in DZ:
        copy_to(split_part.at[z], split_part.at[z], zdeg_sem.at[0], zdeg_sem.at[1], me, at.split(dz)).start()

    lane = iota((WIDTH, TILE), 1)
    diagonal = lane % WIDTH == iota((WIDTH, TILE), 0)
    lane_tile = (lane // WIDTH).astype(F32)
    for slot in range(GROUPS * MOST):
        own = deg_in[slot // MOST, 4 + 2 * (slot % MOST) : 5 + 2 * (slot % MOST), :]
        own = jnp.broadcast_to(jnp.concatenate([own, own], axis=1), (WIDTH, TILE))
        gather[slot * WIDTH : (slot + 1) * WIDTH, :] = jnp.where(diagonal & (own == lane_tile), 1.0, 0.0).astype(BF16)

    wait_all(split_part.at[pl.ds(0, SPLITS - 1)], zdeg_sem.at[0], zdeg_sem.at[1], at)
    inv[...] = 1.0 / jnp.sqrt((split_part[0] + split_part[1]) + (split_part[2] + split_part[3]))

    def set_rows(j, vectors):
        scaled = (vectors * inv[j : j + 1, :]).astype(BF16)
        row_blocks[j] = scaled

    for j in range(BR):
        set_rows(j, start[:, j * TILE : (j + 1) * TILE])

    for it in range(ITERS):
        last = it == ITERS - 1
        a_in, p_in = answer_in.at[it], product_in.at[it]

        answer_out[...] = (
            dot(gather[...], row_blocks[...].reshape(BR * WIDTH, TILE)).astype(BF16).reshape(answer_out.shape)
        )

        for o in PLANE:
            to = at.plane(o)
            copy_to(
                answer_out.at[pair(to)], a_in.at[pair(me)], answer_sem.at[it, 0], answer_sem.at[it, 1], to, z
            ).start()
        a_in[pair(me)] = answer_out[pair(me)]

        def backward(i):
            for u in range(STEP):
                tile = i * STEP + u
                x = row_blocks[table[T_REMOTE_ROW, tile]]
                product[tile] = dot(x, eff[tile]).astype(BF16)

        loop(0, LT // STEP, backward)

        def fill_product(p, ref):
            for s in range(MOST):
                ref[MOST * p + s] = product[table[T_FIRST + s, p]]

        for o in PLANE:
            to = at.plane(o)
            fill_product(to, product_out)
            copy_to(
                product_out.at[pair(to)], p_in.at[pair(me)], product_sem.at[it, 0], product_sem.at[it, 1], to, z
            ).start()
        fill_product(me, p_in)

        if it == 0:
            padded[...] = jnp.zeros_like(padded)
            fetched[...] = jnp.zeros_like(fetched)
            row = iota((BR * WIDTH, HALF), 0)
            lane = iota((BR * WIDTH, HALF), 1)
            row_tile = (row // WIDTH).astype(F32)
            lanes = iota((1, HALF), 1)
            per = HALF // WIDTH
            for q in range(GROUPS * MOST // per):
                column = jnp.zeros((1, HALF), F32)
                for i in range(per):
                    at_slot = deg_in[q * (per // MOST) + i // MOST, 4 + 2 * (i % MOST) : 5 + 2 * (i % MOST), :]
                    column = jnp.where(lanes // WIDTH == i, at_slot, column)
                chosen = (jnp.broadcast_to(column, row.shape) == row_tile) & (lane % WIDTH == row % WIDTH)
                spread[:, q * HALF : (q + 1) * HALF] = jnp.where(chosen, 1.0, 0.0).astype(BF16)
        for j in range(BR):
            padded[j, PAD] = row_blocks[j]

        total[...] = jnp.zeros_like(total)

        def window(ref, index, row_tile):
            return ref[index, pl.ds(PAD - row_tile, BR)].reshape(BR * WIDTH, TILE)

        def local(i):
            value = total[...]
            for u in range(STEP):
                tile = i * STEP + u
                r, c = table[T_LOCAL_ROW, tile], table[T_LOCAL_COL, tile]
                value += dot(window(padded, c, r), eff[LT + tile], ((1,), (1,)))
                value += dot(window(padded, r, c), eff[LT + tile])
            total[...] = value

        loop(0, LOC // STEP, local)

        others = pl.ds(0, MOST * (GROUPS - 1))
        wait_all(a_in.at[others], answer_sem.at[it, 0], answer_sem.at[it, 1], at)

        def forward(i):
            value = total[...]
            for u in range(STEP):
                tile = i * STEP + u
                slot = table[T_SLOT, tile]
                fetched[u, PAD] = a_in[slot]
                value += dot(window(fetched, u, table[T_REMOTE_ROW, tile]), eff[tile], ((1,), (1,)))
            total[...] = value

        loop(0, LT // STEP, forward)

        for dz in DZ:
            other = at.split(dz)
            copy_to(
                total.at[pl.ds(other * QROWS, QROWS)], parts.at[it, dz], part_sem.at[it, 0], part_sem.at[it, 1], me, other
            ).start()
        wait_all(p_in.at[others], product_sem.at[it, 0], product_sem.at[it, 1], at)
        rest = dot(spread[...], p_in[...].reshape(GROUPS * MOST * WIDTH, TILE))
        late_out[...] = rest.astype(BF16)

        for dz in DZ:
            other = at.split(dz)
            copy_to(
                late_out.at[pl.ds(other * QROWS, QROWS)], late_in.at[it, dz],
                late_sem.at[it, 0], late_sem.at[it, 1], me, other,
            ).start()
        late[...] = rest
        mine = pl.ds(z * QROWS, QROWS)
        wait_all(parts.at[it, pl.ds(1, SPLITS - 1)], part_sem.at[it, 0], part_sem.at[it, 1], at)
        summed = (total[mine, :] + late[mine, :]) + ((parts[it, 1] + parts[it, 2]) + parts[it, 3])
        wait_all(late_in.at[it, pl.ds(1, SPLITS - 1)], late_sem.at[it, 0], late_sem.at[it, 1], at)
        summed += (late_in[it, 1].astype(F32) + late_in[it, 2].astype(F32)) + late_in[it, 3].astype(F32)
        tiles = [
            summed[j * WIDTH : (j + 1) * WIDTH, :] * inv[pl.ds(z * (BR // SPLITS) + j, 1), :]
            for j in range(BR // SPLITS)
        ]
        wide = jnp.concatenate(tiles, axis=1)
        wide_parts = split3(wide)
        stacked = jnp.concatenate(wide_parts, axis=0)
        crossed = dot(stacked, stacked, ((1,), (1,)))

        def cross(i, j):
            return crossed[i * WIDTH : (i + 1) * WIDTH, j * WIDTH : (j + 1) * WIDTH]

        gram = cross(0, 0) + ((cross(0, 1) + cross(1, 0)) + ((cross(0, 2) + cross(2, 0)) + cross(1, 1)))
        packed = jnp.concatenate([gram[0:8], gram[8:16], jnp.zeros((8, HALF - 2 * WIDTH), F32)], axis=1)

        own = z * NCORE + at.core
        near_gram[it, own] = packed
        for offset in NEAR:
            row, split, _ = at.near(offset)
            copy_to(
                near_gram.at[it, own], near_gram.at[it, own], near_sem.at[it, 0], near_sem.at[it, 1], row, split
            ).start()
        if not last:
            image[mine, :] = jnp.concatenate(tiles, axis=0)
            for dz in DZ:
                copy_to(image.at[mine], image.at[mine], image_sem.at[0], image_sem.at[1], me, at.split(dz)).start()
        wait_all(near_gram.at[it, pl.ds(0, NCORE * SPLITS - 1)], near_sem.at[it, 0], near_sem.at[it, 1], at)
        near_sum = near_gram[it, 0]
        for i in range(1, NCORE * SPLITS):
            near_sum = near_sum + near_gram[it, i]

        own = at.x * NY + at.y
        far_gram[it, own] = near_sum
        for offset in FAR:
            row, split, _ = at.far(offset)
            copy_to(
                far_gram.at[it, own], far_gram.at[it, own], far_sem.at[it, 0], far_sem.at[it, 1], row, split
            ).start()
        if not last:
            wait_all(image.at[pl.ds(0, (SPLITS - 1) * QROWS)], image_sem.at[0], image_sem.at[1], at)
            for j in range(BR):
                pieces = split3(image[j * WIDTH : (j + 1) * WIDTH, :])
                image_parts[j] = jnp.concatenate([pieces[i] for i in RIGHT], axis=0)
        wait_all(far_gram.at[it, pl.ds(0, NX * NY - 1)], far_sem.at[it, 0], far_sem.at[it, 1], at)
        packed = far_gram[it, 0]
        for i in range(1, NX * NY):
            packed = packed + far_gram[it, i]
        gram = jnp.concatenate([packed[:, 0:WIDTH], packed[:, WIDTH : 2 * WIDTH]], axis=0)
        inverse = factor_inverse(gram / VERTICES)
        if last:
            out[...] = dot(inverse, jnp.concatenate([wide_parts[i] for i in RIGHT], axis=0))
        else:
            for j in range(BR):
                set_rows(j, dot(inverse, image_parts[j]))


def per_device(
    local_weights, local_gains, local_coords, remote_weights, remote_gains, remote_groups, remote_coords, start_block
):
    dma = pltpu.SemaphoreType.DMA
    return pl.pallas_call(
        whole_kernel,
        out_shape=pltpu.VMEM((WIDTH, QROWS // WIDTH * TILE), F32),
        in_specs=[HBM] * 8,
        out_specs=VMEM,
        scratch_shapes=[
            pltpu.VMEM((1, LT), jnp.int32),
            pltpu.VMEM((2, LOC), jnp.int32),
            pltpu.VMEM((2, LT), jnp.int32),
            pltpu.VMEM((LOC, 2, TILE), F32),
            pltpu.VMEM((LT, 2, TILE), F32),
            pltpu.VMEM((WIDTH, BR * TILE), F32),
            pltpu.VMEM((LT + LOC, TILE, TILE), BF16),
            pltpu.VMEM((8, HALF), jnp.int32),
            pltpu.SMEM((8, HALF), jnp.int32),
            pltpu.VMEM((LT, TILE), F32),
            pltpu.VMEM((LT + 2 * LOC, TILE), F32),
            pltpu.VMEM((GROUPS, 8, HALF), F32),
            pltpu.VMEM((GROUPS, 8, HALF), F32),
            pltpu.VMEM((SPLITS, BR, TILE), F32),
            pltpu.VMEM((BR, TILE), F32),
            pltpu.VMEM((BR * WIDTH, GROUPS * MOST * WIDTH), BF16),
            pltpu.VMEM((GROUPS * MOST * WIDTH, BR * WIDTH), BF16),
            pltpu.VMEM((BR, WIDTH, TILE), BF16),
            pltpu.VMEM((BR, 2 * PAD + 1, WIDTH, TILE), BF16),
            pltpu.VMEM((GROUPS * MOST, WIDTH, TILE), BF16),
            pltpu.VMEM((ITERS, GROUPS * MOST, WIDTH, TILE), BF16),
            pltpu.VMEM((LT, WIDTH, TILE), BF16),
            pltpu.VMEM((GROUPS * MOST, WIDTH, TILE), BF16),
            pltpu.VMEM((ITERS, GROUPS * MOST, WIDTH, TILE), BF16),
            pltpu.VMEM((STEP, 2 * PAD + 1, WIDTH, TILE), BF16),
            pltpu.VMEM((BR * WIDTH, TILE), F32),
            pltpu.VMEM((ITERS, SPLITS, QROWS, TILE), F32),
            pltpu.VMEM((BR * WIDTH, TILE), F32),
            pltpu.VMEM((BR * WIDTH, TILE), BF16),
            pltpu.VMEM((ITERS, SPLITS, QROWS, TILE), BF16),
            pltpu.VMEM((BR * WIDTH, TILE), F32),
            pltpu.VMEM((BR, len(RIGHT) * WIDTH, TILE), BF16),
            pltpu.VMEM((ITERS, NCORE * SPLITS, 8, HALF), F32),
            pltpu.VMEM((ITERS, NX * NY, 8, HALF), F32),
            dma(((LT + LOC) // CHUNK,)),
            dma((6,)),
            dma((1,)),
            dma((2,)),
            dma((2,)),
            dma((ITERS, 2)),
            dma((ITERS, 2)),
            dma((ITERS, 2)),
            dma((ITERS, 2)),
            dma((2,)),
            dma((ITERS, 2)),
            dma((ITERS, 2)),
        ],
        compiler_params=pltpu.CompilerParams(
            collective_id=0, has_side_effects=True, vmem_limit_bytes=60 << 20
        ),
        name="iterate",
    )(
        remote_groups[0], local_coords[0, 0].T, remote_coords[0, 0].T, local_gains[0, 0], remote_gains[0, 0],
        start_block, local_weights[0, 0], remote_weights[0, 0],
    )


def solution(mesh):
    in_specs = (
        P("rows", "cols", None, None, None),
        P("rows", "cols", None, None, None),
        P("rows", "cols", None, None),
        P("rows", "cols", None, None, None),
        P("rows", "cols", None, None, None),
        P("rows", "cols", None),
        P("rows", "cols", None, None),
        P(None, "rows"),
    )
    out_specs = P(None, ("rows", "cols"))
    return jax.shard_map(
        per_device, mesh=mesh, in_specs=in_specs, out_specs=out_specs, check_vma=False
    )
```

```python
import jax
import jax.numpy as jnp
from jax import lax
from jax.experimental import pallas as pl
from jax.experimental.pallas import tpu as pltpu
from jax.sharding import PartitionSpec as P

TILE = 256
HALF = 128
WIDTH = 16
BR = 16
MOST = 2
ITERS = 2
LOC = 48
LT = 32
GROUPS = 32
SPLITS = 4
QROWS = BR // SPLITS * WIDTH
NX, NY, NCORE = 4, 4, 2
CHUNK = 8
STEP = 4
VERTICES = GROUPS * BR * TILE
PAD = BR - 1
MESH = pl.DeviceIdType.MESH
VMEM = pl.BlockSpec(memory_space=pltpu.VMEM)
F32 = jnp.float32
BF16 = jnp.bfloat16

HBM = pl.BlockSpec(memory_space=pltpu.HBM)
T_REMOTE_ROW, T_REMOTE_COL, T_LOCAL_ROW, T_LOCAL_COL, T_SLOT, T_FIRST = range(6)
LEFT, RIGHT = (0, 0, 1, 0, 1, 2), (0, 1, 0, 2, 1, 0)


def ring(distance, size):
    return min(distance, size - distance)


PLANE = sorted(
    range(1, NX * NY * NCORE), key=lambda o: -ring(o // (NCORE * NY), NX) - ring(o // NCORE % NY, NY)
)
NEAR = sorted(range(1, NCORE * SPLITS), key=lambda o: -ring(o // NCORE, SPLITS))
FAR = sorted(range(1, NX * NY), key=lambda o: -ring(o // NY, NX) - ring(o % NY, NY))
DZ = (2, 1, 3)


def dot(a, b, dims=((1,), (0,))):
    return lax.dot_general(a, b, (dims, ((), ())), preferred_element_type=F32)


def split3(value):
    high = value.astype(BF16)
    rest = value - high.astype(F32)
    middle = rest.astype(BF16)
    return high, middle, (rest - middle.astype(F32)).astype(BF16)


def select_sum(hot, value, dims=((1,), (0,))):
    high, middle, low = split3(value)
    return dot(hot, high, dims) + (dot(hot, middle, dims) + dot(hot, low, dims))


def iota(shape, dim):
    return lax.broadcasted_iota(jnp.int32, shape, dim)


def factor_inverse(gram):
    copies = len(LEFT) * WIDTH
    shape = (WIDTH, HALF)
    row, lane = iota(shape, 0), iota(shape, 1)
    work = jnp.where((lane % WIDTH == row) & (lane < copies), 1.0, 0.0)
    columns = [jnp.broadcast_to(gram[:, k : k + 1], shape) for k in range(WIDTH)]
    roots = jnp.zeros(shape, F32)
    for k in range(WIDTH):
        pivot = jnp.broadcast_to(columns[k][k : k + 1, :], shape)
        roots = jnp.where(row == k, 1.0 / jnp.sqrt(pivot), roots)
        if k == WIDTH - 1:
            break
        factor = jnp.where(row > k, columns[k] * (1.0 / pivot), 0.0)
        for j in range(k + 1, WIDTH):
            columns[j] = columns[j] - factor * jnp.broadcast_to(columns[j][k : k + 1, :], shape)
        work = work - factor * jnp.broadcast_to(work[k : k + 1, :], shape)
    inverse = work * roots
    high, middle, low = (part.astype(F32) for part in split3(inverse))
    part = lane // WIDTH
    chosen = jnp.where((part == 2) | (part == 4), middle, jnp.where(part == 5, low, high))
    return chosen.astype(BF16)[:, 0:copies]


class Place:
    def __init__(self):
        self.me, self.z = lax.axis_index("rows"), lax.axis_index("cols")
        self.core, self.y, self.x = self.me % NCORE, (self.me // NCORE) % NY, self.me // (NCORE * NY)
        self.cores = [(self.core + d) % NCORE for d in range(NCORE)]
        self.ys = [((self.y + d) % NY) * NCORE for d in range(NY)]
        self.xs = [((self.x + d) % NX) * (NY * NCORE) for d in range(NX)]
        self.zs = [(self.z + d) % SPLITS for d in range(SPLITS)]

    def plane(self, offset):
        return self.xs[offset // (NCORE * NY)] + self.ys[(offset // NCORE) % NY] + self.cores[offset % NCORE]

    def split(self, dz):
        return self.zs[dz]

    def near(self, offset):
        return self.xs[0] + self.ys[0] + self.cores[offset % NCORE], self.zs[offset // NCORE]

    def far(self, offset):
        return self.xs[offset // NY] + self.ys[offset % NY] + self.core, self.z


def copy_to(source, target, send_sem, recv_sem, row, split):
    return pltpu.make_async_remote_copy(
        src_ref=source, dst_ref=target, send_sem=send_sem, recv_sem=recv_sem,
        device_id=(row, split), device_id_type=MESH,
    )


def wait_all(ref, send_sem, recv_sem, place):
    copy_to(ref, ref, send_sem, recv_sem, place.me, place.z).wait()


def loop(start, stop, body):
    def step(i, carry):
        body(i)
        return carry

    lax.fori_loop(start, stop, step, 0)


def whole_kernel(
    groups_h, local_coords_h, remote_coords_h, local_gains_h, remote_gains_h, start_h, local_w, remote_w,
    out,
    groups, local_coords, remote_coords, local_gains, remote_gains, start,
    eff, table_v, table, column_sums, sums, deg_out, deg_in, split_part, inv, spread, gather, row_blocks,
    padded, answer_out, answer_in, product, product_out, product_in, fetched, total,
    parts, late, late_out, late_in, image, image_parts, near_gram, far_gram,
    load_sem, small_sem, table_sem, deg_sem, zdeg_sem, answer_sem, product_sem,
    part_sem, late_sem, image_sem, near_sem, far_sem,
):
    at = Place()
    me, z = at.me, at.z
    first = LT // CHUNK
    chunks = (LT + LOC) // CHUNK

    def load(c):
        chunk = pl.ds(c * CHUNK, CHUNK)
        source = remote_w.at[chunk] if c < first else local_w.at[pl.ds((c - first) * CHUNK, CHUNK)]
        return pltpu.make_async_copy(source, eff.at[chunk], load_sem.at[c])

    small = [
        pltpu.make_async_copy(source, target, small_sem.at[i])
        for i, (source, target) in enumerate(
            [
                (groups_h, groups), (remote_coords_h, remote_coords), (local_coords_h, local_coords),
                (remote_gains_h, remote_gains), (local_gains_h, local_gains), (start_h, start),
            ]
        )
    ]
    for copy in small[:4]:
        copy.start()
    for c in range(chunks):
        load(c).start()
    for copy in small[4:]:
        copy.start()

    barrier = pltpu.get_barrier_semaphore()

    def signal(row, split):
        pl.semaphore_signal(barrier, inc=1, device_id=(row, split), device_id_type=MESH)

    for o in PLANE:
        signal(at.plane(o), z)
    for offset in range(2, NCORE * SPLITS):
        row, split = at.near(offset)
        signal(row, split)

    for copy in small[:3]:
        copy.wait()
    group = jnp.broadcast_to(groups[...], (GROUPS, LT))
    slot_group, tile_id = iota((GROUPS, LT), 0), iota((GROUPS, LT), 1)
    named = group == slot_group
    lowest = jnp.min(jnp.where(named, tile_id, LT - 1), axis=1, keepdims=True)
    highest = jnp.max(jnp.where(named, tile_id, -1), axis=1, keepdims=True)
    is_first, is_second = named & (tile_id == lowest), named & (tile_id == highest)
    slot = MOST * slot_group + jnp.where(is_second, 1, 0)
    named_t = jnp.transpose(group) == iota((LT, GROUPS), 1)
    tile_t = iota((LT, GROUPS), 0)
    table_v[...] = jnp.zeros_like(table_v)
    table_v[T_REMOTE_ROW : T_REMOTE_ROW + 2, 0:LT] = remote_coords[...]
    table_v[T_LOCAL_ROW : T_LOCAL_ROW + 2, 0:LOC] = local_coords[...]
    table_v[T_SLOT : T_SLOT + 1, 0:LT] = jnp.sum(jnp.where(named, slot, 0), axis=0, keepdims=True)
    table_v[T_FIRST : T_FIRST + 1, 0:GROUPS] = jnp.min(jnp.where(named_t, tile_t, LT - 1), axis=0, keepdims=True)
    table_v[T_FIRST + 1 : T_FIRST + 2, 0:GROUPS] = jnp.max(jnp.where(named_t, tile_t, 0), axis=0, keepdims=True)
    table_copy = pltpu.make_async_copy(table_v, table, table_sem.at[0])
    table_copy.start()
    hot_slots = jnp.concatenate([jnp.where(hot, 1.0, 0.0) for hot in (is_first, is_second)], axis=0)
    target = jnp.broadcast_to(remote_coords[1:2, :].astype(F32) + 1.0, (MOST * GROUPS, LT))
    slot_column = jnp.sum(hot_slots * target, axis=1, keepdims=True) - 1.0
    slot_column = jnp.broadcast_to(slot_column, (MOST * GROUPS, HALF))
    hot_slots = hot_slots.astype(BF16)
    small[3].wait()

    def pair(p):
        return pl.ds(MOST * p, MOST)

    ones = jnp.ones((8, TILE), BF16)

    def scale(tile0, gains, gain0, row_at, keep, col_at):
        row_gains = jnp.concatenate([gains[gain0 + t, 0:1, :] for t in range(CHUNK)], axis=0).T
        for t in range(CHUNK):
            scaled = (
                row_gains[:, t : t + 1] * eff[tile0 + t].astype(F32) * gains[gain0 + t, 1:2, :]
            ).astype(BF16)
            eff[tile0 + t] = scaled
            size = jnp.abs(scaled)
            sums[pl.ds(row_at + t, 1), :] = dot(ones, size, ((1,), (1,)))[0:1, :]
            keep(col_at + t, dot(ones, size))

    def remote_chunk(c):
        chunk = pl.ds(c * CHUNK, CHUNK)
        pltpu.make_async_copy(remote_w.at[chunk], eff.at[chunk], load_sem.at[c]).wait()

        def keep(t, value):
            column_sums[pl.ds(t, 1), :] = value[0:1, :]

        scale(c * CHUNK, remote_gains, c * CHUNK, c * CHUNK, keep, c * CHUNK)

    def local_chunk(c):
        pltpu.make_async_copy(
            local_w.at[pl.ds(c * CHUNK, CHUNK)],
            eff.at[pl.ds(LT + c * CHUNK, CHUNK)],
            load_sem.at[first + c],
        ).wait()

        def keep(t, value):
            sums[pl.ds(t, 1), :] = value[0:1, :]

        scale(LT + c * CHUNK, local_gains, c * CHUNK, LT + c * CHUNK, keep, LT + LOC + c * CHUNK)

    loop(0, first, remote_chunk)
    pl.semaphore_wait(barrier, GROUPS - 1 + NCORE * SPLITS - 2)

    slot_sums = select_sum(hot_slots, column_sums[...])
    for p in range(GROUPS):
        pieces = []
        for s in range(MOST):
            row = slot_sums[s * GROUPS + p : s * GROUPS + p + 1, :]
            pieces += [row[:, 0:HALF], row[:, HALF:TILE]]
        for s in range(MOST):
            pieces += [slot_column[s * GROUPS + p : s * GROUPS + p + 1, :]] * 2
        deg_out[p] = jnp.concatenate(pieces, axis=0)
    for o in PLANE:
        to = at.plane(o)
        copy_to(deg_out.at[to], deg_in.at[me], deg_sem.at[0], deg_sem.at[1], to, z).start()
    deg_in[me] = deg_out[me]
    small[4].wait()
    loop(0, LOC // CHUNK, local_chunk)
    small[5].wait()
    table_copy.wait()

    def hot_rows(row):
        return jnp.where(jnp.broadcast_to(row, (BR, row.shape[1])) == iota((BR, row.shape[1]), 0), 1.0, 0.0).astype(BF16)

    own = select_sum(hot_rows(remote_coords[0:1, :]), sums[0:LT, :])
    own += select_sum(hot_rows(local_coords[0:1, :]), sums[LT : LT + LOC, :])
    own += select_sum(hot_rows(local_coords[1:2, :]), sums[LT + LOC : LT + 2 * LOC, :])
    wait_all(deg_in.at[pl.ds(0, GROUPS - 1)], deg_sem.at[0], deg_sem.at[1], at)
    came = deg_in[...].reshape(GROUPS * 8, HALF)
    column = pltpu.roll(came, GROUPS * 8 - 4, 0)
    row8 = iota((GROUPS * 8, HALF), 0) % 8
    lane_f = iota((GROUPS * 8, HALF), 1).astype(F32)
    added = []
    for half in range(2):
        chosen = (column == lane_f) & ((row8 == half) | (row8 == 2 + half))
        hot = jnp.where(chosen, 1.0, 0.0).astype(BF16)
        added.append(select_sum(hot, came, ((0,), (0,)))[0:BR, :])
    split_part[z] = own + jnp.concatenate(added, axis=1)

    for dz in DZ:
        copy_to(split_part.at[z], split_part.at[z], zdeg_sem.at[0], zdeg_sem.at[1], me, at.split(dz)).start()

    padded[...] = jnp.zeros_like(padded)
    fetched[...] = jnp.zeros_like(fetched)
    row = iota((BR * WIDTH, HALF), 0)
    lane = iota((BR * WIDTH, HALF), 1)
    row_tile = (row // WIDTH).astype(F32)
    lanes = iota((1, HALF), 1)
    per = HALF // WIDTH
    for q in range(GROUPS * MOST // per):
        column = jnp.zeros((1, HALF), F32)
        for i in range(per):
            at_slot = deg_in[q * (per // MOST) + i // MOST, 4 + 2 * (i % MOST) : 5 + 2 * (i % MOST), :]
            column = jnp.where(lanes // WIDTH == i, at_slot, column)
        chosen = (jnp.broadcast_to(column, row.shape) == row_tile) & (lane % WIDTH == row % WIDTH)
        spread[:, q * HALF : (q + 1) * HALF] = jnp.where(chosen, 1.0, 0.0).astype(BF16)
    lane = iota((WIDTH, TILE), 1)
    diagonal = lane % WIDTH == iota((WIDTH, TILE), 0)
    lane_tile = (lane // WIDTH).astype(F32)
    for slot in range(GROUPS * MOST):
        own = deg_in[slot // MOST, 4 + 2 * (slot % MOST) : 5 + 2 * (slot % MOST), :]
        own = jnp.broadcast_to(jnp.concatenate([own, own], axis=1), (WIDTH, TILE))
        gather[slot * WIDTH : (slot + 1) * WIDTH, :] = jnp.where(diagonal & (own == lane_tile), 1.0, 0.0).astype(BF16)

    wait_all(split_part.at[pl.ds(0, SPLITS - 1)], zdeg_sem.at[0], zdeg_sem.at[1], at)
    inv[...] = 1.0 / jnp.sqrt((split_part[0] + split_part[1]) + (split_part[2] + split_part[3]))

    def set_rows(j, vectors):
        scaled = (vectors * inv[j : j + 1, :]).astype(BF16)
        row_blocks[j] = scaled

    for j in range(BR):
        set_rows(j, start[:, j * TILE : (j + 1) * TILE])

    for it in range(ITERS):
        last = it == ITERS - 1
        a_in, p_in = answer_in.at[it], product_in.at[it]

        answer_out[...] = (
            dot(gather[...], row_blocks[...].reshape(BR * WIDTH, TILE)).astype(BF16).reshape(answer_out.shape)
        )

        for o in PLANE:
            to = at.plane(o)
            copy_to(
                answer_out.at[pair(to)], a_in.at[pair(me)], answer_sem.at[it, 0], answer_sem.at[it, 1], to, z
            ).start()
        a_in[pair(me)] = answer_out[pair(me)]

        def backward(i):
            for u in range(STEP):
                tile = i * STEP + u
                x = row_blocks[table[T_REMOTE_ROW, tile]]
                product[tile] = dot(x, eff[tile]).astype(BF16)

        loop(0, LT // STEP, backward)

        def fill_product(p, ref):
            for s in range(MOST):
                ref[MOST * p + s] = product[table[T_FIRST + s, p]]

        for o in PLANE:
            to = at.plane(o)
            fill_product(to, product_out)
            copy_to(
                product_out.at[pair(to)], p_in.at[pair(me)], product_sem.at[it, 0], product_sem.at[it, 1], to, z
            ).start()
        fill_product(me, p_in)

        for j in range(BR):
            padded[j, PAD] = row_blocks[j]

        total[...] = jnp.zeros_like(total)

        def window(ref, index, row_tile):
            return ref[index, pl.ds(PAD - row_tile, BR)].reshape(BR * WIDTH, TILE)

        def local(i):
            value = total[...]
            for u in range(STEP):
                tile = i * STEP + u
                r, c = table[T_LOCAL_ROW, tile], table[T_LOCAL_COL, tile]
                value += dot(window(padded, c, r), eff[LT + tile], ((1,), (1,)))
                value += dot(window(padded, r, c), eff[LT + tile])
            total[...] = value

        loop(0, LOC // STEP, local)

        for dz in DZ:
            other = at.split(dz)
            copy_to(
                total.at[pl.ds(other * QROWS, QROWS)], parts.at[it, dz], part_sem.at[it, 0], part_sem.at[it, 1], me, other
            ).start()
        late[...] = jnp.zeros_like(late)

        others = pl.ds(0, MOST * (GROUPS - 1))
        wait_all(a_in.at[others], answer_sem.at[it, 0], answer_sem.at[it, 1], at)

        def forward(i):
            value = late[...]
            for u in range(STEP):
                tile = i * STEP + u
                slot = table[T_SLOT, tile]
                fetched[u, PAD] = a_in[slot]
                value += dot(window(fetched, u, table[T_REMOTE_ROW, tile]), eff[tile], ((1,), (1,)))
            late[...] = value

        loop(0, LT // STEP, forward)

        wait_all(p_in.at[others], product_sem.at[it, 0], product_sem.at[it, 1], at)
        rest = late[...] + dot(spread[...], p_in[...].reshape(GROUPS * MOST * WIDTH, TILE))
        late_out[...] = rest.astype(BF16)

        for dz in DZ:
            other = at.split(dz)
            copy_to(
                late_out.at[pl.ds(other * QROWS, QROWS)], late_in.at[it, dz],
                late_sem.at[it, 0], late_sem.at[it, 1], me, other,
            ).start()
        late[...] = rest
        mine = pl.ds(z * QROWS, QROWS)
        wait_all(parts.at[it, pl.ds(1, SPLITS - 1)], part_sem.at[it, 0], part_sem.at[it, 1], at)
        summed = (total[mine, :] + late[mine, :]) + ((parts[it, 1] + parts[it, 2]) + parts[it, 3])
        wait_all(late_in.at[it, pl.ds(1, SPLITS - 1)], late_sem.at[it, 0], late_sem.at[it, 1], at)
        summed += (late_in[it, 1].astype(F32) + late_in[it, 2].astype(F32)) + late_in[it, 3].astype(F32)
        tiles = [
            summed[j * WIDTH : (j + 1) * WIDTH, :] * inv[pl.ds(z * (BR // SPLITS) + j, 1), :]
            for j in range(BR // SPLITS)
        ]
        wide = jnp.concatenate(tiles, axis=1)
        wide_parts = split3(wide)
        stacked = jnp.concatenate(wide_parts, axis=0)
        crossed = dot(stacked, stacked, ((1,), (1,)))

        def cross(i, j):
            return crossed[i * WIDTH : (i + 1) * WIDTH, j * WIDTH : (j + 1) * WIDTH]

        gram = cross(0, 0) + ((cross(0, 1) + cross(1, 0)) + ((cross(0, 2) + cross(2, 0)) + cross(1, 1)))
        packed = jnp.concatenate([gram[0:8], gram[8:16], jnp.zeros((8, HALF - 2 * WIDTH), F32)], axis=1)

        own = z * NCORE + at.core
        near_gram[it, own] = packed
        for offset in NEAR:
            row, split = at.near(offset)
            copy_to(
                near_gram.at[it, own], near_gram.at[it, own], near_sem.at[it, 0], near_sem.at[it, 1], row, split
            ).start()
        if not last:
            image[mine, :] = jnp.concatenate(tiles, axis=0)
            for dz in DZ:
                copy_to(image.at[mine], image.at[mine], image_sem.at[0], image_sem.at[1], me, at.split(dz)).start()
        wait_all(near_gram.at[it, pl.ds(0, NCORE * SPLITS - 1)], near_sem.at[it, 0], near_sem.at[it, 1], at)
        near_sum = near_gram[it, 0]
        for i in range(1, NCORE * SPLITS):
            near_sum = near_sum + near_gram[it, i]

        own = at.x * NY + at.y
        far_gram[it, own] = near_sum
        for offset in FAR:
            row, split = at.far(offset)
            copy_to(
                far_gram.at[it, own], far_gram.at[it, own], far_sem.at[it, 0], far_sem.at[it, 1], row, split
            ).start()
        if not last:
            wait_all(image.at[pl.ds(0, (SPLITS - 1) * QROWS)], image_sem.at[0], image_sem.at[1], at)
            for j in range(BR):
                pieces = split3(image[j * WIDTH : (j + 1) * WIDTH, :])
                image_parts[j] = jnp.concatenate([pieces[i] for i in RIGHT], axis=0)
        wait_all(far_gram.at[it, pl.ds(0, NX * NY - 1)], far_sem.at[it, 0], far_sem.at[it, 1], at)
        packed = far_gram[it, 0]
        for i in range(1, NX * NY):
            packed = packed + far_gram[it, i]
        gram = jnp.concatenate([packed[:, 0:WIDTH], packed[:, WIDTH : 2 * WIDTH]], axis=0)
        inverse = factor_inverse(gram / VERTICES)
        if last:
            out[...] = dot(inverse, jnp.concatenate([wide_parts[i] for i in RIGHT], axis=0))
        else:
            for j in range(BR):
                set_rows(j, dot(inverse, image_parts[j]))


def per_device(
    local_weights, local_gains, local_coords, remote_weights, remote_gains, remote_groups, remote_coords, start_block
):
    dma = pltpu.SemaphoreType.DMA
    return pl.pallas_call(
        whole_kernel,
        out_shape=pltpu.VMEM((WIDTH, QROWS // WIDTH * TILE), F32),
        in_specs=[HBM] * 8,
        out_specs=VMEM,
        scratch_shapes=[
            pltpu.VMEM((1, LT), jnp.int32),
            pltpu.VMEM((2, LOC), jnp.int32),
            pltpu.VMEM((2, LT), jnp.int32),
            pltpu.VMEM((LOC, 2, TILE), F32),
            pltpu.VMEM((LT, 2, TILE), F32),
            pltpu.VMEM((WIDTH, BR * TILE), F32),
            pltpu.VMEM((LT + LOC, TILE, TILE), BF16),
            pltpu.VMEM((8, HALF), jnp.int32),
            pltpu.SMEM((8, HALF), jnp.int32),
            pltpu.VMEM((LT, TILE), F32),
            pltpu.VMEM((LT + 2 * LOC, TILE), F32),
            pltpu.VMEM((GROUPS, 8, HALF), F32),
            pltpu.VMEM((GROUPS, 8, HALF), F32),
            pltpu.VMEM((SPLITS, BR, TILE), F32),
            pltpu.VMEM((BR, TILE), F32),
            pltpu.VMEM((BR * WIDTH, GROUPS * MOST * WIDTH), BF16),
            pltpu.VMEM((GROUPS * MOST * WIDTH, BR * WIDTH), BF16),
            pltpu.VMEM((BR, WIDTH, TILE), BF16),
            pltpu.VMEM((BR, 2 * PAD + 1, WIDTH, TILE), BF16),
            pltpu.VMEM((GROUPS * MOST, WIDTH, TILE), BF16),
            pltpu.VMEM((ITERS, GROUPS * MOST, WIDTH, TILE), BF16),
            pltpu.VMEM((LT, WIDTH, TILE), BF16),
            pltpu.VMEM((GROUPS * MOST, WIDTH, TILE), BF16),
            pltpu.VMEM((ITERS, GROUPS * MOST, WIDTH, TILE), BF16),
            pltpu.VMEM((STEP, 2 * PAD + 1, WIDTH, TILE), BF16),
            pltpu.VMEM((BR * WIDTH, TILE), F32),
            pltpu.VMEM((ITERS, SPLITS, QROWS, TILE), F32),
            pltpu.VMEM((BR * WIDTH, TILE), F32),
            pltpu.VMEM((BR * WIDTH, TILE), BF16),
            pltpu.VMEM((ITERS, SPLITS, QROWS, TILE), BF16),
            pltpu.VMEM((BR * WIDTH, TILE), F32),
            pltpu.VMEM((BR, len(RIGHT) * WIDTH, TILE), BF16),
            pltpu.VMEM((ITERS, NCORE * SPLITS, 8, HALF), F32),
            pltpu.VMEM((ITERS, NX * NY, 8, HALF), F32),
            dma(((LT + LOC) // CHUNK,)),
            dma((6,)),
            dma((1,)),
            dma((2,)),
            dma((2,)),
            dma((ITERS, 2)),
            dma((ITERS, 2)),
            dma((ITERS, 2)),
            dma((ITERS, 2)),
            dma((2,)),
            dma((ITERS, 2)),
            dma((ITERS, 2)),
        ],
        compiler_params=pltpu.CompilerParams(
            collective_id=0, has_side_effects=True, vmem_limit_bytes=60 << 20
        ),
        name="iterate",
    )(
        remote_groups[0], local_coords[0, 0].T, remote_coords[0, 0].T, local_gains[0, 0], remote_gains[0, 0],
        start_block, local_weights[0, 0], remote_weights[0, 0],
    )


def solution(mesh):
    in_specs = (
        P("rows", "cols", None, None, None),
        P("rows", "cols", None, None, None),
        P("rows", "cols", None, None),
        P("rows", "cols", None, None, None),
        P("rows", "cols", None, None, None),
        P("rows", "cols", None),
        P("rows", "cols", None, None),
        P(None, "rows"),
    )
    out_specs = P(None, ("rows", "cols"))
    return jax.shard_map(
        per_device, mesh=mesh, in_specs=in_specs, out_specs=out_specs, check_vma=False
    )
```

```python
import jax
import jax.numpy as jnp
from jax import lax
from jax.experimental import pallas as pl
from jax.experimental.pallas import tpu as pltpu
from jax.sharding import PartitionSpec as P

TILE = 256
HALF = 128
WIDTH = 16
BR = 16
MOST = 2
ITERS = 2
LOC = 48
LT = 32
GROUPS = 32
SPLITS = 4
QROWS = BR // SPLITS * WIDTH
NX, NY, NCORE = 4, 4, 2
CHUNK = 8
STEP = 4
VERTICES = GROUPS * BR * TILE
PAD = BR - 1
MESH = pl.DeviceIdType.MESH
VMEM = pl.BlockSpec(memory_space=pltpu.VMEM)
F32 = jnp.float32
BF16 = jnp.bfloat16

HBM = pl.BlockSpec(memory_space=pltpu.HBM)
T_REMOTE_ROW, T_REMOTE_COL, T_LOCAL_ROW, T_LOCAL_COL, T_SLOT, T_FIRST = range(6)
LEFT, RIGHT = (0, 0, 1, 0, 1, 2), (0, 1, 0, 2, 1, 0)


def ring(distance, size):
    return min(distance, size - distance)


PLANE = sorted(
    range(1, NX * NY * NCORE), key=lambda o: -ring(o // (NCORE * NY), NX) - ring(o // NCORE % NY, NY)
)
NEAR = sorted(range(1, NCORE * SPLITS), key=lambda o: -ring(o // NCORE, SPLITS))
FAR = sorted(range(1, NX * NY), key=lambda o: -ring(o // NY, NX) - ring(o % NY, NY))
DZ = (2, 1, 3)


def dot(a, b, dims=((1,), (0,))):
    return lax.dot_general(a, b, (dims, ((), ())), preferred_element_type=F32)


def split3(value):
    high = value.astype(BF16)
    rest = value - high.astype(F32)
    middle = rest.astype(BF16)
    return high, middle, (rest - middle.astype(F32)).astype(BF16)


def select_sum(hot, value, dims=((1,), (0,))):
    high, middle, low = split3(value)
    return dot(hot, high, dims) + (dot(hot, middle, dims) + dot(hot, low, dims))


def iota(shape, dim):
    return lax.broadcasted_iota(jnp.int32, shape, dim)


def factor_inverse(gram):
    copies = len(LEFT) * WIDTH
    shape = (WIDTH, HALF)
    row, lane = iota(shape, 0), iota(shape, 1)
    work = jnp.where((lane % WIDTH == row) & (lane < copies), 1.0, 0.0)
    columns = [jnp.broadcast_to(gram[:, k : k + 1], shape) for k in range(WIDTH)]
    roots = jnp.zeros(shape, F32)
    for k in range(WIDTH):
        pivot = jnp.broadcast_to(columns[k][k : k + 1, :], shape)
        roots = jnp.where(row == k, 1.0 / jnp.sqrt(pivot), roots)
        if k == WIDTH - 1:
            break
        factor = jnp.where(row > k, columns[k] * (1.0 / pivot), 0.0)
        for j in range(k + 1, WIDTH):
            columns[j] = columns[j] - factor * jnp.broadcast_to(columns[j][k : k + 1, :], shape)
        work = work - factor * jnp.broadcast_to(work[k : k + 1, :], shape)
    inverse = work * roots
    high, middle, low = (part.astype(F32) for part in split3(inverse))
    part = lane // WIDTH
    chosen = jnp.where((part == 2) | (part == 4), middle, jnp.where(part == 5, low, high))
    return chosen.astype(BF16)[:, 0:copies]


class Place:
    def __init__(self):
        self.me, self.z = lax.axis_index("rows"), lax.axis_index("cols")
        self.core, self.y, self.x = self.me % NCORE, (self.me // NCORE) % NY, self.me // (NCORE * NY)
        self.cores = [(self.core + d) % NCORE for d in range(NCORE)]
        self.ys = [((self.y + d) % NY) * NCORE for d in range(NY)]
        self.xs = [((self.x + d) % NX) * (NY * NCORE) for d in range(NX)]
        self.zs = [(self.z + d) % SPLITS for d in range(SPLITS)]

    def plane(self, offset):
        return self.xs[offset // (NCORE * NY)] + self.ys[(offset // NCORE) % NY] + self.cores[offset % NCORE]

    def split(self, dz):
        return self.zs[dz]

    def near(self, offset):
        return self.xs[0] + self.ys[0] + self.cores[offset % NCORE], self.zs[offset // NCORE]

    def far(self, offset):
        return self.xs[offset // NY] + self.ys[offset % NY] + self.core, self.z


def copy_to(source, target, send_sem, recv_sem, row, split):
    return pltpu.make_async_remote_copy(
        src_ref=source, dst_ref=target, send_sem=send_sem, recv_sem=recv_sem,
        device_id=(row, split), device_id_type=MESH,
    )


def wait_all(ref, send_sem, recv_sem, place):
    copy_to(ref, ref, send_sem, recv_sem, place.me, place.z).wait()


def loop(start, stop, body):
    def step(i, carry):
        body(i)
        return carry

    lax.fori_loop(start, stop, step, 0)


def whole_kernel(
    groups_h, local_coords_h, remote_coords_h, local_gains_h, remote_gains_h, start_h, local_w, remote_w,
    out,
    groups, local_coords, remote_coords, local_gains, remote_gains, start,
    eff, table_v, table, column_sums, sums, deg_out, deg_in, split_part, inv, spread, gather, row_blocks,
    padded, answer_out, answer_in, product, product_out, product_in, fetched, total,
    parts, late, late_out, late_in, image, image_parts, near_gram, far_gram,
    load_sem, small_sem, table_sem, deg_sem, zdeg_sem, answer_sem, product_sem,
    part_sem, late_sem, image_sem, near_sem, far_sem,
):
    at = Place()
    me, z = at.me, at.z
    first = LT // CHUNK
    chunks = (LT + LOC) // CHUNK

    def load(c):
        chunk = pl.ds(c * CHUNK, CHUNK)
        source = remote_w.at[chunk] if c < first else local_w.at[pl.ds((c - first) * CHUNK, CHUNK)]
        return pltpu.make_async_copy(source, eff.at[chunk], load_sem.at[c])

    small = [
        pltpu.make_async_copy(source, target, small_sem.at[i])
        for i, (source, target) in enumerate(
            [
                (groups_h, groups), (remote_coords_h, remote_coords), (local_coords_h, local_coords),
                (remote_gains_h, remote_gains), (local_gains_h, local_gains), (start_h, start),
            ]
        )
    ]
    small[3].start()
    for c in range(first):
        load(c).start()
    for copy in small[:3]:
        copy.start()

    barrier = pltpu.get_barrier_semaphore()
    greeted = [(at.plane(o), z) for o in PLANE] + [at.near(o) for o in NEAR if o >= NCORE]

    def pair(p):
        return pl.ds(MOST * p, MOST)

    ones = jnp.ones((8, TILE), BF16)

    def scale(tile0, gains, gain0, row_at, keep, col_at):
        row_gains = jnp.concatenate([gains[gain0 + t, 0:1, :] for t in range(CHUNK)], axis=0).T
        for t in range(CHUNK):
            scaled = (
                row_gains[:, t : t + 1] * eff[tile0 + t].astype(F32) * gains[gain0 + t, 1:2, :]
            ).astype(BF16)
            eff[tile0 + t] = scaled
            size = jnp.abs(scaled)
            sums[pl.ds(row_at + t, 1), :] = dot(ones, size, ((1,), (1,)))[0:1, :]
            keep(col_at + t, dot(ones, size))

    def remote_chunk(c):
        chunk = pl.ds(c * CHUNK, CHUNK)
        pltpu.make_async_copy(remote_w.at[chunk], eff.at[chunk], load_sem.at[c]).wait()

        def keep(t, value):
            column_sums[pl.ds(t, 1), :] = value[0:1, :]

        scale(c * CHUNK, remote_gains, c * CHUNK, c * CHUNK, keep, c * CHUNK)

    def local_chunk(c):
        pltpu.make_async_copy(
            local_w.at[pl.ds(c * CHUNK, CHUNK)],
            eff.at[pl.ds(LT + c * CHUNK, CHUNK)],
            load_sem.at[first + c],
        ).wait()

        def keep(t, value):
            sums[pl.ds(t, 1), :] = value[0:1, :]

        scale(LT + c * CHUNK, local_gains, c * CHUNK, LT + c * CHUNK, keep, LT + LOC + c * CHUNK)

    small[3].wait()
    share = -(-len(greeted) // (first - 1))
    later = [load(c) for c in range(first, chunks)] + small[4:]
    for c in range(first):
        for row, split in greeted[c * share : (c + 1) * share]:
            pl.semaphore_signal(barrier, inc=1, device_id=(row, split), device_id_type=MESH)
        for copy in later[c * 2 : c * 2 + 2]:
            copy.start()
        remote_chunk(c)

    for copy in small[:3]:
        copy.wait()
    group = jnp.broadcast_to(groups[...], (GROUPS, LT))
    slot_group, tile_id = iota((GROUPS, LT), 0), iota((GROUPS, LT), 1)
    named = group == slot_group
    lowest = jnp.min(jnp.where(named, tile_id, LT - 1), axis=1, keepdims=True)
    highest = jnp.max(jnp.where(named, tile_id, -1), axis=1, keepdims=True)
    is_first, is_second = named & (tile_id == lowest), named & (tile_id == highest)
    slot = MOST * slot_group + jnp.where(is_second, 1, 0)
    named_t = jnp.transpose(group) == iota((LT, GROUPS), 1)
    tile_t = iota((LT, GROUPS), 0)
    table_v[...] = jnp.zeros_like(table_v)
    table_v[T_REMOTE_ROW : T_REMOTE_ROW + 2, 0:LT] = remote_coords[...]
    table_v[T_LOCAL_ROW : T_LOCAL_ROW + 2, 0:LOC] = local_coords[...]
    table_v[T_SLOT : T_SLOT + 1, 0:LT] = jnp.sum(jnp.where(named, slot, 0), axis=0, keepdims=True)
    table_v[T_FIRST : T_FIRST + 1, 0:GROUPS] = jnp.min(jnp.where(named_t, tile_t, LT - 1), axis=0, keepdims=True)
    table_v[T_FIRST + 1 : T_FIRST + 2, 0:GROUPS] = jnp.max(jnp.where(named_t, tile_t, 0), axis=0, keepdims=True)
    table_copy = pltpu.make_async_copy(table_v, table, table_sem.at[0])
    table_copy.start()
    hot_slots = jnp.concatenate([jnp.where(hot, 1.0, 0.0) for hot in (is_first, is_second)], axis=0)
    target = jnp.broadcast_to(remote_coords[1:2, :].astype(F32) + 1.0, (MOST * GROUPS, LT))
    slot_column = jnp.sum(hot_slots * target, axis=1, keepdims=True) - 1.0
    slot_column = jnp.broadcast_to(slot_column, (MOST * GROUPS, HALF))
    hot_slots = hot_slots.astype(BF16)

    pl.semaphore_wait(barrier, GROUPS - 1 + NCORE * SPLITS - 2)

    lanes = iota((1, HALF), 1)
    slot_sums = select_sum(hot_slots, column_sums[...])
    for p in range(GROUPS):
        pieces = []
        for s in range(MOST):
            row = slot_sums[s * GROUPS + p : s * GROUPS + p + 1, :]
            pieces += [row[:, 0:HALF], row[:, HALF:TILE]]
        columns = [slot_column[s * GROUPS + p : s * GROUPS + p + 1, :] for s in range(MOST)]
        by_lane = jnp.where(lanes % 8 < 2, columns[0], jnp.where(lanes % 8 < 4, columns[1], -1.0))
        deg_out[p] = jnp.concatenate(pieces + [by_lane, *columns, jnp.zeros((1, HALF), F32)], axis=0)
    for o in PLANE:
        to = at.plane(o)
        copy_to(deg_out.at[to], deg_in.at[me], deg_sem.at[0], deg_sem.at[1], to, z).start()
    deg_in[me] = deg_out[me]
    small[4].wait()
    loop(0, LOC // CHUNK, local_chunk)
    small[5].wait()
    table_copy.wait()

    def hot_rows(row):
        return jnp.where(jnp.broadcast_to(row, (BR, row.shape[1])) == iota((BR, row.shape[1]), 0), 1.0, 0.0).astype(BF16)

    own = select_sum(hot_rows(remote_coords[0:1, :]), sums[0:LT, :])
    own += select_sum(hot_rows(local_coords[0:1, :]), sums[LT : LT + LOC, :])
    own += select_sum(hot_rows(local_coords[1:2, :]), sums[LT + LOC : LT + 2 * LOC, :])
    wait_all(deg_in.at[pl.ds(0, GROUPS - 1)], deg_sem.at[0], deg_sem.at[1], at)
    came = deg_in[...].reshape(GROUPS * 8, HALF)
    blocks = []
    for b in range(GROUPS * 8 // HALF):
        column = jnp.full((1, HALF), -1.0, F32)
        for i in range(HALF // 8):
            column = jnp.where(lanes // 8 == i, deg_in[b * (HALF // 8) + i, 4:5, :], column)
        blocks.append(column)
    column = jnp.broadcast_to(jnp.concatenate(blocks, axis=1), (2 * BR, GROUPS * 8))
    row, lane8 = iota(column.shape, 0), iota(column.shape, 1) % 4
    chosen = (column == (row % BR).astype(F32)) & (lane8 % 2 == row // BR)
    added = select_sum(jnp.where(chosen, 1.0, 0.0).astype(BF16), came)
    split_part[z] = own + jnp.concatenate([added[0:BR, :], added[BR : 2 * BR, :]], axis=1)

    for dz in DZ:
        copy_to(split_part.at[z], split_part.at[z], zdeg_sem.at[0], zdeg_sem.at[1], me, at.split(dz)).start()

    padded[...] = jnp.zeros_like(padded)
    fetched[...] = jnp.zeros_like(fetched)
    row = iota((BR * WIDTH, HALF), 0)
    lane = iota((BR * WIDTH, HALF), 1)
    row_tile = (row // WIDTH).astype(F32)
    per = HALF // WIDTH
    for q in range(GROUPS * MOST // per):
        column = jnp.zeros((1, HALF), F32)
        for i in range(per):
            at_slot = deg_in[q * (per // MOST) + i // MOST, 5 + i % MOST : 6 + i % MOST, :]
            column = jnp.where(lanes // WIDTH == i, at_slot, column)
        chosen = (jnp.broadcast_to(column, row.shape) == row_tile) & (lane % WIDTH == row % WIDTH)
        spread[:, q * HALF : (q + 1) * HALF] = jnp.where(chosen, 1.0, 0.0).astype(BF16)
    lane = iota((WIDTH, TILE), 1)
    diagonal = lane % WIDTH == iota((WIDTH, TILE), 0)
    lane_tile = (lane // WIDTH).astype(F32)
    for slot in range(GROUPS * MOST):
        own = deg_in[slot // MOST, 5 + slot % MOST : 6 + slot % MOST, :]
        own = jnp.broadcast_to(jnp.concatenate([own, own], axis=1), (WIDTH, TILE))
        gather[slot * WIDTH : (slot + 1) * WIDTH, :] = jnp.where(diagonal & (own == lane_tile), 1.0, 0.0).astype(BF16)

    wait_all(split_part.at[pl.ds(0, SPLITS - 1)], zdeg_sem.at[0], zdeg_sem.at[1], at)
    inv[...] = 1.0 / jnp.sqrt((split_part[0] + split_part[1]) + (split_part[2] + split_part[3]))

    def set_rows(j, vectors):
        scaled = (vectors * inv[j : j + 1, :]).astype(BF16)
        row_blocks[j] = scaled

    for j in range(BR):
        set_rows(j, start[:, j * TILE : (j + 1) * TILE])

    for it in range(ITERS):
        last = it == ITERS - 1
        a_in, p_in = answer_in.at[it], product_in.at[it]

        answer_out[...] = (
            dot(gather[...], row_blocks[...].reshape(BR * WIDTH, TILE)).astype(BF16).reshape(answer_out.shape)
        )

        for o in PLANE:
            to = at.plane(o)
            copy_to(
                answer_out.at[pair(to)], a_in.at[pair(me)], answer_sem.at[it, 0], answer_sem.at[it, 1], to, z
            ).start()
        a_in[pair(me)] = answer_out[pair(me)]

        def backward(i):
            for u in range(STEP):
                tile = i * STEP + u
                x = row_blocks[table[T_REMOTE_ROW, tile]]
                product[tile] = dot(x, eff[tile]).astype(BF16)

        loop(0, LT // STEP, backward)

        def fill_product(p, ref):
            for s in range(MOST):
                ref[MOST * p + s] = product[table[T_FIRST + s, p]]

        for o in PLANE:
            to = at.plane(o)
            fill_product(to, product_out)
            copy_to(
                product_out.at[pair(to)], p_in.at[pair(me)], product_sem.at[it, 0], product_sem.at[it, 1], to, z
            ).start()
        fill_product(me, p_in)

        for j in range(BR):
            padded[j, PAD] = row_blocks[j]

        total[...] = jnp.zeros_like(total)

        def window(ref, index, row_tile):
            return ref[index, pl.ds(PAD - row_tile, BR)].reshape(BR * WIDTH, TILE)

        def local(i):
            value = total[...]
            for u in range(STEP):
                tile = i * STEP + u
                r, c = table[T_LOCAL_ROW, tile], table[T_LOCAL_COL, tile]
                value += dot(window(padded, c, r), eff[LT + tile], ((1,), (1,)))
                value += dot(window(padded, r, c), eff[LT + tile])
            total[...] = value

        loop(0, LOC // STEP, local)

        for dz in DZ:
            other = at.split(dz)
            copy_to(
                total.at[pl.ds(other * QROWS, QROWS)], parts.at[it, dz], part_sem.at[it, 0], part_sem.at[it, 1], me, other
            ).start()
        late[...] = jnp.zeros_like(late)

        others = pl.ds(0, MOST * (GROUPS - 1))
        wait_all(a_in.at[others], answer_sem.at[it, 0], answer_sem.at[it, 1], at)

        def forward(i):
            value = late[...]
            for u in range(STEP):
                tile = i * STEP + u
                slot = table[T_SLOT, tile]
                fetched[u, PAD] = a_in[slot]
                value += dot(window(fetched, u, table[T_REMOTE_ROW, tile]), eff[tile], ((1,), (1,)))
            late[...] = value

        loop(0, LT // STEP, forward)

        wait_all(p_in.at[others], product_sem.at[it, 0], product_sem.at[it, 1], at)
        came = p_in[...].reshape(GROUPS * MOST * WIDTH, TILE)
        for dz in (*DZ, 0):
            other = at.split(dz)
            rows = pl.ds(pl.multiple_of(other * QROWS, QROWS), QROWS)
            rest = late[rows, :] + dot(spread[rows, :], came)
            if dz:
                late_out[rows, :] = rest.astype(BF16)
                copy_to(
                    late_out.at[rows], late_in.at[it, dz], late_sem.at[it, 0], late_sem.at[it, 1], me, other
                ).start()
        mine = pl.ds(z * QROWS, QROWS)
        wait_all(parts.at[it, pl.ds(1, SPLITS - 1)], part_sem.at[it, 0], part_sem.at[it, 1], at)
        summed = (total[mine, :] + rest) + ((parts[it, 1] + parts[it, 2]) + parts[it, 3])
        wait_all(late_in.at[it, pl.ds(1, SPLITS - 1)], late_sem.at[it, 0], late_sem.at[it, 1], at)
        summed += (late_in[it, 1].astype(F32) + late_in[it, 2].astype(F32)) + late_in[it, 3].astype(F32)
        tiles = [
            summed[j * WIDTH : (j + 1) * WIDTH, :] * inv[pl.ds(z * (BR // SPLITS) + j, 1), :]
            for j in range(BR // SPLITS)
        ]
        wide = jnp.concatenate(tiles, axis=1)
        wide_parts = split3(wide)
        gram = jnp.zeros((WIDTH, WIDTH), F32)
        for i in reversed(range(3)):
            left = jnp.concatenate(wide_parts[: 3 - i], axis=0)
            crossed = dot(left, wide_parts[i], ((1,), (1,)))
            for j in reversed(range(3 - i)):
                gram = gram + crossed[j * WIDTH : (j + 1) * WIDTH, :]
        packed = jnp.concatenate([gram[0:8], gram[8:16], jnp.zeros((8, HALF - 2 * WIDTH), F32)], axis=1)

        own = z * NCORE + at.core
        near_gram[it, own] = packed
        for offset in NEAR:
            row, split = at.near(offset)
            copy_to(
                near_gram.at[it, own], near_gram.at[it, own], near_sem.at[it, 0], near_sem.at[it, 1], row, split
            ).start()
        if not last:
            image[mine, :] = jnp.concatenate(tiles, axis=0)
            for dz in DZ:
                copy_to(image.at[mine], image.at[mine], image_sem.at[0], image_sem.at[1], me, at.split(dz)).start()
        wait_all(near_gram.at[it, pl.ds(0, NCORE * SPLITS - 1)], near_sem.at[it, 0], near_sem.at[it, 1], at)
        near_sum = near_gram[it, 0]
        for i in range(1, NCORE * SPLITS):
            near_sum = near_sum + near_gram[it, i]

        own = at.x * NY + at.y
        far_gram[it, own] = near_sum
        for offset in FAR:
            row, split = at.far(offset)
            copy_to(
                far_gram.at[it, own], far_gram.at[it, own], far_sem.at[it, 0], far_sem.at[it, 1], row, split
            ).start()
        if not last:
            wait_all(image.at[pl.ds(0, (SPLITS - 1) * QROWS)], image_sem.at[0], image_sem.at[1], at)
            for j in range(BR):
                pieces = split3(image[j * WIDTH : (j + 1) * WIDTH, :])
                image_parts[j] = jnp.concatenate([pieces[i] for i in RIGHT], axis=0)
        wait_all(far_gram.at[it, pl.ds(0, NX * NY - 1)], far_sem.at[it, 0], far_sem.at[it, 1], at)
        packed = far_gram[it, 0]
        for i in range(1, NX * NY):
            packed = packed + far_gram[it, i]
        gram = jnp.concatenate([packed[:, 0:WIDTH], packed[:, WIDTH : 2 * WIDTH]], axis=0)
        inverse = factor_inverse(gram / VERTICES)
        if last:
            out[...] = dot(inverse, jnp.concatenate([wide_parts[i] for i in RIGHT], axis=0))
        else:
            for j in range(BR):
                set_rows(j, dot(inverse, image_parts[j]))


def per_device(
    local_weights, local_gains, local_coords, remote_weights, remote_gains, remote_groups, remote_coords, start_block
):
    dma = pltpu.SemaphoreType.DMA
    return pl.pallas_call(
        whole_kernel,
        out_shape=pltpu.VMEM((WIDTH, QROWS // WIDTH * TILE), F32),
        in_specs=[HBM] * 8,
        out_specs=VMEM,
        scratch_shapes=[
            pltpu.VMEM((1, LT), jnp.int32),
            pltpu.VMEM((2, LOC), jnp.int32),
            pltpu.VMEM((2, LT), jnp.int32),
            pltpu.VMEM((LOC, 2, TILE), F32),
            pltpu.VMEM((LT, 2, TILE), F32),
            pltpu.VMEM((WIDTH, BR * TILE), F32),
            pltpu.VMEM((LT + LOC, TILE, TILE), BF16),
            pltpu.VMEM((8, HALF), jnp.int32),
            pltpu.SMEM((8, HALF), jnp.int32),
            pltpu.VMEM((LT, TILE), F32),
            pltpu.VMEM((LT + 2 * LOC, TILE), F32),
            pltpu.VMEM((GROUPS, 8, HALF), F32),
            pltpu.VMEM((GROUPS, 8, HALF), F32),
            pltpu.VMEM((SPLITS, BR, TILE), F32),
            pltpu.VMEM((BR, TILE), F32),
            pltpu.VMEM((BR * WIDTH, GROUPS * MOST * WIDTH), BF16),
            pltpu.VMEM((GROUPS * MOST * WIDTH, BR * WIDTH), BF16),
            pltpu.VMEM((BR, WIDTH, TILE), BF16),
            pltpu.VMEM((BR, 2 * PAD + 1, WIDTH, TILE), BF16),
            pltpu.VMEM((GROUPS * MOST, WIDTH, TILE), BF16),
            pltpu.VMEM((ITERS, GROUPS * MOST, WIDTH, TILE), BF16),
            pltpu.VMEM((LT, WIDTH, TILE), BF16),
            pltpu.VMEM((GROUPS * MOST, WIDTH, TILE), BF16),
            pltpu.VMEM((ITERS, GROUPS * MOST, WIDTH, TILE), BF16),
            pltpu.VMEM((STEP, 2 * PAD + 1, WIDTH, TILE), BF16),
            pltpu.VMEM((BR * WIDTH, TILE), F32),
            pltpu.VMEM((ITERS, SPLITS, QROWS, TILE), F32),
            pltpu.VMEM((BR * WIDTH, TILE), F32),
            pltpu.VMEM((BR * WIDTH, TILE), BF16),
            pltpu.VMEM((ITERS, SPLITS, QROWS, TILE), BF16),
            pltpu.VMEM((BR * WIDTH, TILE), F32),
            pltpu.VMEM((BR, len(RIGHT) * WIDTH, TILE), BF16),
            pltpu.VMEM((ITERS, NCORE * SPLITS, 8, HALF), F32),
            pltpu.VMEM((ITERS, NX * NY, 8, HALF), F32),
            dma(((LT + LOC) // CHUNK,)),
            dma((6,)),
            dma((1,)),
            dma((2,)),
            dma((2,)),
            dma((ITERS, 2)),
            dma((ITERS, 2)),
            dma((ITERS, 2)),
            dma((ITERS, 2)),
            dma((2,)),
            dma((ITERS, 2)),
            dma((ITERS, 2)),
        ],
        compiler_params=pltpu.CompilerParams(
            collective_id=0, has_side_effects=True, vmem_limit_bytes=60 << 20
        ),
        name="iterate",
    )(
        remote_groups[0], local_coords[0, 0].T, remote_coords[0, 0].T, local_gains[0, 0], remote_gains[0, 0],
        start_block, local_weights[0, 0], remote_weights[0, 0],
    )


def solution(mesh):
    in_specs = (
        P("rows", "cols", None, None, None),
        P("rows", "cols", None, None, None),
        P("rows", "cols", None, None),
        P("rows", "cols", None, None, None),
        P("rows", "cols", None, None, None),
        P("rows", "cols", None),
        P("rows", "cols", None, None),
        P(None, "rows"),
    )
    out_specs = P(None, ("rows", "cols"))
    return jax.shard_map(
        per_device, mesh=mesh, in_specs=in_specs, out_specs=out_specs, check_vma=False
    )
```

```python
import jax
import jax.numpy as jnp
from jax import lax
from jax.experimental import pallas as pl
from jax.experimental.pallas import tpu as pltpu
from jax.sharding import PartitionSpec as P

TILE = 256
HALF = 128
WIDTH = 16
BR = 16
MOST = 2
ITERS = 2
LOC = 48
LT = 32
GROUPS = 32
SPLITS = 4
QROWS = BR // SPLITS * WIDTH
NX, NY, NCORE = 4, 4, 2
CHUNK = 8
STEP = 4
VERTICES = GROUPS * BR * TILE
PAD = BR - 1
MESH = pl.DeviceIdType.MESH
VMEM = pl.BlockSpec(memory_space=pltpu.VMEM)
F32 = jnp.float32
BF16 = jnp.bfloat16

HBM = pl.BlockSpec(memory_space=pltpu.HBM)
T_REMOTE_ROW, T_REMOTE_COL, T_LOCAL_ROW, T_LOCAL_COL, T_SLOT, T_FIRST = range(6)
LEFT, RIGHT = (0, 0, 1, 0, 1, 2), (0, 1, 0, 2, 1, 0)


def ring(distance, size):
    return min(distance, size - distance)


PLANE = sorted(
    range(1, NX * NY * NCORE), key=lambda o: -ring(o // (NCORE * NY), NX) - ring(o // NCORE % NY, NY)
)
NEAR = sorted(range(1, NCORE * SPLITS), key=lambda o: -ring(o // NCORE, SPLITS))
FAR = sorted(range(1, NX * NY), key=lambda o: -ring(o // NY, NX) - ring(o % NY, NY))
DZ = (2, 1, 3)


def dot(a, b, dims=((1,), (0,))):
    return lax.dot_general(a, b, (dims, ((), ())), preferred_element_type=F32)


def split3(value):
    high = value.astype(BF16)
    rest = value - high.astype(F32)
    middle = rest.astype(BF16)
    return high, middle, (rest - middle.astype(F32)).astype(BF16)


def select_sum(hot, value, dims=((1,), (0,))):
    high, middle, low = split3(value)
    return dot(hot, high, dims) + (dot(hot, middle, dims) + dot(hot, low, dims))


def iota(shape, dim):
    return lax.broadcasted_iota(jnp.int32, shape, dim)


def factor_inverse(gram):
    copies = len(LEFT) * WIDTH
    shape = (WIDTH, HALF)
    row, lane = iota(shape, 0), iota(shape, 1)
    work = jnp.where((lane % WIDTH == row) & (lane < copies), 1.0, 0.0)
    columns = [jnp.broadcast_to(gram[:, k : k + 1], shape) for k in range(WIDTH)]
    roots = jnp.zeros(shape, F32)
    for k in range(WIDTH):
        pivot = jnp.broadcast_to(columns[k][k : k + 1, :], shape)
        roots = jnp.where(row == k, 1.0 / jnp.sqrt(pivot), roots)
        if k == WIDTH - 1:
            break
        factor = jnp.where(row > k, columns[k] * (1.0 / pivot), 0.0)
        for j in range(k + 1, WIDTH):
            columns[j] = columns[j] - factor * jnp.broadcast_to(columns[j][k : k + 1, :], shape)
        work = work - factor * jnp.broadcast_to(work[k : k + 1, :], shape)
    inverse = work * roots
    high, middle, low = (part.astype(F32) for part in split3(inverse))
    part = lane // WIDTH
    chosen = jnp.where((part == 2) | (part == 4), middle, jnp.where(part == 5, low, high))
    return chosen.astype(BF16)[:, 0:copies]


class Place:
    def __init__(self):
        self.me, self.z = lax.axis_index("rows"), lax.axis_index("cols")
        self.core, self.y, self.x = self.me % NCORE, (self.me // NCORE) % NY, self.me // (NCORE * NY)
        self.cores = [(self.core + d) % NCORE for d in range(NCORE)]
        self.ys = [((self.y + d) % NY) * NCORE for d in range(NY)]
        self.xs = [((self.x + d) % NX) * (NY * NCORE) for d in range(NX)]
        self.zs = [(self.z + d) % SPLITS for d in range(SPLITS)]

    def plane(self, offset):
        return self.xs[offset // (NCORE * NY)] + self.ys[(offset // NCORE) % NY] + self.cores[offset % NCORE]

    def split(self, dz):
        return self.zs[dz]

    def near(self, offset):
        return self.xs[0] + self.ys[0] + self.cores[offset % NCORE], self.zs[offset // NCORE]

    def far(self, offset):
        return self.xs[offset // NY] + self.ys[offset % NY] + self.core, self.z


def copy_to(source, target, send_sem, recv_sem, row, split):
    return pltpu.make_async_remote_copy(
        src_ref=source, dst_ref=target, send_sem=send_sem, recv_sem=recv_sem,
        device_id=(row, split), device_id_type=MESH,
    )


def wait_all(ref, send_sem, recv_sem, place):
    copy_to(ref, ref, send_sem, recv_sem, place.me, place.z).wait()


def loop(start, stop, body):
    def step(i, carry):
        body(i)
        return carry

    lax.fori_loop(start, stop, step, 0)


def whole_kernel(
    groups_h, local_coords_h, remote_coords_h, local_gains_h, remote_gains_h, start_h, local_w, remote_w,
    out,
    groups, local_coords, remote_coords, local_gains, remote_gains, start,
    eff, table_v, table, column_sums, sums, deg_out, deg_in, split_part, inv, spread, gather, row_blocks,
    padded, answer_out, answer_in, product, product_out, product_in, fetched, total,
    parts, late, late_out, late_in, image, image_parts, near_gram, far_gram,
    load_sem, small_sem, table_sem, deg_sem, zdeg_sem, answer_sem, product_sem,
    part_sem, late_sem, image_sem, near_sem, far_sem,
):
    at = Place()
    me, z = at.me, at.z
    first = LT // CHUNK
    chunks = (LT + LOC) // CHUNK

    def load(c):
        chunk = pl.ds(c * CHUNK, CHUNK)
        source = remote_w.at[chunk] if c < first else local_w.at[pl.ds((c - first) * CHUNK, CHUNK)]
        return pltpu.make_async_copy(source, eff.at[chunk], load_sem.at[c])

    small = [
        pltpu.make_async_copy(source, target, small_sem.at[i])
        for i, (source, target) in enumerate(
            [
                (groups_h, groups), (remote_coords_h, remote_coords), (local_coords_h, local_coords),
                (remote_gains_h, remote_gains), (local_gains_h, local_gains), (start_h, start),
            ]
        )
    ]
    for copy in small[:4]:
        copy.start()
    for c in range(first):
        load(c).start()

    barrier = pltpu.get_barrier_semaphore()
    greeted = [(at.plane(o), z) for o in PLANE] + [at.near(o) for o in NEAR if o >= NCORE]

    def pair(p):
        return pl.ds(MOST * p, MOST)

    ones = jnp.ones((8, TILE), BF16)

    def scale(tile0, gains, gain0, row_at, keep, col_at):
        row_gains = jnp.concatenate([gains[gain0 + t, 0:1, :] for t in range(CHUNK)], axis=0).T
        for t in range(CHUNK):
            scaled = (
                row_gains[:, t : t + 1] * eff[tile0 + t].astype(F32) * gains[gain0 + t, 1:2, :]
            ).astype(BF16)
            eff[tile0 + t] = scaled
            size = jnp.abs(scaled)
            sums[pl.ds(row_at + t, 1), :] = dot(ones, size, ((1,), (1,)))[0:1, :]
            keep(col_at + t, dot(ones, size))

    def remote_chunk(c):
        chunk = pl.ds(c * CHUNK, CHUNK)
        pltpu.make_async_copy(remote_w.at[chunk], eff.at[chunk], load_sem.at[c]).wait()

        def keep(t, value):
            column_sums[pl.ds(t, 1), :] = value[0:1, :]

        scale(c * CHUNK, remote_gains, c * CHUNK, c * CHUNK, keep, c * CHUNK)

    def local_chunk(c):
        pltpu.make_async_copy(
            local_w.at[pl.ds(c * CHUNK, CHUNK)],
            eff.at[pl.ds(LT + c * CHUNK, CHUNK)],
            load_sem.at[first + c],
        ).wait()

        def keep(t, value):
            sums[pl.ds(t, 1), :] = value[0:1, :]

        scale(LT + c * CHUNK, local_gains, c * CHUNK, LT + c * CHUNK, keep, LT + LOC + c * CHUNK)

    def make_tables():
        for copy in small[:3]:
            copy.wait()
        group = jnp.broadcast_to(groups[...], (GROUPS, LT))
        slot_group, tile_id = iota((GROUPS, LT), 0), iota((GROUPS, LT), 1)
        named = group == slot_group
        lowest = jnp.min(jnp.where(named, tile_id, LT - 1), axis=1, keepdims=True)
        highest = jnp.max(jnp.where(named, tile_id, -1), axis=1, keepdims=True)
        is_first, is_second = named & (tile_id == lowest), named & (tile_id == highest)
        slot = MOST * slot_group + jnp.where(is_second, 1, 0)
        named_t = jnp.transpose(group) == iota((LT, GROUPS), 1)
        tile_t = iota((LT, GROUPS), 0)
        table_v[...] = jnp.zeros_like(table_v)
        table_v[T_REMOTE_ROW : T_REMOTE_ROW + 2, 0:LT] = remote_coords[...]
        table_v[T_LOCAL_ROW : T_LOCAL_ROW + 2, 0:LOC] = local_coords[...]
        table_v[T_SLOT : T_SLOT + 1, 0:LT] = jnp.sum(jnp.where(named, slot, 0), axis=0, keepdims=True)
        table_v[T_FIRST : T_FIRST + 1, 0:GROUPS] = jnp.min(jnp.where(named_t, tile_t, LT - 1), axis=0, keepdims=True)
        table_v[T_FIRST + 1 : T_FIRST + 2, 0:GROUPS] = jnp.max(jnp.where(named_t, tile_t, 0), axis=0, keepdims=True)
        table_copy = pltpu.make_async_copy(table_v, table, table_sem.at[0])
        table_copy.start()
        hot_slots = jnp.concatenate([jnp.where(hot, 1.0, 0.0) for hot in (is_first, is_second)], axis=0)
        target = jnp.broadcast_to(remote_coords[1:2, :].astype(F32) + 1.0, (MOST * GROUPS, LT))
        slot_column = jnp.sum(hot_slots * target, axis=1, keepdims=True) - 1.0
        slot_column = jnp.broadcast_to(slot_column, (MOST * GROUPS, HALF))
        return hot_slots.astype(BF16), slot_column, table_copy

    share = -(-len(greeted) // (first - 1))
    later = [load(c) for c in range(first, chunks)] + small[4:]
    for c in range(first):
        for row, split in greeted[c * share : (c + 1) * share]:
            pl.semaphore_signal(barrier, inc=1, device_id=(row, split), device_id_type=MESH)
        for copy in later[c * 2 : c * 2 + 2]:
            copy.start()
        if c == 0:
            tables = make_tables()
            small[3].wait()
        remote_chunk(c)

    hot_slots, slot_column, table_copy = tables
    pl.semaphore_wait(barrier, GROUPS - 1 + NCORE * SPLITS - 2)

    lanes = iota((1, HALF), 1)
    slot_sums = select_sum(hot_slots, column_sums[...])
    for p in range(GROUPS):
        pieces = []
        for s in range(MOST):
            row = slot_sums[s * GROUPS + p : s * GROUPS + p + 1, :]
            pieces += [row[:, 0:HALF], row[:, HALF:TILE]]
        columns = [slot_column[s * GROUPS + p : s * GROUPS + p + 1, :] for s in range(MOST)]
        by_lane = jnp.where(lanes % 8 < 2, columns[0], jnp.where(lanes % 8 < 4, columns[1], -1.0))
        deg_out[p] = jnp.concatenate(pieces + [by_lane, *columns, jnp.zeros((1, HALF), F32)], axis=0)
    for o in PLANE:
        to = at.plane(o)
        copy_to(deg_out.at[to], deg_in.at[me], deg_sem.at[0], deg_sem.at[1], to, z).start()
    deg_in[me] = deg_out[me]
    small[4].wait()
    loop(0, LOC // CHUNK, local_chunk)
    small[5].wait()
    table_copy.wait()

    def hot_rows(row):
        return jnp.where(jnp.broadcast_to(row, (BR, row.shape[1])) == iota((BR, row.shape[1]), 0), 1.0, 0.0).astype(BF16)

    own = select_sum(hot_rows(remote_coords[0:1, :]), sums[0:LT, :])
    own += select_sum(hot_rows(local_coords[0:1, :]), sums[LT : LT + LOC, :])
    own += select_sum(hot_rows(local_coords[1:2, :]), sums[LT + LOC : LT + 2 * LOC, :])
    wait_all(deg_in.at[pl.ds(0, GROUPS - 1)], deg_sem.at[0], deg_sem.at[1], at)
    came = deg_in[...].reshape(GROUPS * 8, HALF)
    blocks = []
    for b in range(GROUPS * 8 // HALF):
        column = jnp.full((1, HALF), -1.0, F32)
        for i in range(HALF // 8):
            column = jnp.where(lanes // 8 == i, deg_in[b * (HALF // 8) + i, 4:5, :], column)
        blocks.append(column)
    column = jnp.broadcast_to(jnp.concatenate(blocks, axis=1), (2 * BR, GROUPS * 8))
    row, lane8 = iota(column.shape, 0), iota(column.shape, 1) % 4
    chosen = (column == (row % BR).astype(F32)) & (lane8 % 2 == row // BR)
    added = select_sum(jnp.where(chosen, 1.0, 0.0).astype(BF16), came)
    split_part[z] = own + jnp.concatenate([added[0:BR, :], added[BR : 2 * BR, :]], axis=1)

    for dz in DZ:
        copy_to(split_part.at[z], split_part.at[z], zdeg_sem.at[0], zdeg_sem.at[1], me, at.split(dz)).start()

    padded[...] = jnp.zeros_like(padded)
    fetched[...] = jnp.zeros_like(fetched)
    row = iota((BR * WIDTH, HALF), 0)
    lane = iota((BR * WIDTH, HALF), 1)
    row_tile = (row // WIDTH).astype(F32)
    per = HALF // WIDTH
    for q in range(GROUPS * MOST // per):
        column = jnp.zeros((1, HALF), F32)
        for i in range(per):
            at_slot = deg_in[q * (per // MOST) + i // MOST, 5 + i % MOST : 6 + i % MOST, :]
            column = jnp.where(lanes // WIDTH == i, at_slot, column)
        chosen = (jnp.broadcast_to(column, row.shape) == row_tile) & (lane % WIDTH == row % WIDTH)
        spread[:, q * HALF : (q + 1) * HALF] = jnp.where(chosen, 1.0, 0.0).astype(BF16)
    lane = iota((WIDTH, TILE), 1)
    diagonal = lane % WIDTH == iota((WIDTH, TILE), 0)
    lane_tile = (lane // WIDTH).astype(F32)
    for slot in range(GROUPS * MOST):
        own = deg_in[slot // MOST, 5 + slot % MOST : 6 + slot % MOST, :]
        own = jnp.broadcast_to(jnp.concatenate([own, own], axis=1), (WIDTH, TILE))
        gather[slot * WIDTH : (slot + 1) * WIDTH, :] = jnp.where(diagonal & (own == lane_tile), 1.0, 0.0).astype(BF16)

    wait_all(split_part.at[pl.ds(0, SPLITS - 1)], zdeg_sem.at[0], zdeg_sem.at[1], at)
    inv[...] = 1.0 / jnp.sqrt((split_part[0] + split_part[1]) + (split_part[2] + split_part[3]))

    def set_rows(j, vectors):
        scaled = (vectors * inv[j : j + 1, :]).astype(BF16)
        row_blocks[j] = scaled

    for j in range(BR):
        set_rows(j, start[:, j * TILE : (j + 1) * TILE])

    for it in range(ITERS):
        last = it == ITERS - 1
        a_in, p_in = answer_in.at[it], product_in.at[it]

        values = row_blocks[...].reshape(BR * WIDTH, TILE)

        def answers(partners):
            chosen = [
                gather[pl.ds(pl.multiple_of(to * (MOST * WIDTH), MOST * WIDTH), MOST * WIDTH), :] for to in partners
            ]
            found = dot(jnp.concatenate(chosen, axis=0), values).astype(BF16)
            return found.reshape(len(partners), MOST, WIDTH, TILE)

        for begin in range(0, len(PLANE), 4):
            partners = [at.plane(o) for o in PLANE[begin : begin + 4]]
            found = answers(partners)
            for i, to in enumerate(partners):
                answer_out[pair(to)] = found[i]
            for to in partners:
                copy_to(
                    answer_out.at[pair(to)], a_in.at[pair(me)], answer_sem.at[it, 0], answer_sem.at[it, 1], to, z
                ).start()
        a_in[pair(me)] = answers([me])[0]

        def backward(i):
            for u in range(STEP):
                tile = i * STEP + u
                x = row_blocks[table[T_REMOTE_ROW, tile]]
                product[tile] = dot(x, eff[tile]).astype(BF16)

        loop(0, LT // STEP, backward)

        def fill_product(p, ref):
            for s in range(MOST):
                ref[MOST * p + s] = product[table[T_FIRST + s, p]]

        for o in PLANE:
            to = at.plane(o)
            fill_product(to, product_out)
            copy_to(
                product_out.at[pair(to)], p_in.at[pair(me)], product_sem.at[it, 0], product_sem.at[it, 1], to, z
            ).start()
        fill_product(me, p_in)

        for j in range(BR):
            padded[j, PAD] = row_blocks[j]

        total[...] = jnp.zeros_like(total)

        def window(ref, index, row_tile):
            return ref[index, pl.ds(PAD - row_tile, BR)].reshape(BR * WIDTH, TILE)

        def local(i):
            value = total[...]
            for u in range(STEP):
                tile = i * STEP + u
                r, c = table[T_LOCAL_ROW, tile], table[T_LOCAL_COL, tile]
                value += dot(window(padded, c, r), eff[LT + tile], ((1,), (1,)))
                value += dot(window(padded, r, c), eff[LT + tile])
            total[...] = value

        loop(0, LOC // STEP, local)

        for dz in DZ:
            other = at.split(dz)
            copy_to(
                total.at[pl.ds(other * QROWS, QROWS)], parts.at[it, dz], part_sem.at[it, 0], part_sem.at[it, 1], me, other
            ).start()
        late[...] = jnp.zeros_like(late)

        others = pl.ds(0, MOST * (GROUPS - 1))
        wait_all(a_in.at[others], answer_sem.at[it, 0], answer_sem.at[it, 1], at)

        def forward(i):
            value = late[...]
            for u in range(STEP):
                tile = i * STEP + u
                slot = table[T_SLOT, tile]
                fetched[u, PAD] = a_in[slot]
                value += dot(window(fetched, u, table[T_REMOTE_ROW, tile]), eff[tile], ((1,), (1,)))
            late[...] = value

        loop(0, LT // STEP, forward)

        wait_all(p_in.at[others], product_sem.at[it, 0], product_sem.at[it, 1], at)
        came = p_in[...].reshape(GROUPS * MOST * WIDTH, TILE)
        for dz in (*DZ, 0):
            other = at.split(dz)
            rows = pl.ds(pl.multiple_of(other * QROWS, QROWS), QROWS)
            rest = late[rows, :] + dot(spread[rows, :], came)
            if dz:
                late_out[rows, :] = rest.astype(BF16)
                copy_to(
                    late_out.at[rows], late_in.at[it, dz], late_sem.at[it, 0], late_sem.at[it, 1], me, other
                ).start()
        mine = pl.ds(z * QROWS, QROWS)
        wait_all(parts.at[it, pl.ds(1, SPLITS - 1)], part_sem.at[it, 0], part_sem.at[it, 1], at)
        summed = (total[mine, :] + rest) + ((parts[it, 1] + parts[it, 2]) + parts[it, 3])
        wait_all(late_in.at[it, pl.ds(1, SPLITS - 1)], late_sem.at[it, 0], late_sem.at[it, 1], at)
        summed += (late_in[it, 1].astype(F32) + late_in[it, 2].astype(F32)) + late_in[it, 3].astype(F32)
        tiles = [
            summed[j * WIDTH : (j + 1) * WIDTH, :] * inv[pl.ds(z * (BR // SPLITS) + j, 1), :]
            for j in range(BR // SPLITS)
        ]
        wide = jnp.concatenate(tiles, axis=1)
        wide_parts = split3(wide)
        gram = jnp.zeros((WIDTH, WIDTH), F32)
        for i in reversed(range(3)):
            left = jnp.concatenate(wide_parts[: 3 - i], axis=0)
            crossed = dot(left, wide_parts[i], ((1,), (1,)))
            for j in reversed(range(3 - i)):
                gram = gram + crossed[j * WIDTH : (j + 1) * WIDTH, :]
        packed = jnp.concatenate([gram[0:8], gram[8:16], jnp.zeros((8, HALF - 2 * WIDTH), F32)], axis=1)

        own = z * NCORE + at.core
        near_gram[it, own] = packed
        for offset in NEAR:
            row, split = at.near(offset)
            copy_to(
                near_gram.at[it, own], near_gram.at[it, own], near_sem.at[it, 0], near_sem.at[it, 1], row, split
            ).start()
        if not last:
            image[mine, :] = jnp.concatenate(tiles, axis=0)
            for dz in DZ:
                copy_to(image.at[mine], image.at[mine], image_sem.at[0], image_sem.at[1], me, at.split(dz)).start()
        wait_all(near_gram.at[it, pl.ds(0, NCORE * SPLITS - 1)], near_sem.at[it, 0], near_sem.at[it, 1], at)
        near_sum = near_gram[it, 0]
        for i in range(1, NCORE * SPLITS):
            near_sum = near_sum + near_gram[it, i]

        own = at.x * NY + at.y
        far_gram[it, own] = near_sum
        for offset in FAR:
            row, split = at.far(offset)
            copy_to(
                far_gram.at[it, own], far_gram.at[it, own], far_sem.at[it, 0], far_sem.at[it, 1], row, split
            ).start()
        if not last:
            wait_all(image.at[pl.ds(0, (SPLITS - 1) * QROWS)], image_sem.at[0], image_sem.at[1], at)
            for j in range(BR):
                pieces = split3(image[j * WIDTH : (j + 1) * WIDTH, :])
                image_parts[j] = jnp.concatenate([pieces[i] for i in RIGHT], axis=0)
        wait_all(far_gram.at[it, pl.ds(0, NX * NY - 1)], far_sem.at[it, 0], far_sem.at[it, 1], at)
        packed = far_gram[it, 0]
        for i in range(1, NX * NY):
            packed = packed + far_gram[it, i]
        gram = jnp.concatenate([packed[:, 0:WIDTH], packed[:, WIDTH : 2 * WIDTH]], axis=0)
        inverse = factor_inverse(gram / VERTICES)
        if last:
            out[...] = dot(inverse, jnp.concatenate([wide_parts[i] for i in RIGHT], axis=0))
        else:
            for j in range(BR):
                set_rows(j, dot(inverse, image_parts[j]))


def per_device(
    local_weights, local_gains, local_coords, remote_weights, remote_gains, remote_groups, remote_coords, start_block
):
    dma = pltpu.SemaphoreType.DMA
    return pl.pallas_call(
        whole_kernel,
        out_shape=pltpu.VMEM((WIDTH, QROWS // WIDTH * TILE), F32),
        in_specs=[HBM] * 8,
        out_specs=VMEM,
        scratch_shapes=[
            pltpu.VMEM((1, LT), jnp.int32),
            pltpu.VMEM((2, LOC), jnp.int32),
            pltpu.VMEM((2, LT), jnp.int32),
            pltpu.VMEM((LOC, 2, TILE), F32),
            pltpu.VMEM((LT, 2, TILE), F32),
            pltpu.VMEM((WIDTH, BR * TILE), F32),
            pltpu.VMEM((LT + LOC, TILE, TILE), BF16),
            pltpu.VMEM((8, HALF), jnp.int32),
            pltpu.SMEM((8, HALF), jnp.int32),
            pltpu.VMEM((LT, TILE), F32),
            pltpu.VMEM((LT + 2 * LOC, TILE), F32),
            pltpu.VMEM((GROUPS, 8, HALF), F32),
            pltpu.VMEM((GROUPS, 8, HALF), F32),
            pltpu.VMEM((SPLITS, BR, TILE), F32),
            pltpu.VMEM((BR, TILE), F32),
            pltpu.VMEM((BR * WIDTH, GROUPS * MOST * WIDTH), BF16),
            pltpu.VMEM((GROUPS * MOST * WIDTH, BR * WIDTH), BF16),
            pltpu.VMEM((BR, WIDTH, TILE), BF16),
            pltpu.VMEM((BR, 2 * PAD + 1, WIDTH, TILE), BF16),
            pltpu.VMEM((GROUPS * MOST, WIDTH, TILE), BF16),
            pltpu.VMEM((ITERS, GROUPS * MOST, WIDTH, TILE), BF16),
            pltpu.VMEM((LT, WIDTH, TILE), BF16),
            pltpu.VMEM((GROUPS * MOST, WIDTH, TILE), BF16),
            pltpu.VMEM((ITERS, GROUPS * MOST, WIDTH, TILE), BF16),
            pltpu.VMEM((STEP, 2 * PAD + 1, WIDTH, TILE), BF16),
            pltpu.VMEM((BR * WIDTH, TILE), F32),
            pltpu.VMEM((ITERS, SPLITS, QROWS, TILE), F32),
            pltpu.VMEM((BR * WIDTH, TILE), F32),
            pltpu.VMEM((BR * WIDTH, TILE), BF16),
            pltpu.VMEM((ITERS, SPLITS, QROWS, TILE), BF16),
            pltpu.VMEM((BR * WIDTH, TILE), F32),
            pltpu.VMEM((BR, len(RIGHT) * WIDTH, TILE), BF16),
            pltpu.VMEM((ITERS, NCORE * SPLITS, 8, HALF), F32),
            pltpu.VMEM((ITERS, NX * NY, 8, HALF), F32),
            dma(((LT + LOC) // CHUNK,)),
            dma((6,)),
            dma((1,)),
            dma((2,)),
            dma((2,)),
            dma((ITERS, 2)),
            dma((ITERS, 2)),
            dma((ITERS, 2)),
            dma((ITERS, 2)),
            dma((2,)),
            dma((ITERS, 2)),
            dma((ITERS, 2)),
        ],
        compiler_params=pltpu.CompilerParams(
            collective_id=0, has_side_effects=True, vmem_limit_bytes=60 << 20
        ),
        name="iterate",
    )(
        remote_groups[0], local_coords[0, 0].T, remote_coords[0, 0].T, local_gains[0, 0], remote_gains[0, 0],
        start_block, local_weights[0, 0], remote_weights[0, 0],
    )


def solution(mesh):
    in_specs = (
        P("rows", "cols", None, None, None),
        P("rows", "cols", None, None, None),
        P("rows", "cols", None, None),
        P("rows", "cols", None, None, None),
        P("rows", "cols", None, None, None),
        P("rows", "cols", None),
        P("rows", "cols", None, None),
        P(None, "rows"),
    )
    out_specs = P(None, ("rows", "cols"))
    return jax.shard_map(
        per_device, mesh=mesh, in_specs=in_specs, out_specs=out_specs, check_vma=False
    )
```

```python
import jax
import jax.numpy as jnp
from jax import lax
from jax.experimental import pallas as pl
from jax.experimental.pallas import tpu as pltpu
from jax.sharding import PartitionSpec as P

TILE = 256
HALF = 128
WIDTH = 16
BR = 16
MOST = 2
ITERS = 2
LOC = 48
LT = 32
GROUPS = 32
SPLITS = 4
QROWS = BR // SPLITS * WIDTH
NX, NY, NCORE = 4, 4, 2
CHUNK = 8
STEP = 4
VERTICES = GROUPS * BR * TILE
PAD = BR - 1
MESH = pl.DeviceIdType.MESH
VMEM = pl.BlockSpec(memory_space=pltpu.VMEM)
F32 = jnp.float32
BF16 = jnp.bfloat16

HBM = pl.BlockSpec(memory_space=pltpu.HBM)
T_REMOTE_ROW, T_REMOTE_COL, T_LOCAL_ROW, T_LOCAL_COL, T_SLOT, T_FIRST = range(6)
LEFT, RIGHT = (0, 0, 1, 0, 1, 2), (0, 1, 0, 2, 1, 0)


def ring(distance, size):
    return min(distance, size - distance)


PLANE = sorted(
    range(1, NX * NY * NCORE), key=lambda o: -ring(o // (NCORE * NY), NX) - ring(o // NCORE % NY, NY)
)
NEAR = sorted(range(1, NCORE * SPLITS), key=lambda o: -ring(o // NCORE, SPLITS))
FAR = sorted(range(1, NX * NY), key=lambda o: -ring(o // NY, NX) - ring(o % NY, NY))
DZ = (2, 1, 3)


def dot(a, b, dims=((1,), (0,))):
    return lax.dot_general(a, b, (dims, ((), ())), preferred_element_type=F32)


def split3(value):
    high = value.astype(BF16)
    rest = value - high.astype(F32)
    middle = rest.astype(BF16)
    return high, middle, (rest - middle.astype(F32)).astype(BF16)


def select_sum(hot, value, dims=((1,), (0,))):
    high, middle, low = split3(value)
    return dot(hot, high, dims) + (dot(hot, middle, dims) + dot(hot, low, dims))


def iota(shape, dim):
    return lax.broadcasted_iota(jnp.int32, shape, dim)


def factor_inverse(gram):
    copies = len(LEFT) * WIDTH
    shape = (WIDTH, HALF)
    row, lane = iota(shape, 0), iota(shape, 1)
    work = jnp.where((lane % WIDTH == row) & (lane < copies), 1.0, 0.0)
    columns = [jnp.broadcast_to(gram[:, k : k + 1], shape) for k in range(WIDTH)]
    roots = jnp.zeros(shape, F32)
    for k in range(WIDTH):
        pivot = jnp.broadcast_to(columns[k][k : k + 1, :], shape)
        roots = jnp.where(row == k, 1.0 / jnp.sqrt(pivot), roots)
        if k == WIDTH - 1:
            break
        factor = jnp.where(row > k, columns[k] * (1.0 / pivot), 0.0)
        for j in range(k + 1, WIDTH):
            columns[j] = columns[j] - factor * jnp.broadcast_to(columns[j][k : k + 1, :], shape)
        work = work - factor * jnp.broadcast_to(work[k : k + 1, :], shape)
    inverse = work * roots
    high, middle, low = (part.astype(F32) for part in split3(inverse))
    part = lane // WIDTH
    chosen = jnp.where((part == 2) | (part == 4), middle, jnp.where(part == 5, low, high))
    return chosen.astype(BF16)[:, 0:copies]


class Place:
    def __init__(self):
        self.me, self.z = lax.axis_index("rows"), lax.axis_index("cols")
        self.core, self.y, self.x = self.me % NCORE, (self.me // NCORE) % NY, self.me // (NCORE * NY)
        self.cores = [(self.core + d) % NCORE for d in range(NCORE)]
        self.ys = [((self.y + d) % NY) * NCORE for d in range(NY)]
        self.xs = [((self.x + d) % NX) * (NY * NCORE) for d in range(NX)]
        self.zs = [(self.z + d) % SPLITS for d in range(SPLITS)]

    def plane(self, offset):
        return self.xs[offset // (NCORE * NY)] + self.ys[(offset // NCORE) % NY] + self.cores[offset % NCORE]

    def split(self, dz):
        return self.zs[dz]

    def near(self, offset):
        return self.xs[0] + self.ys[0] + self.cores[offset % NCORE], self.zs[offset // NCORE]

    def far(self, offset):
        return self.xs[offset // NY] + self.ys[offset % NY] + self.core, self.z


def copy_to(source, target, send_sem, recv_sem, row, split):
    return pltpu.make_async_remote_copy(
        src_ref=source, dst_ref=target, send_sem=send_sem, recv_sem=recv_sem,
        device_id=(row, split), device_id_type=MESH,
    )


def wait_all(ref, send_sem, recv_sem, place):
    copy_to(ref, ref, send_sem, recv_sem, place.me, place.z).wait()


def loop(start, stop, body):
    def step(i, carry):
        body(i)
        return carry

    lax.fori_loop(start, stop, step, 0)


def whole_kernel(
    groups_h, local_coords_h, remote_coords_h, local_gains_h, remote_gains_h, start_h, local_w, remote_w,
    out,
    groups, local_coords, remote_coords, local_gains, remote_gains, start,
    eff, table_v, table, column_sums, sums, deg_out, deg_in, split_part, inv, spread, gather, row_blocks,
    padded, answer_out, answer_in, product, product_out, product_in, fetched, total,
    parts, late, late_out, late_in, image, image_parts, near_gram, far_gram,
    load_sem, small_sem, table_sem, deg_sem, zdeg_sem, answer_sem, product_sem,
    part_sem, late_sem, image_sem, near_sem, far_sem,
):
    at = Place()
    me, z = at.me, at.z
    first = LT // CHUNK
    chunks = (LT + LOC) // CHUNK

    def load(c):
        chunk = pl.ds(c * CHUNK, CHUNK)
        source = remote_w.at[chunk] if c < first else local_w.at[pl.ds((c - first) * CHUNK, CHUNK)]
        return pltpu.make_async_copy(source, eff.at[chunk], load_sem.at[c])

    small = [
        pltpu.make_async_copy(source, target, small_sem.at[i])
        for i, (source, target) in enumerate(
            [
                (groups_h, groups), (remote_coords_h, remote_coords), (local_coords_h, local_coords),
                (remote_gains_h, remote_gains), (local_gains_h, local_gains), (start_h, start),
            ]
        )
    ]
    for copy in small[:4]:
        copy.start()
    for c in range(first):
        load(c).start()

    barrier = pltpu.get_barrier_semaphore()
    greeted = [(at.plane(o), z) for o in PLANE] + [at.near(o) for o in NEAR if o >= NCORE]

    def pair(p):
        return pl.ds(MOST * p, MOST)

    ones = jnp.ones((8, TILE), BF16)

    def scale(tile0, gains, gain0, row_at, keep, col_at):
        row_gains = jnp.concatenate([gains[gain0 + t, 0:1, :] for t in range(CHUNK)], axis=0).T
        for t in range(CHUNK):
            scaled = (
                row_gains[:, t : t + 1] * eff[tile0 + t].astype(F32) * gains[gain0 + t, 1:2, :]
            ).astype(BF16)
            eff[tile0 + t] = scaled
            size = jnp.abs(scaled)
            sums[pl.ds(row_at + t, 1), :] = dot(ones, size, ((1,), (1,)))[0:1, :]
            keep(col_at + t, dot(ones, size))

    def remote_chunk(c):
        chunk = pl.ds(c * CHUNK, CHUNK)
        pltpu.make_async_copy(remote_w.at[chunk], eff.at[chunk], load_sem.at[c]).wait()

        def keep(t, value):
            column_sums[pl.ds(t, 1), :] = value[0:1, :]

        scale(c * CHUNK, remote_gains, c * CHUNK, c * CHUNK, keep, c * CHUNK)

    def local_chunk(c):
        pltpu.make_async_copy(
            local_w.at[pl.ds(c * CHUNK, CHUNK)],
            eff.at[pl.ds(LT + c * CHUNK, CHUNK)],
            load_sem.at[first + c],
        ).wait()

        def keep(t, value):
            sums[pl.ds(t, 1), :] = value[0:1, :]

        scale(LT + c * CHUNK, local_gains, c * CHUNK, LT + c * CHUNK, keep, LT + LOC + c * CHUNK)

    def make_tables():
        for copy in small[:3]:
            copy.wait()
        group = jnp.broadcast_to(groups[...], (GROUPS, LT))
        slot_group, tile_id = iota((GROUPS, LT), 0), iota((GROUPS, LT), 1)
        named = group == slot_group
        lowest = jnp.min(jnp.where(named, tile_id, LT - 1), axis=1, keepdims=True)
        highest = jnp.max(jnp.where(named, tile_id, -1), axis=1, keepdims=True)
        is_first, is_second = named & (tile_id == lowest), named & (tile_id == highest)
        slot = MOST * slot_group + jnp.where(is_second, 1, 0)
        named_t = jnp.transpose(group) == iota((LT, GROUPS), 1)
        tile_t = iota((LT, GROUPS), 0)
        table_v[...] = jnp.zeros_like(table_v)
        table_v[T_REMOTE_ROW : T_REMOTE_ROW + 2, 0:LT] = remote_coords[...]
        table_v[T_LOCAL_ROW : T_LOCAL_ROW + 2, 0:LOC] = local_coords[...]
        table_v[T_SLOT : T_SLOT + 1, 0:LT] = jnp.sum(jnp.where(named, slot, 0), axis=0, keepdims=True)
        table_v[T_FIRST : T_FIRST + 1, 0:GROUPS] = jnp.min(jnp.where(named_t, tile_t, LT - 1), axis=0, keepdims=True)
        table_v[T_FIRST + 1 : T_FIRST + 2, 0:GROUPS] = jnp.max(jnp.where(named_t, tile_t, 0), axis=0, keepdims=True)
        table_copy = pltpu.make_async_copy(table_v, table, table_sem.at[0])
        table_copy.start()
        hot_slots = jnp.concatenate([jnp.where(hot, 1.0, 0.0) for hot in (is_first, is_second)], axis=0)
        target = jnp.broadcast_to(remote_coords[1:2, :].astype(F32) + 1.0, (MOST * GROUPS, LT))
        slot_column = jnp.sum(hot_slots * target, axis=1, keepdims=True) - 1.0
        slot_column = jnp.broadcast_to(slot_column, (MOST * GROUPS, HALF))
        return hot_slots.astype(BF16), slot_column, table_copy

    share = -(-len(greeted) // (first - 1))
    later = [load(c) for c in range(first, chunks)] + small[4:]
    for c in range(first):
        for row, split in greeted[c * share : (c + 1) * share]:
            pl.semaphore_signal(barrier, inc=1, device_id=(row, split), device_id_type=MESH)
        for copy in later[c * 2 : c * 2 + 2]:
            copy.start()
        if c == 0:
            tables = make_tables()
            small[3].wait()
        remote_chunk(c)

    hot_slots, slot_column, table_copy = tables
    pl.semaphore_wait(barrier, GROUPS - 1 + NCORE * SPLITS - 2)

    lanes = iota((1, HALF), 1)
    slot_sums = select_sum(hot_slots, column_sums[...])
    for p in range(GROUPS):
        pieces = []
        for s in range(MOST):
            row = slot_sums[s * GROUPS + p : s * GROUPS + p + 1, :]
            pieces += [row[:, 0:HALF], row[:, HALF:TILE]]
        columns = [slot_column[s * GROUPS + p : s * GROUPS + p + 1, :] for s in range(MOST)]
        by_lane = jnp.where(lanes % 8 < 2, columns[0], jnp.where(lanes % 8 < 4, columns[1], -1.0))
        deg_out[p] = jnp.concatenate(pieces + [by_lane, *columns, jnp.zeros((1, HALF), F32)], axis=0)
    for o in PLANE:
        to = at.plane(o)
        copy_to(deg_out.at[to], deg_in.at[me], deg_sem.at[0], deg_sem.at[1], to, z).start()
    deg_in[me] = deg_out[me]
    small[4].wait()
    loop(0, LOC // CHUNK, local_chunk)
    small[5].wait()
    table_copy.wait()

    def hot_rows(row):
        return jnp.where(jnp.broadcast_to(row, (BR, row.shape[1])) == iota((BR, row.shape[1]), 0), 1.0, 0.0).astype(BF16)

    own = select_sum(hot_rows(remote_coords[0:1, :]), sums[0:LT, :])
    own += select_sum(hot_rows(local_coords[0:1, :]), sums[LT : LT + LOC, :])
    own += select_sum(hot_rows(local_coords[1:2, :]), sums[LT + LOC : LT + 2 * LOC, :])
    wait_all(deg_in.at[pl.ds(0, GROUPS - 1)], deg_sem.at[0], deg_sem.at[1], at)
    came = deg_in[...].reshape(GROUPS * 8, HALF)
    blocks = []
    for b in range(GROUPS * 8 // HALF):
        column = jnp.full((1, HALF), -1.0, F32)
        for i in range(HALF // 8):
            column = jnp.where(lanes // 8 == i, deg_in[b * (HALF // 8) + i, 4:5, :], column)
        blocks.append(column)
    column = jnp.broadcast_to(jnp.concatenate(blocks, axis=1), (2 * BR, GROUPS * 8))
    row, lane8 = iota(column.shape, 0), iota(column.shape, 1) % 4
    chosen = (column == (row % BR).astype(F32)) & (lane8 % 2 == row // BR)
    added = select_sum(jnp.where(chosen, 1.0, 0.0).astype(BF16), came)
    split_part[z] = own + jnp.concatenate([added[0:BR, :], added[BR : 2 * BR, :]], axis=1)

    for dz in DZ:
        copy_to(split_part.at[z], split_part.at[z], zdeg_sem.at[0], zdeg_sem.at[1], me, at.split(dz)).start()

    padded[...] = jnp.zeros_like(padded)
    fetched[...] = jnp.zeros_like(fetched)
    row = iota((BR * WIDTH, HALF), 0)
    lane = iota((BR * WIDTH, HALF), 1)
    row_tile = (row // WIDTH).astype(F32)
    per = HALF // WIDTH
    for q in range(GROUPS * MOST // per):
        column = jnp.zeros((1, HALF), F32)
        for i in range(per):
            at_slot = deg_in[q * (per // MOST) + i // MOST, 5 + i % MOST : 6 + i % MOST, :]
            column = jnp.where(lanes // WIDTH == i, at_slot, column)
        chosen = (jnp.broadcast_to(column, row.shape) == row_tile) & (lane % WIDTH == row % WIDTH)
        spread[:, q * HALF : (q + 1) * HALF] = jnp.where(chosen, 1.0, 0.0).astype(BF16)
    lane = iota((WIDTH, TILE), 1)
    diagonal = lane % WIDTH == iota((WIDTH, TILE), 0)
    lane_tile = (lane // WIDTH).astype(F32)
    for slot in range(GROUPS * MOST):
        own = deg_in[slot // MOST, 5 + slot % MOST : 6 + slot % MOST, :]
        own = jnp.broadcast_to(jnp.concatenate([own, own], axis=1), (WIDTH, TILE))
        gather[slot * WIDTH : (slot + 1) * WIDTH, :] = jnp.where(diagonal & (own == lane_tile), 1.0, 0.0).astype(BF16)

    wait_all(split_part.at[pl.ds(0, SPLITS - 1)], zdeg_sem.at[0], zdeg_sem.at[1], at)
    inv[...] = 1.0 / jnp.sqrt((split_part[0] + split_part[1]) + (split_part[2] + split_part[3]))

    def set_rows(j, vectors):
        scaled = (vectors * inv[j : j + 1, :]).astype(BF16)
        row_blocks[j] = scaled

    for j in range(BR):
        set_rows(j, start[:, j * TILE : (j + 1) * TILE])

    for it in range(ITERS):
        last = it == ITERS - 1
        a_in, p_in = answer_in.at[it], product_in.at[it]

        answer_out[...] = (
            dot(gather[...], row_blocks[...].reshape(BR * WIDTH, TILE)).astype(BF16).reshape(answer_out.shape)
        )

        for o in PLANE:
            to = at.plane(o)
            copy_to(
                answer_out.at[pair(to)], a_in.at[pair(me)], answer_sem.at[it, 0], answer_sem.at[it, 1], to, z
            ).start()
        a_in[pair(me)] = answer_out[pair(me)]

        def backward(i):
            for u in range(STEP):
                tile = i * STEP + u
                x = row_blocks[table[T_REMOTE_ROW, tile]]
                product[tile] = dot(x, eff[tile]).astype(BF16)

        loop(0, LT // STEP, backward)

        def fill_product(p, ref):
            for s in range(MOST):
                ref[MOST * p + s] = product[table[T_FIRST + s, p]]

        for o in PLANE:
            to = at.plane(o)
            fill_product(to, product_out)
            copy_to(
                product_out.at[pair(to)], p_in.at[pair(me)], product_sem.at[it, 0], product_sem.at[it, 1], to, z
            ).start()
        fill_product(me, p_in)

        for j in range(BR):
            padded[j, PAD] = row_blocks[j]

        total[...] = jnp.zeros_like(total)

        def window(ref, index, row_tile):
            return ref[index, pl.ds(PAD - row_tile, BR)].reshape(BR * WIDTH, TILE)

        def local(i):
            value = total[...]
            for u in range(STEP):
                tile = i * STEP + u
                r, c = table[T_LOCAL_ROW, tile], table[T_LOCAL_COL, tile]
                value += dot(window(padded, c, r), eff[LT + tile], ((1,), (1,)))
                value += dot(window(padded, r, c), eff[LT + tile])
            total[...] = value

        loop(0, LOC // STEP, local)

        for dz in DZ:
            other = at.split(dz)
            copy_to(
                total.at[pl.ds(other * QROWS, QROWS)], parts.at[it, dz], part_sem.at[it, 0], part_sem.at[it, 1], me, other
            ).start()
        late[...] = jnp.zeros_like(late)

        others = pl.ds(0, MOST * (GROUPS - 1))
        wait_all(a_in.at[others], answer_sem.at[it, 0], answer_sem.at[it, 1], at)

        def forward(i):
            value = late[...]
            for u in range(STEP):
                tile = i * STEP + u
                slot = table[T_SLOT, tile]
                fetched[u, PAD] = a_in[slot]
                value += dot(window(fetched, u, table[T_REMOTE_ROW, tile]), eff[tile], ((1,), (1,)))
            late[...] = value

        loop(0, LT // STEP, forward)

        wait_all(p_in.at[others], product_sem.at[it, 0], product_sem.at[it, 1], at)
        came = p_in[...].reshape(GROUPS * MOST * WIDTH, TILE)
        for dz in (*DZ, 0):
            other = at.split(dz)
            rows = pl.ds(pl.multiple_of(other * QROWS, QROWS), QROWS)
            rest = late[rows, :] + dot(spread[rows, :], came)
            if dz:
                late_out[rows, :] = rest.astype(BF16)
                copy_to(
                    late_out.at[rows], late_in.at[it, dz], late_sem.at[it, 0], late_sem.at[it, 1], me, other
                ).start()
        mine = pl.ds(z * QROWS, QROWS)
        wait_all(parts.at[it, pl.ds(1, SPLITS - 1)], part_sem.at[it, 0], part_sem.at[it, 1], at)
        summed = (total[mine, :] + rest) + ((parts[it, 1] + parts[it, 2]) + parts[it, 3])
        wait_all(late_in.at[it, pl.ds(1, SPLITS - 1)], late_sem.at[it, 0], late_sem.at[it, 1], at)
        summed += (late_in[it, 1].astype(F32) + late_in[it, 2].astype(F32)) + late_in[it, 3].astype(F32)
        tiles = [
            summed[j * WIDTH : (j + 1) * WIDTH, :] * inv[pl.ds(z * (BR // SPLITS) + j, 1), :]
            for j in range(BR // SPLITS)
        ]
        wide = jnp.concatenate(tiles, axis=1)
        wide_parts = split3(wide)
        gram = jnp.zeros((WIDTH, WIDTH), F32)
        for i in reversed(range(3)):
            left = jnp.concatenate(wide_parts[: 3 - i], axis=0)
            crossed = dot(left, wide_parts[i], ((1,), (1,)))
            for j in reversed(range(3 - i)):
                gram = gram + crossed[j * WIDTH : (j + 1) * WIDTH, :]
        packed = jnp.concatenate([gram[0:8], gram[8:16], jnp.zeros((8, HALF - 2 * WIDTH), F32)], axis=1)

        own = z * NCORE + at.core
        near_gram[it, own] = packed
        for offset in NEAR:
            row, split = at.near(offset)
            copy_to(
                near_gram.at[it, own], near_gram.at[it, own], near_sem.at[it, 0], near_sem.at[it, 1], row, split
            ).start()
        if not last:
            image[mine, :] = jnp.concatenate(tiles, axis=0)
            for dz in DZ:
                copy_to(image.at[mine], image.at[mine], image_sem.at[0], image_sem.at[1], me, at.split(dz)).start()
        wait_all(near_gram.at[it, pl.ds(0, NCORE * SPLITS - 1)], near_sem.at[it, 0], near_sem.at[it, 1], at)
        near_sum = near_gram[it, 0]
        for i in range(1, NCORE * SPLITS):
            near_sum = near_sum + near_gram[it, i]

        own = at.x * NY + at.y
        far_gram[it, own] = near_sum
        for offset in FAR:
            row, split = at.far(offset)
            copy_to(
                far_gram.at[it, own], far_gram.at[it, own], far_sem.at[it, 0], far_sem.at[it, 1], row, split
            ).start()
        if not last:
            wait_all(image.at[pl.ds(0, (SPLITS - 1) * QROWS)], image_sem.at[0], image_sem.at[1], at)
            for j in range(BR):
                pieces = split3(image[j * WIDTH : (j + 1) * WIDTH, :])
                image_parts[j] = jnp.concatenate([pieces[i] for i in RIGHT], axis=0)
        wait_all(far_gram.at[it, pl.ds(0, NX * NY - 1)], far_sem.at[it, 0], far_sem.at[it, 1], at)
        packed = far_gram[it, 0]
        for i in range(1, NX * NY):
            packed = packed + far_gram[it, i]
        gram = jnp.concatenate([packed[:, 0:WIDTH], packed[:, WIDTH : 2 * WIDTH]], axis=0)
        inverse = factor_inverse(gram / VERTICES)
        if last:
            out[...] = dot(inverse, jnp.concatenate([wide_parts[i] for i in RIGHT], axis=0))
        else:
            for j in range(BR):
                set_rows(j, dot(inverse, image_parts[j]))


def per_device(
    local_weights, local_gains, local_coords, remote_weights, remote_gains, remote_groups, remote_coords, start_block
):
    dma = pltpu.SemaphoreType.DMA
    return pl.pallas_call(
        whole_kernel,
        out_shape=pltpu.VMEM((WIDTH, QROWS // WIDTH * TILE), F32),
        in_specs=[HBM] * 8,
        out_specs=VMEM,
        scratch_shapes=[
            pltpu.VMEM((1, LT), jnp.int32),
            pltpu.VMEM((2, LOC), jnp.int32),
            pltpu.VMEM((2, LT), jnp.int32),
            pltpu.VMEM((LOC, 2, TILE), F32),
            pltpu.VMEM((LT, 2, TILE), F32),
            pltpu.VMEM((WIDTH, BR * TILE), F32),
            pltpu.VMEM((LT + LOC, TILE, TILE), BF16),
            pltpu.VMEM((8, HALF), jnp.int32),
            pltpu.SMEM((8, HALF), jnp.int32),
            pltpu.VMEM((LT, TILE), F32),
            pltpu.VMEM((LT + 2 * LOC, TILE), F32),
            pltpu.VMEM((GROUPS, 8, HALF), F32),
            pltpu.VMEM((GROUPS, 8, HALF), F32),
            pltpu.VMEM((SPLITS, BR, TILE), F32),
            pltpu.VMEM((BR, TILE), F32),
            pltpu.VMEM((BR * WIDTH, GROUPS * MOST * WIDTH), BF16),
            pltpu.VMEM((GROUPS * MOST * WIDTH, BR * WIDTH), BF16),
            pltpu.VMEM((BR, WIDTH, TILE), BF16),
            pltpu.VMEM((BR, 2 * PAD + 1, WIDTH, TILE), BF16),
            pltpu.VMEM((GROUPS * MOST, WIDTH, TILE), BF16),
            pltpu.VMEM((ITERS, GROUPS * MOST, WIDTH, TILE), BF16),
            pltpu.VMEM((LT, WIDTH, TILE), BF16),
            pltpu.VMEM((GROUPS * MOST, WIDTH, TILE), BF16),
            pltpu.VMEM((ITERS, GROUPS * MOST, WIDTH, TILE), BF16),
            pltpu.VMEM((STEP, 2 * PAD + 1, WIDTH, TILE), BF16),
            pltpu.VMEM((BR * WIDTH, TILE), F32),
            pltpu.VMEM((ITERS, SPLITS, QROWS, TILE), F32),
            pltpu.VMEM((BR * WIDTH, TILE), F32),
            pltpu.VMEM((BR * WIDTH, TILE), BF16),
            pltpu.VMEM((ITERS, SPLITS, QROWS, TILE), BF16),
            pltpu.VMEM((BR * WIDTH, TILE), F32),
            pltpu.VMEM((BR, len(RIGHT) * WIDTH, TILE), BF16),
            pltpu.VMEM((ITERS, NCORE * SPLITS, 8, HALF), F32),
            pltpu.VMEM((ITERS, NX * NY, 8, HALF), F32),
            dma(((LT + LOC) // CHUNK,)),
            dma((6,)),
            dma((1,)),
            dma((2,)),
            dma((2,)),
            dma((ITERS, 2)),
            dma((ITERS, 2)),
            dma((ITERS, 2)),
            dma((ITERS, 2)),
            dma((2,)),
            dma((ITERS, 2)),
            dma((ITERS, 2)),
        ],
        compiler_params=pltpu.CompilerParams(
            collective_id=0, has_side_effects=True, vmem_limit_bytes=60 << 20
        ),
        name="iterate",
    )(
        remote_groups[0], local_coords[0, 0].T, remote_coords[0, 0].T, local_gains[0, 0], remote_gains[0, 0],
        start_block, local_weights[0, 0], remote_weights[0, 0],
    )


def solution(mesh):
    in_specs = (
        P("rows", "cols", None, None, None),
        P("rows", "cols", None, None, None),
        P("rows", "cols", None, None),
        P("rows", "cols", None, None, None),
        P("rows", "cols", None, None, None),
        P("rows", "cols", None),
        P("rows", "cols", None, None),
        P(None, "rows"),
    )
    out_specs = P(None, ("rows", "cols"))
    return jax.shard_map(
        per_device, mesh=mesh, in_specs=in_specs, out_specs=out_specs, check_vma=False
    )
```

```python
import jax
import jax.numpy as jnp
from jax import lax
from jax.experimental import pallas as pl
from jax.experimental.pallas import tpu as pltpu
from jax.sharding import PartitionSpec as P

TILE = 256
HALF = 128
WIDTH = 16
BR = 16
MOST = 2
ITERS = 2
LOC = 48
LT = 32
GROUPS = 32
SPLITS = 4
QROWS = BR // SPLITS * WIDTH
NX, NY, NCORE = 4, 4, 2
CHUNK = 8
STEP = 4
VERTICES = GROUPS * BR * TILE
PAD = BR - 1
MESH = pl.DeviceIdType.MESH
VMEM = pl.BlockSpec(memory_space=pltpu.VMEM)
F32 = jnp.float32
BF16 = jnp.bfloat16

HBM = pl.BlockSpec(memory_space=pltpu.HBM)
T_REMOTE_ROW, T_REMOTE_COL, T_LOCAL_ROW, T_LOCAL_COL, T_SLOT, T_FIRST = range(6)
LEFT, RIGHT = (0, 0, 1, 0, 1, 2), (0, 1, 0, 2, 1, 0)


def ring(distance, size):
    return min(distance, size - distance)


PLANE = sorted(
    range(1, NX * NY * NCORE), key=lambda o: -ring(o // (NCORE * NY), NX) - ring(o // NCORE % NY, NY)
)
NEAR = sorted(range(1, NCORE * SPLITS), key=lambda o: -ring(o // NCORE, SPLITS))
FAR = sorted(range(1, NX * NY), key=lambda o: -ring(o // NY, NX) - ring(o % NY, NY))
DZ = (2, 1, 3)


def dot(a, b, dims=((1,), (0,))):
    return lax.dot_general(a, b, (dims, ((), ())), preferred_element_type=F32)


def split3(value):
    high = value.astype(BF16)
    rest = value - high.astype(F32)
    middle = rest.astype(BF16)
    return high, middle, (rest - middle.astype(F32)).astype(BF16)


def select_sum(hot, value, dims=((1,), (0,))):
    high, middle, low = split3(value)
    return dot(hot, high, dims) + (dot(hot, middle, dims) + dot(hot, low, dims))


def iota(shape, dim):
    return lax.broadcasted_iota(jnp.int32, shape, dim)


def factor_inverse(gram):
    copies = len(LEFT) * WIDTH
    shape = (WIDTH, HALF)
    row, lane = iota(shape, 0), iota(shape, 1)
    work = jnp.where((lane % WIDTH == row) & (lane < copies), 1.0, 0.0)
    columns = [jnp.broadcast_to(gram[:, k : k + 1], shape) for k in range(WIDTH)]
    roots = jnp.zeros(shape, F32)
    for k in range(WIDTH):
        pivot = jnp.broadcast_to(columns[k][k : k + 1, :], shape)
        roots = jnp.where(row == k, 1.0 / jnp.sqrt(pivot), roots)
        if k == WIDTH - 1:
            break
        factor = jnp.where(row > k, columns[k] * (1.0 / pivot), 0.0)
        for j in range(k + 1, WIDTH):
            columns[j] = columns[j] - factor * jnp.broadcast_to(columns[j][k : k + 1, :], shape)
        work = work - factor * jnp.broadcast_to(work[k : k + 1, :], shape)
    inverse = work * roots
    high, middle, low = (part.astype(F32) for part in split3(inverse))
    part = lane // WIDTH
    chosen = jnp.where((part == 2) | (part == 4), middle, jnp.where(part == 5, low, high))
    return chosen.astype(BF16)[:, 0:copies]


class Place:
    def __init__(self):
        self.me, self.z = lax.axis_index("rows"), lax.axis_index("cols")
        self.core, self.y, self.x = self.me % NCORE, (self.me // NCORE) % NY, self.me // (NCORE * NY)
        self.cores = [(self.core + d) % NCORE for d in range(NCORE)]
        self.ys = [((self.y + d) % NY) * NCORE for d in range(NY)]
        self.xs = [((self.x + d) % NX) * (NY * NCORE) for d in range(NX)]
        self.zs = [(self.z + d) % SPLITS for d in range(SPLITS)]

    def plane(self, offset):
        return self.xs[offset // (NCORE * NY)] + self.ys[(offset // NCORE) % NY] + self.cores[offset % NCORE]

    def split(self, dz):
        return self.zs[dz]

    def near(self, offset):
        return self.xs[0] + self.ys[0] + self.cores[offset % NCORE], self.zs[offset // NCORE]

    def far(self, offset):
        return self.xs[offset // NY] + self.ys[offset % NY] + self.core, self.z


def copy_to(source, target, send_sem, recv_sem, row, split):
    return pltpu.make_async_remote_copy(
        src_ref=source, dst_ref=target, send_sem=send_sem, recv_sem=recv_sem,
        device_id=(row, split), device_id_type=MESH,
    )


def wait_all(ref, send_sem, recv_sem, place):
    copy_to(ref, ref, send_sem, recv_sem, place.me, place.z).wait()


def loop(start, stop, body):
    def step(i, carry):
        body(i)
        return carry

    lax.fori_loop(start, stop, step, 0)


def whole_kernel(
    groups_h, local_coords_h, remote_coords_h, local_gains_h, remote_gains_h, start_h, local_w, remote_w,
    out,
    groups, local_coords, remote_coords, local_gains, remote_gains, start,
    eff, table_v, table, column_sums, sums, deg_out, deg_in, split_part, inv, spread, gather, row_blocks,
    padded, answer_out, answer_in, product, product_out, product_in, fetched, total,
    parts, late, late_out, late_in, image, image_parts, near_gram, far_gram,
    load_sem, small_sem, table_sem, deg_sem, zdeg_sem, answer_sem, product_sem,
    part_sem, late_sem, image_sem, near_sem, far_sem,
):
    at = Place()
    me, z = at.me, at.z
    first = LT // CHUNK
    chunks = (LT + LOC) // CHUNK

    def load(c):
        chunk = pl.ds(c * CHUNK, CHUNK)
        source = remote_w.at[chunk] if c < first else local_w.at[pl.ds((c - first) * CHUNK, CHUNK)]
        return pltpu.make_async_copy(source, eff.at[chunk], load_sem.at[c])

    small = [
        pltpu.make_async_copy(source, target, small_sem.at[i])
        for i, (source, target) in enumerate(
            [
                (groups_h, groups), (remote_coords_h, remote_coords), (local_coords_h, local_coords),
                (remote_gains_h, remote_gains), (local_gains_h, local_gains), (start_h, start),
            ]
        )
    ]
    for copy in small[:4]:
        copy.start()
    for c in range(first):
        load(c).start()

    barrier = pltpu.get_barrier_semaphore()
    greeted = [(at.plane(o), z) for o in PLANE] + [at.near(o) for o in NEAR if o >= NCORE]

    def pair(p):
        return pl.ds(MOST * p, MOST)

    ones = jnp.ones((8, TILE), BF16)

    def scale(tile0, gains, gain0, row_at, keep, col_at):
        row_gains = jnp.concatenate([gains[gain0 + t, 0:1, :] for t in range(CHUNK)], axis=0).T
        for t in range(CHUNK):
            scaled = (
                row_gains[:, t : t + 1] * eff[tile0 + t].astype(F32) * gains[gain0 + t, 1:2, :]
            ).astype(BF16)
            eff[tile0 + t] = scaled
            size = jnp.abs(scaled)
            sums[pl.ds(row_at + t, 1), :] = dot(ones, size, ((1,), (1,)))[0:1, :]
            keep(col_at + t, dot(ones, size))

    def remote_chunk(c):
        chunk = pl.ds(c * CHUNK, CHUNK)
        pltpu.make_async_copy(remote_w.at[chunk], eff.at[chunk], load_sem.at[c]).wait()

        def keep(t, value):
            column_sums[pl.ds(t, 1), :] = value[0:1, :]

        scale(c * CHUNK, remote_gains, c * CHUNK, c * CHUNK, keep, c * CHUNK)

    def local_chunk(c):
        pltpu.make_async_copy(
            local_w.at[pl.ds(c * CHUNK, CHUNK)],
            eff.at[pl.ds(LT + c * CHUNK, CHUNK)],
            load_sem.at[first + c],
        ).wait()

        def keep(t, value):
            sums[pl.ds(t, 1), :] = value[0:1, :]

        scale(LT + c * CHUNK, local_gains, c * CHUNK, LT + c * CHUNK, keep, LT + LOC + c * CHUNK)

    def make_tables():
        for copy in small[:3]:
            copy.wait()
        group = jnp.broadcast_to(groups[...], (GROUPS, LT))
        slot_group, tile_id = iota((GROUPS, LT), 0), iota((GROUPS, LT), 1)
        named = group == slot_group
        lowest = jnp.min(jnp.where(named, tile_id, LT - 1), axis=1, keepdims=True)
        highest = jnp.max(jnp.where(named, tile_id, -1), axis=1, keepdims=True)
        is_first, is_second = named & (tile_id == lowest), named & (tile_id == highest)
        slot = MOST * slot_group + jnp.where(is_second, 1, 0)
        named_t = jnp.transpose(group) == iota((LT, GROUPS), 1)
        tile_t = iota((LT, GROUPS), 0)
        table_v[...] = jnp.zeros_like(table_v)
        table_v[T_REMOTE_ROW : T_REMOTE_ROW + 2, 0:LT] = remote_coords[...]
        table_v[T_LOCAL_ROW : T_LOCAL_ROW + 2, 0:LOC] = local_coords[...]
        table_v[T_SLOT : T_SLOT + 1, 0:LT] = jnp.sum(jnp.where(named, slot, 0), axis=0, keepdims=True)
        table_v[T_FIRST : T_FIRST + 1, 0:GROUPS] = jnp.min(jnp.where(named_t, tile_t, LT - 1), axis=0, keepdims=True)
        table_v[T_FIRST + 1 : T_FIRST + 2, 0:GROUPS] = jnp.max(jnp.where(named_t, tile_t, 0), axis=0, keepdims=True)
        table_copy = pltpu.make_async_copy(table_v, table, table_sem.at[0])
        table_copy.start()
        hot_slots = jnp.concatenate([jnp.where(hot, 1.0, 0.0) for hot in (is_first, is_second)], axis=0)
        target = jnp.broadcast_to(remote_coords[1:2, :].astype(F32) + 1.0, (MOST * GROUPS, LT))
        slot_column = jnp.sum(hot_slots * target, axis=1, keepdims=True) - 1.0
        slot_column = jnp.broadcast_to(slot_column, (MOST * GROUPS, HALF))
        return hot_slots.astype(BF16), slot_column, table_copy

    share = -(-len(greeted) // (first - 1))
    later = [load(c) for c in range(first, chunks)] + small[4:]
    for c in range(first):
        for row, split in greeted[c * share : (c + 1) * share]:
            pl.semaphore_signal(barrier, inc=1, device_id=(row, split), device_id_type=MESH)
        for copy in later[c * 2 : c * 2 + 2]:
            copy.start()
        if c == 0:
            tables = make_tables()
            small[3].wait()
        remote_chunk(c)

    hot_slots, slot_column, table_copy = tables
    pl.semaphore_wait(barrier, GROUPS - 1 + NCORE * SPLITS - 2)

    lanes = iota((1, HALF), 1)
    slot_sums = select_sum(hot_slots, column_sums[...])
    for p in range(GROUPS):
        pieces = []
        for s in range(MOST):
            row = slot_sums[s * GROUPS + p : s * GROUPS + p + 1, :]
            pieces += [row[:, 0:HALF], row[:, HALF:TILE]]
        columns = [slot_column[s * GROUPS + p : s * GROUPS + p + 1, :] for s in range(MOST)]
        by_lane = jnp.where(lanes % 8 < 2, columns[0], jnp.where(lanes % 8 < 4, columns[1], -1.0))
        deg_out[p] = jnp.concatenate(pieces + [by_lane, *columns, jnp.zeros((1, HALF), F32)], axis=0)
    for o in PLANE:
        to = at.plane(o)
        copy_to(deg_out.at[to], deg_in.at[me], deg_sem.at[0], deg_sem.at[1], to, z).start()
    deg_in[me] = deg_out[me]
    small[4].wait()
    loop(0, LOC // CHUNK, local_chunk)
    small[5].wait()
    table_copy.wait()

    def hot_rows(row):
        return jnp.where(jnp.broadcast_to(row, (BR, row.shape[1])) == iota((BR, row.shape[1]), 0), 1.0, 0.0).astype(BF16)

    own = select_sum(hot_rows(remote_coords[0:1, :]), sums[0:LT, :])
    own += select_sum(hot_rows(local_coords[0:1, :]), sums[LT : LT + LOC, :])
    own += select_sum(hot_rows(local_coords[1:2, :]), sums[LT + LOC : LT + 2 * LOC, :])
    wait_all(deg_in.at[pl.ds(0, GROUPS - 1)], deg_sem.at[0], deg_sem.at[1], at)
    came = deg_in[...].reshape(GROUPS * 8, HALF)
    blocks = []
    for b in range(GROUPS * 8 // HALF):
        column = jnp.full((1, HALF), -1.0, F32)
        for i in range(HALF // 8):
            column = jnp.where(lanes // 8 == i, deg_in[b * (HALF // 8) + i, 4:5, :], column)
        blocks.append(column)
    column = jnp.broadcast_to(jnp.concatenate(blocks, axis=1), (2 * BR, GROUPS * 8))
    row, lane8 = iota(column.shape, 0), iota(column.shape, 1) % 4
    chosen = (column == (row % BR).astype(F32)) & (lane8 % 2 == row // BR)
    added = select_sum(jnp.where(chosen, 1.0, 0.0).astype(BF16), came)
    split_part[z] = own + jnp.concatenate([added[0:BR, :], added[BR : 2 * BR, :]], axis=1)

    for dz in DZ:
        copy_to(split_part.at[z], split_part.at[z], zdeg_sem.at[0], zdeg_sem.at[1], me, at.split(dz)).start()

    padded[...] = jnp.zeros_like(padded)
    fetched[...] = jnp.zeros_like(fetched)
    row = iota((BR * WIDTH, HALF), 0)
    lane = iota((BR * WIDTH, HALF), 1)
    row_tile = (row // WIDTH).astype(F32)
    per = HALF // WIDTH
    for q in range(GROUPS * MOST // per):
        column = jnp.zeros((1, HALF), F32)
        for i in range(per):
            at_slot = deg_in[q * (per // MOST) + i // MOST, 5 + i % MOST : 6 + i % MOST, :]
            column = jnp.where(lanes // WIDTH == i, at_slot, column)
        chosen = (jnp.broadcast_to(column, row.shape) == row_tile) & (lane % WIDTH == row % WIDTH)
        spread[:, q * HALF : (q + 1) * HALF] = jnp.where(chosen, 1.0, 0.0).astype(BF16)
    lane = iota((WIDTH, TILE), 1)
    diagonal = lane % WIDTH == iota((WIDTH, TILE), 0)
    lane_tile = (lane // WIDTH).astype(F32)
    for slot in range(GROUPS * MOST):
        own = deg_in[slot // MOST, 5 + slot % MOST : 6 + slot % MOST, :]
        own = jnp.broadcast_to(jnp.concatenate([own, own], axis=1), (WIDTH, TILE))
        gather[slot * WIDTH : (slot + 1) * WIDTH, :] = jnp.where(diagonal & (own == lane_tile), 1.0, 0.0).astype(BF16)

    wait_all(split_part.at[pl.ds(0, SPLITS - 1)], zdeg_sem.at[0], zdeg_sem.at[1], at)
    inv[...] = 1.0 / jnp.sqrt((split_part[0] + split_part[1]) + (split_part[2] + split_part[3]))

    def set_rows(j, vectors):
        scaled = (vectors * inv[j : j + 1, :]).astype(BF16)
        row_blocks[j] = scaled

    for j in range(BR):
        set_rows(j, start[:, j * TILE : (j + 1) * TILE])

    for it in range(ITERS):
        last = it == ITERS - 1
        a_in, p_in = answer_in.at[it], product_in.at[it]

        answer_out[...] = (
            dot(gather[...], row_blocks[...].reshape(BR * WIDTH, TILE)).astype(BF16).reshape(answer_out.shape)
        )

        for o in PLANE:
            to = at.plane(o)
            copy_to(
                answer_out.at[pair(to)], a_in.at[pair(me)], answer_sem.at[it, 0], answer_sem.at[it, 1], to, z
            ).start()
        a_in[pair(me)] = answer_out[pair(me)]

        def backward(i):
            for u in range(STEP):
                tile = i * STEP + u
                x = row_blocks[table[T_REMOTE_ROW, tile]]
                product[tile] = dot(x, eff[tile]).astype(BF16)

        loop(0, LT // STEP, backward)

        def fill_product(p, ref):
            for s in range(MOST):
                ref[MOST * p + s] = product[table[T_FIRST + s, p]]

        for o in PLANE:
            to = at.plane(o)
            fill_product(to, product_out)
            copy_to(
                product_out.at[pair(to)], p_in.at[pair(me)], product_sem.at[it, 0], product_sem.at[it, 1], to, z
            ).start()
        fill_product(me, p_in)

        for j in range(BR):
            padded[j, PAD] = row_blocks[j]

        total[...] = jnp.zeros_like(total)

        def window(ref, index, row_tile):
            return ref[index, pl.ds(PAD - row_tile, BR)].reshape(BR * WIDTH, TILE)

        def local(i):
            value = total[...]
            for u in range(STEP):
                tile = i * STEP + u
                r, c = table[T_LOCAL_ROW, tile], table[T_LOCAL_COL, tile]
                value += dot(window(padded, c, r), eff[LT + tile], ((1,), (1,)))
                value += dot(window(padded, r, c), eff[LT + tile])
            total[...] = value

        loop(0, LOC // STEP, local)

        for dz in DZ:
            other = at.split(dz)
            copy_to(
                total.at[pl.ds(other * QROWS, QROWS)], parts.at[it, dz], part_sem.at[it, 0], part_sem.at[it, 1], me, other
            ).start()
        late[...] = jnp.zeros_like(late)

        others = pl.ds(0, MOST * (GROUPS - 1))
        wait_all(a_in.at[others], answer_sem.at[it, 0], answer_sem.at[it, 1], at)

        def forward(i):
            value = late[...]
            for u in range(STEP):
                tile = i * STEP + u
                slot = table[T_SLOT, tile]
                fetched[u, PAD] = a_in[slot]
                value += dot(window(fetched, u, table[T_REMOTE_ROW, tile]), eff[tile], ((1,), (1,)))
            late[...] = value

        loop(0, LT // STEP, forward)

        wait_all(p_in.at[others], product_sem.at[it, 0], product_sem.at[it, 1], at)
        rest = late[...] + dot(spread[...], p_in[...].reshape(GROUPS * MOST * WIDTH, TILE))
        late_out[...] = rest.astype(BF16)
        for dz in DZ:
            other = at.split(dz)
            copy_to(
                late_out.at[pl.ds(other * QROWS, QROWS)], late_in.at[it, dz],
                late_sem.at[it, 0], late_sem.at[it, 1], me, other,
            ).start()
        late[...] = rest
        mine = pl.ds(z * QROWS, QROWS)
        wait_all(parts.at[it, pl.ds(1, SPLITS - 1)], part_sem.at[it, 0], part_sem.at[it, 1], at)
        summed = (total[mine, :] + late[mine, :]) + ((parts[it, 1] + parts[it, 2]) + parts[it, 3])
        wait_all(late_in.at[it, pl.ds(1, SPLITS - 1)], late_sem.at[it, 0], late_sem.at[it, 1], at)
        summed += (late_in[it, 1].astype(F32) + late_in[it, 2].astype(F32)) + late_in[it, 3].astype(F32)
        tiles = [
            summed[j * WIDTH : (j + 1) * WIDTH, :] * inv[pl.ds(z * (BR // SPLITS) + j, 1), :]
            for j in range(BR // SPLITS)
        ]
        wide = jnp.concatenate(tiles, axis=1)
        wide_parts = split3(wide)
        gram = jnp.zeros((WIDTH, WIDTH), F32)
        for i in reversed(range(3)):
            left = jnp.concatenate(wide_parts[: 3 - i], axis=0)
            crossed = dot(left, wide_parts[i], ((1,), (1,)))
            for j in reversed(range(3 - i)):
                gram = gram + crossed[j * WIDTH : (j + 1) * WIDTH, :]
        packed = jnp.concatenate([gram[0:8], gram[8:16], jnp.zeros((8, HALF - 2 * WIDTH), F32)], axis=1)

        own = z * NCORE + at.core
        near_gram[it, own] = packed
        for offset in NEAR:
            row, split = at.near(offset)
            copy_to(
                near_gram.at[it, own], near_gram.at[it, own], near_sem.at[it, 0], near_sem.at[it, 1], row, split
            ).start()
        if not last:
            image[mine, :] = jnp.concatenate(tiles, axis=0)
            for dz in DZ:
                copy_to(image.at[mine], image.at[mine], image_sem.at[0], image_sem.at[1], me, at.split(dz)).start()
        wait_all(near_gram.at[it, pl.ds(0, NCORE * SPLITS - 1)], near_sem.at[it, 0], near_sem.at[it, 1], at)
        near_sum = near_gram[it, 0]
        for i in range(1, NCORE * SPLITS):
            near_sum = near_sum + near_gram[it, i]

        own = at.x * NY + at.y
        far_gram[it, own] = near_sum
        for offset in FAR:
            row, split = at.far(offset)
            copy_to(
                far_gram.at[it, own], far_gram.at[it, own], far_sem.at[it, 0], far_sem.at[it, 1], row, split
            ).start()
        if not last:
            wait_all(image.at[pl.ds(0, (SPLITS - 1) * QROWS)], image_sem.at[0], image_sem.at[1], at)
            for j in range(BR):
                pieces = split3(image[j * WIDTH : (j + 1) * WIDTH, :])
                image_parts[j] = jnp.concatenate([pieces[i] for i in RIGHT], axis=0)
        wait_all(far_gram.at[it, pl.ds(0, NX * NY - 1)], far_sem.at[it, 0], far_sem.at[it, 1], at)
        packed = far_gram[it, 0]
        for i in range(1, NX * NY):
            packed = packed + far_gram[it, i]
        gram = jnp.concatenate([packed[:, 0:WIDTH], packed[:, WIDTH : 2 * WIDTH]], axis=0)
        inverse = factor_inverse(gram / VERTICES)
        if last:
            out[...] = dot(inverse, jnp.concatenate([wide_parts[i] for i in RIGHT], axis=0))
        else:
            for j in range(BR):
                set_rows(j, dot(inverse, image_parts[j]))


def per_device(
    local_weights, local_gains, local_coords, remote_weights, remote_gains, remote_groups, remote_coords, start_block
):
    dma = pltpu.SemaphoreType.DMA
    return pl.pallas_call(
        whole_kernel,
        out_shape=pltpu.VMEM((WIDTH, QROWS // WIDTH * TILE), F32),
        in_specs=[HBM] * 8,
        out_specs=VMEM,
        scratch_shapes=[
            pltpu.VMEM((1, LT), jnp.int32),
            pltpu.VMEM((2, LOC), jnp.int32),
            pltpu.VMEM((2, LT), jnp.int32),
            pltpu.VMEM((LOC, 2, TILE), F32),
            pltpu.VMEM((LT, 2, TILE), F32),
            pltpu.VMEM((WIDTH, BR * TILE), F32),
            pltpu.VMEM((LT + LOC, TILE, TILE), BF16),
            pltpu.VMEM((8, HALF), jnp.int32),
            pltpu.SMEM((8, HALF), jnp.int32),
            pltpu.VMEM((LT, TILE), F32),
            pltpu.VMEM((LT + 2 * LOC, TILE), F32),
            pltpu.VMEM((GROUPS, 8, HALF), F32),
            pltpu.VMEM((GROUPS, 8, HALF), F32),
            pltpu.VMEM((SPLITS, BR, TILE), F32),
            pltpu.VMEM((BR, TILE), F32),
            pltpu.VMEM((BR * WIDTH, GROUPS * MOST * WIDTH), BF16),
            pltpu.VMEM((GROUPS * MOST * WIDTH, BR * WIDTH), BF16),
            pltpu.VMEM((BR, WIDTH, TILE), BF16),
            pltpu.VMEM((BR, 2 * PAD + 1, WIDTH, TILE), BF16),
            pltpu.VMEM((GROUPS * MOST, WIDTH, TILE), BF16),
            pltpu.VMEM((ITERS, GROUPS * MOST, WIDTH, TILE), BF16),
            pltpu.VMEM((LT, WIDTH, TILE), BF16),
            pltpu.VMEM((GROUPS * MOST, WIDTH, TILE), BF16),
            pltpu.VMEM((ITERS, GROUPS * MOST, WIDTH, TILE), BF16),
            pltpu.VMEM((STEP, 2 * PAD + 1, WIDTH, TILE), BF16),
            pltpu.VMEM((BR * WIDTH, TILE), F32),
            pltpu.VMEM((ITERS, SPLITS, QROWS, TILE), F32),
            pltpu.VMEM((BR * WIDTH, TILE), F32),
            pltpu.VMEM((BR * WIDTH, TILE), BF16),
            pltpu.VMEM((ITERS, SPLITS, QROWS, TILE), BF16),
            pltpu.VMEM((BR * WIDTH, TILE), F32),
            pltpu.VMEM((BR, len(RIGHT) * WIDTH, TILE), BF16),
            pltpu.VMEM((ITERS, NCORE * SPLITS, 8, HALF), F32),
            pltpu.VMEM((ITERS, NX * NY, 8, HALF), F32),
            dma(((LT + LOC) // CHUNK,)),
            dma((6,)),
            dma((1,)),
            dma((2,)),
            dma((2,)),
            dma((ITERS, 2)),
            dma((ITERS, 2)),
            dma((ITERS, 2)),
            dma((ITERS, 2)),
            dma((2,)),
            dma((ITERS, 2)),
            dma((ITERS, 2)),
        ],
        compiler_params=pltpu.CompilerParams(
            collective_id=0, has_side_effects=True, vmem_limit_bytes=60 << 20
        ),
        name="iterate",
    )(
        remote_groups[0], local_coords[0, 0].T, remote_coords[0, 0].T, local_gains[0, 0], remote_gains[0, 0],
        start_block, local_weights[0, 0], remote_weights[0, 0],
    )


def solution(mesh):
    in_specs = (
        P("rows", "cols", None, None, None),
        P("rows", "cols", None, None, None),
        P("rows", "cols", None, None),
        P("rows", "cols", None, None, None),
        P("rows", "cols", None, None, None),
        P("rows", "cols", None),
        P("rows", "cols", None, None),
        P(None, "rows"),
    )
    out_specs = P(None, ("rows", "cols"))
    return jax.shard_map(
        per_device, mesh=mesh, in_specs=in_specs, out_specs=out_specs, check_vma=False
    )
```

```python
import jax
import jax.numpy as jnp
from jax import lax
from jax.experimental import pallas as pl
from jax.experimental.pallas import tpu as pltpu
from jax.sharding import PartitionSpec as P

TILE = 256
HALF = 128
WIDTH = 16
BR = 16
MOST = 2
ITERS = 2
LOC = 48
LT = 32
GROUPS = 32
SPLITS = 4
QROWS = BR // SPLITS * WIDTH
NX, NY, NCORE = 4, 4, 2
CHUNK = 8
STEP = 4
VERTICES = GROUPS * BR * TILE
PAD = BR - 1
MESH = pl.DeviceIdType.MESH
VMEM = pl.BlockSpec(memory_space=pltpu.VMEM)
F32 = jnp.float32
BF16 = jnp.bfloat16

HBM = pl.BlockSpec(memory_space=pltpu.HBM)
T_REMOTE_ROW, T_REMOTE_COL, T_LOCAL_ROW, T_LOCAL_COL, T_SLOT, T_FIRST = range(6)
LEFT, RIGHT = (0, 0, 1, 0, 1, 2), (0, 1, 0, 2, 1, 0)


def ring(distance, size):
    return min(distance, size - distance)


PLANE = sorted(
    range(1, NX * NY * NCORE), key=lambda o: -ring(o // (NCORE * NY), NX) - ring(o // NCORE % NY, NY)
)
NEAR = sorted(range(1, NCORE * SPLITS), key=lambda o: -ring(o // NCORE, SPLITS))
FAR = sorted(range(1, NX * NY), key=lambda o: -ring(o // NY, NX) - ring(o % NY, NY))
DZ = (2, 1, 3)


def dot(a, b, dims=((1,), (0,))):
    return lax.dot_general(a, b, (dims, ((), ())), preferred_element_type=F32)


def split3(value):
    high = value.astype(BF16)
    rest = value - high.astype(F32)
    middle = rest.astype(BF16)
    return high, middle, (rest - middle.astype(F32)).astype(BF16)


def select_sum(hot, value, dims=((1,), (0,))):
    high, middle, low = split3(value)
    return dot(hot, high, dims) + (dot(hot, middle, dims) + dot(hot, low, dims))


def iota(shape, dim):
    return lax.broadcasted_iota(jnp.int32, shape, dim)


def factor_inverse(gram):
    copies = len(LEFT) * WIDTH
    shape = (WIDTH, HALF)
    row, lane = iota(shape, 0), iota(shape, 1)
    work = jnp.where((lane % WIDTH == row) & (lane < copies), 1.0, 0.0)
    columns = [jnp.broadcast_to(gram[:, k : k + 1], shape) for k in range(WIDTH)]
    roots = jnp.zeros(shape, F32)
    for k in range(WIDTH):
        pivot = jnp.broadcast_to(columns[k][k : k + 1, :], shape)
        roots = jnp.where(row == k, 1.0 / jnp.sqrt(pivot), roots)
        if k == WIDTH - 1:
            break
        factor = jnp.where(row > k, columns[k] * (1.0 / pivot), 0.0)
        for j in range(k + 1, WIDTH):
            columns[j] = columns[j] - factor * jnp.broadcast_to(columns[j][k : k + 1, :], shape)
        work = work - factor * jnp.broadcast_to(work[k : k + 1, :], shape)
    inverse = work * roots
    high, middle, low = (part.astype(F32) for part in split3(inverse))
    part = lane // WIDTH
    chosen = jnp.where((part == 2) | (part == 4), middle, jnp.where(part == 5, low, high))
    return chosen.astype(BF16)[:, 0:copies]


class Place:
    def __init__(self):
        self.me, self.z = lax.axis_index("rows"), lax.axis_index("cols")
        self.core, self.y, self.x = self.me % NCORE, (self.me // NCORE) % NY, self.me // (NCORE * NY)
        self.cores = [(self.core + d) % NCORE for d in range(NCORE)]
        self.ys = [((self.y + d) % NY) * NCORE for d in range(NY)]
        self.xs = [((self.x + d) % NX) * (NY * NCORE) for d in range(NX)]
        self.zs = [(self.z + d) % SPLITS for d in range(SPLITS)]

    def plane(self, offset):
        return self.xs[offset // (NCORE * NY)] + self.ys[(offset // NCORE) % NY] + self.cores[offset % NCORE]

    def split(self, dz):
        return self.zs[dz]

    def near(self, offset):
        return self.xs[0] + self.ys[0] + self.cores[offset % NCORE], self.zs[offset // NCORE]

    def far(self, offset):
        return self.xs[offset // NY] + self.ys[offset % NY] + self.core, self.z


def copy_to(source, target, send_sem, recv_sem, row, split):
    return pltpu.make_async_remote_copy(
        src_ref=source, dst_ref=target, send_sem=send_sem, recv_sem=recv_sem,
        device_id=(row, split), device_id_type=MESH,
    )


def wait_all(ref, send_sem, recv_sem, place):
    copy_to(ref, ref, send_sem, recv_sem, place.me, place.z).wait()


def loop(start, stop, body):
    def step(i, carry):
        body(i)
        return carry

    lax.fori_loop(start, stop, step, 0)


def whole_kernel(
    groups_h, local_coords_h, remote_coords_h, local_gains_h, remote_gains_h, start_h, local_w, remote_w,
    out,
    groups, local_coords, remote_coords, local_gains, remote_gains, start,
    eff, table_v, table, column_sums, sums, deg_out, deg_in, split_part, inv, spread, gather, row_blocks,
    padded, answer_out, answer_in, product, product_out, product_in, fetched, total,
    parts, late, late_out, late_in, image, image_parts, near_gram, far_gram,
    load_sem, small_sem, table_sem, deg_sem, zdeg_sem, answer_sem, product_sem,
    part_sem, late_sem, image_sem, near_sem, far_sem,
):
    at = Place()
    me, z = at.me, at.z
    first = LT // CHUNK
    chunks = (LT + LOC) // CHUNK

    def load(c):
        chunk = pl.ds(c * CHUNK, CHUNK)
        source = remote_w.at[chunk] if c < first else local_w.at[pl.ds((c - first) * CHUNK, CHUNK)]
        return pltpu.make_async_copy(source, eff.at[chunk], load_sem.at[c])

    small = [
        pltpu.make_async_copy(source, target, small_sem.at[i])
        for i, (source, target) in enumerate(
            [
                (groups_h, groups), (remote_coords_h, remote_coords), (local_coords_h, local_coords),
                (remote_gains_h, remote_gains), (local_gains_h, local_gains), (start_h, start),
            ]
        )
    ]
    for copy in small[:4]:
        copy.start()
    for c in range(first):
        load(c).start()

    barrier = pltpu.get_barrier_semaphore()
    greeted = [(at.plane(o), z) for o in PLANE] + [at.near(o) for o in NEAR if o >= NCORE]

    def pair(p):
        return pl.ds(MOST * p, MOST)

    ones = jnp.ones((8, TILE), BF16)

    def scale(tile0, gains, gain0, row_at, keep, col_at):
        row_gains = jnp.concatenate([gains[gain0 + t, 0:1, :] for t in range(CHUNK)], axis=0).T
        for t in range(CHUNK):
            scaled = (
                row_gains[:, t : t + 1] * eff[tile0 + t].astype(F32) * gains[gain0 + t, 1:2, :]
            ).astype(BF16)
            eff[tile0 + t] = scaled
            size = jnp.abs(scaled)
            if row_at is not None:
                sums[pl.ds(row_at + t, 1), :] = dot(ones, size, ((1,), (1,)))[0:1, :]
            keep(col_at + t, dot(ones, size))

    def remote_chunk(c):
        chunk = pl.ds(c * CHUNK, CHUNK)
        pltpu.make_async_copy(remote_w.at[chunk], eff.at[chunk], load_sem.at[c]).wait()

        def keep(t, value):
            column_sums[pl.ds(t, 1), :] = value[0:1, :]

        scale(c * CHUNK, remote_gains, c * CHUNK, None, keep, c * CHUNK)

    def local_chunk(c):
        pltpu.make_async_copy(
            local_w.at[pl.ds(c * CHUNK, CHUNK)],
            eff.at[pl.ds(LT + c * CHUNK, CHUNK)],
            load_sem.at[first + c],
        ).wait()

        def keep(t, value):
            sums[pl.ds(t, 1), :] = value[0:1, :]

        scale(LT + c * CHUNK, local_gains, c * CHUNK, LT + c * CHUNK, keep, LT + LOC + c * CHUNK)

    def make_tables():
        for copy in small[:3]:
            copy.wait()
        group = jnp.broadcast_to(groups[...], (GROUPS, LT))
        slot_group, tile_id = iota((GROUPS, LT), 0), iota((GROUPS, LT), 1)
        named = group == slot_group
        lowest = jnp.min(jnp.where(named, tile_id, LT - 1), axis=1, keepdims=True)
        highest = jnp.max(jnp.where(named, tile_id, -1), axis=1, keepdims=True)
        is_first, is_second = named & (tile_id == lowest), named & (tile_id == highest)
        slot = MOST * slot_group + jnp.where(is_second, 1, 0)
        named_t = jnp.transpose(group) == iota((LT, GROUPS), 1)
        tile_t = iota((LT, GROUPS), 0)
        table_v[...] = jnp.zeros_like(table_v)
        table_v[T_REMOTE_ROW : T_REMOTE_ROW + 2, 0:LT] = remote_coords[...]
        table_v[T_LOCAL_ROW : T_LOCAL_ROW + 2, 0:LOC] = local_coords[...]
        table_v[T_SLOT : T_SLOT + 1, 0:LT] = jnp.sum(jnp.where(named, slot, 0), axis=0, keepdims=True)
        table_v[T_FIRST : T_FIRST + 1, 0:GROUPS] = jnp.min(jnp.where(named_t, tile_t, LT - 1), axis=0, keepdims=True)
        table_v[T_FIRST + 1 : T_FIRST + 2, 0:GROUPS] = jnp.max(jnp.where(named_t, tile_t, 0), axis=0, keepdims=True)
        table_copy = pltpu.make_async_copy(table_v, table, table_sem.at[0])
        table_copy.start()
        hot_slots = jnp.concatenate([jnp.where(hot, 1.0, 0.0) for hot in (is_first, is_second)], axis=0)
        target = jnp.broadcast_to(remote_coords[1:2, :].astype(F32) + 1.0, (MOST * GROUPS, LT))
        slot_column = jnp.sum(hot_slots * target, axis=1, keepdims=True) - 1.0
        slot_column = jnp.broadcast_to(slot_column, (MOST * GROUPS, HALF))
        return hot_slots.astype(BF16), slot_column, table_copy

    share = -(-len(greeted) // (first - 1))
    later = [load(c) for c in range(first, chunks)] + small[4:]
    for c in range(first):
        for row, split in greeted[c * share : (c + 1) * share]:
            pl.semaphore_signal(barrier, inc=1, device_id=(row, split), device_id_type=MESH)
        for copy in later[c * 2 : c * 2 + 2]:
            copy.start()
        if c == 0:
            tables = make_tables()
            small[3].wait()
        remote_chunk(c)

    hot_slots, slot_column, table_copy = tables
    pl.semaphore_wait(barrier, GROUPS - 1 + NCORE * SPLITS - 2)

    lanes = iota((1, HALF), 1)
    slot_sums = select_sum(hot_slots, column_sums[...])
    for p in range(GROUPS):
        pieces = []
        for s in range(MOST):
            row = slot_sums[s * GROUPS + p : s * GROUPS + p + 1, :]
            pieces += [row[:, 0:HALF], row[:, HALF:TILE]]
        columns = [slot_column[s * GROUPS + p : s * GROUPS + p + 1, :] for s in range(MOST)]
        by_lane = jnp.where(lanes % 8 < 2, columns[0], jnp.where(lanes % 8 < 4, columns[1], -1.0))
        deg_out[p] = jnp.concatenate(pieces + [by_lane, *columns, jnp.zeros((1, HALF), F32)], axis=0)
    for o in PLANE:
        to = at.plane(o)
        copy_to(deg_out.at[to], deg_in.at[me], deg_sem.at[0], deg_sem.at[1], to, z).start()
    deg_in[me] = deg_out[me]
    small[4].wait()
    loop(0, LOC // CHUNK, local_chunk)

    def remote_row_sums(c):
        for t in range(CHUNK):
            tile = c * CHUNK + t
            sums[pl.ds(tile, 1), :] = dot(ones, jnp.abs(eff[tile]), ((1,), (1,)))[0:1, :]

    loop(0, first, remote_row_sums)
    small[5].wait()
    table_copy.wait()

    def hot_rows(row):
        return jnp.where(jnp.broadcast_to(row, (BR, row.shape[1])) == iota((BR, row.shape[1]), 0), 1.0, 0.0).astype(BF16)

    own = select_sum(hot_rows(remote_coords[0:1, :]), sums[0:LT, :])
    own += select_sum(hot_rows(local_coords[0:1, :]), sums[LT : LT + LOC, :])
    own += select_sum(hot_rows(local_coords[1:2, :]), sums[LT + LOC : LT + 2 * LOC, :])
    wait_all(deg_in.at[pl.ds(0, GROUPS - 1)], deg_sem.at[0], deg_sem.at[1], at)
    came = deg_in[...].reshape(GROUPS * 8, HALF)
    blocks = []
    for b in range(GROUPS * 8 // HALF):
        column = jnp.full((1, HALF), -1.0, F32)
        for i in range(HALF // 8):
            column = jnp.where(lanes // 8 == i, deg_in[b * (HALF // 8) + i, 4:5, :], column)
        blocks.append(column)
    column = jnp.broadcast_to(jnp.concatenate(blocks, axis=1), (2 * BR, GROUPS * 8))
    row, lane8 = iota(column.shape, 0), iota(column.shape, 1) % 4
    chosen = (column == (row % BR).astype(F32)) & (lane8 % 2 == row // BR)
    added = select_sum(jnp.where(chosen, 1.0, 0.0).astype(BF16), came)
    split_part[z] = own + jnp.concatenate([added[0:BR, :], added[BR : 2 * BR, :]], axis=1)

    for dz in DZ:
        copy_to(split_part.at[z], split_part.at[z], zdeg_sem.at[0], zdeg_sem.at[1], me, at.split(dz)).start()

    padded[...] = jnp.zeros_like(padded)
    fetched[...] = jnp.zeros_like(fetched)
    row = iota((BR * WIDTH, HALF), 0)
    lane = iota((BR * WIDTH, HALF), 1)
    row_tile = (row // WIDTH).astype(F32)
    per = HALF // WIDTH
    for q in range(GROUPS * MOST // per):
        column = jnp.zeros((1, HALF), F32)
        for i in range(per):
            at_slot = deg_in[q * (per // MOST) + i // MOST, 5 + i % MOST : 6 + i % MOST, :]
            column = jnp.where(lanes // WIDTH == i, at_slot, column)
        chosen = (jnp.broadcast_to(column, row.shape) == row_tile) & (lane % WIDTH == row % WIDTH)
        spread[:, q * HALF : (q + 1) * HALF] = jnp.where(chosen, 1.0, 0.0).astype(BF16)
    lane = iota((WIDTH, TILE), 1)
    diagonal = lane % WIDTH == iota((WIDTH, TILE), 0)
    lane_tile = (lane // WIDTH).astype(F32)
    for slot in range(GROUPS * MOST):
        own = deg_in[slot // MOST, 5 + slot % MOST : 6 + slot % MOST, :]
        own = jnp.broadcast_to(jnp.concatenate([own, own], axis=1), (WIDTH, TILE))
        gather[slot * WIDTH : (slot + 1) * WIDTH, :] = jnp.where(diagonal & (own == lane_tile), 1.0, 0.0).astype(BF16)

    wait_all(split_part.at[pl.ds(0, SPLITS - 1)], zdeg_sem.at[0], zdeg_sem.at[1], at)
    inv[...] = 1.0 / jnp.sqrt((split_part[0] + split_part[1]) + (split_part[2] + split_part[3]))

    def set_rows(j, vectors):
        scaled = (vectors * inv[j : j + 1, :]).astype(BF16)
        row_blocks[j] = scaled

    for j in range(BR):
        set_rows(j, start[:, j * TILE : (j + 1) * TILE])

    for it in range(ITERS):
        last = it == ITERS - 1
        a_in, p_in = answer_in.at[it], product_in.at[it]

        answer_out[...] = (
            dot(gather[...], row_blocks[...].reshape(BR * WIDTH, TILE)).astype(BF16).reshape(answer_out.shape)
        )

        for o in PLANE:
            to = at.plane(o)
            copy_to(
                answer_out.at[pair(to)], a_in.at[pair(me)], answer_sem.at[it, 0], answer_sem.at[it, 1], to, z
            ).start()
        a_in[pair(me)] = answer_out[pair(me)]

        def backward(i):
            for u in range(STEP):
                tile = i * STEP + u
                x = row_blocks[table[T_REMOTE_ROW, tile]]
                product[tile] = dot(x, eff[tile]).astype(BF16)

        loop(0, LT // STEP, backward)

        def fill_product(p, ref):
            for s in range(MOST):
                ref[MOST * p + s] = product[table[T_FIRST + s, p]]

        for o in PLANE:
            to = at.plane(o)
            fill_product(to, product_out)
            copy_to(
                product_out.at[pair(to)], p_in.at[pair(me)], product_sem.at[it, 0], product_sem.at[it, 1], to, z
            ).start()
        fill_product(me, p_in)

        for j in range(BR):
            padded[j, PAD] = row_blocks[j]

        total[...] = jnp.zeros_like(total)

        def window(ref, index, row_tile):
            return ref[index, pl.ds(PAD - row_tile, BR)].reshape(BR * WIDTH, TILE)

        def local(i):
            value = total[...]
            for u in range(STEP):
                tile = i * STEP + u
                r, c = table[T_LOCAL_ROW, tile], table[T_LOCAL_COL, tile]
                value += dot(window(padded, c, r), eff[LT + tile], ((1,), (1,)))
                value += dot(window(padded, r, c), eff[LT + tile])
            total[...] = value

        loop(0, LOC // STEP, local)

        for dz in DZ:
            other = at.split(dz)
            copy_to(
                total.at[pl.ds(other * QROWS, QROWS)], parts.at[it, dz], part_sem.at[it, 0], part_sem.at[it, 1], me, other
            ).start()
        late[...] = jnp.zeros_like(late)

        others = pl.ds(0, MOST * (GROUPS - 1))
        wait_all(a_in.at[others], answer_sem.at[it, 0], answer_sem.at[it, 1], at)

        def forward(i):
            value = late[...]
            for u in range(STEP):
                tile = i * STEP + u
                slot = table[T_SLOT, tile]
                fetched[u, PAD] = a_in[slot]
                value += dot(window(fetched, u, table[T_REMOTE_ROW, tile]), eff[tile], ((1,), (1,)))
            late[...] = value

        loop(0, LT // STEP, forward)

        wait_all(p_in.at[others], product_sem.at[it, 0], product_sem.at[it, 1], at)
        came = p_in[...].reshape(GROUPS * MOST * WIDTH, TILE)
        for dz in (*DZ, 0):
            other = at.split(dz)
            rows = pl.ds(pl.multiple_of(other * QROWS, QROWS), QROWS)
            rest = late[rows, :] + dot(spread[rows, :], came)
            if dz:
                late_out[rows, :] = rest.astype(BF16)
                copy_to(
                    late_out.at[rows], late_in.at[it, dz], late_sem.at[it, 0], late_sem.at[it, 1], me, other
                ).start()
        mine = pl.ds(z * QROWS, QROWS)
        wait_all(parts.at[it, pl.ds(1, SPLITS - 1)], part_sem.at[it, 0], part_sem.at[it, 1], at)
        summed = (total[mine, :] + rest) + ((parts[it, 1] + parts[it, 2]) + parts[it, 3])
        wait_all(late_in.at[it, pl.ds(1, SPLITS - 1)], late_sem.at[it, 0], late_sem.at[it, 1], at)
        summed += (late_in[it, 1].astype(F32) + late_in[it, 2].astype(F32)) + late_in[it, 3].astype(F32)
        tiles = [
            summed[j * WIDTH : (j + 1) * WIDTH, :] * inv[pl.ds(z * (BR // SPLITS) + j, 1), :]
            for j in range(BR // SPLITS)
        ]
        wide = jnp.concatenate(tiles, axis=1)
        wide_parts = split3(wide)
        gram = jnp.zeros((WIDTH, WIDTH), F32)
        for i in reversed(range(3)):
            left = jnp.concatenate(wide_parts[: 3 - i], axis=0)
            crossed = dot(left, wide_parts[i], ((1,), (1,)))
            for j in reversed(range(3 - i)):
                gram = gram + crossed[j * WIDTH : (j + 1) * WIDTH, :]
        packed = jnp.concatenate([gram[0:8], gram[8:16], jnp.zeros((8, HALF - 2 * WIDTH), F32)], axis=1)

        own = z * NCORE + at.core
        near_gram[it, own] = packed
        for offset in NEAR:
            row, split = at.near(offset)
            copy_to(
                near_gram.at[it, own], near_gram.at[it, own], near_sem.at[it, 0], near_sem.at[it, 1], row, split
            ).start()
        if not last:
            image[mine, :] = jnp.concatenate(tiles, axis=0)
            for dz in DZ:
                copy_to(image.at[mine], image.at[mine], image_sem.at[0], image_sem.at[1], me, at.split(dz)).start()
        wait_all(near_gram.at[it, pl.ds(0, NCORE * SPLITS - 1)], near_sem.at[it, 0], near_sem.at[it, 1], at)
        near_sum = near_gram[it, 0]
        for i in range(1, NCORE * SPLITS):
            near_sum = near_sum + near_gram[it, i]

        own = at.x * NY + at.y
        far_gram[it, own] = near_sum
        for offset in FAR:
            row, split = at.far(offset)
            copy_to(
                far_gram.at[it, own], far_gram.at[it, own], far_sem.at[it, 0], far_sem.at[it, 1], row, split
            ).start()
        if not last:
            wait_all(image.at[pl.ds(0, (SPLITS - 1) * QROWS)], image_sem.at[0], image_sem.at[1], at)
            for j in range(BR):
                pieces = split3(image[j * WIDTH : (j + 1) * WIDTH, :])
                image_parts[j] = jnp.concatenate([pieces[i] for i in RIGHT], axis=0)
        wait_all(far_gram.at[it, pl.ds(0, NX * NY - 1)], far_sem.at[it, 0], far_sem.at[it, 1], at)
        packed = far_gram[it, 0]
        for i in range(1, NX * NY):
            packed = packed + far_gram[it, i]
        gram = jnp.concatenate([packed[:, 0:WIDTH], packed[:, WIDTH : 2 * WIDTH]], axis=0)
        inverse = factor_inverse(gram / VERTICES)
        if last:
            out[...] = dot(inverse, jnp.concatenate([wide_parts[i] for i in RIGHT], axis=0))
        else:
            for j in range(BR):
                set_rows(j, dot(inverse, image_parts[j]))


def per_device(
    local_weights, local_gains, local_coords, remote_weights, remote_gains, remote_groups, remote_coords, start_block
):
    dma = pltpu.SemaphoreType.DMA
    return pl.pallas_call(
        whole_kernel,
        out_shape=pltpu.VMEM((WIDTH, QROWS // WIDTH * TILE), F32),
        in_specs=[HBM] * 8,
        out_specs=VMEM,
        scratch_shapes=[
            pltpu.VMEM((1, LT), jnp.int32),
            pltpu.VMEM((2, LOC), jnp.int32),
            pltpu.VMEM((2, LT), jnp.int32),
            pltpu.VMEM((LOC, 2, TILE), F32),
            pltpu.VMEM((LT, 2, TILE), F32),
            pltpu.VMEM((WIDTH, BR * TILE), F32),
            pltpu.VMEM((LT + LOC, TILE, TILE), BF16),
            pltpu.VMEM((8, HALF), jnp.int32),
            pltpu.SMEM((8, HALF), jnp.int32),
            pltpu.VMEM((LT, TILE), F32),
            pltpu.VMEM((LT + 2 * LOC, TILE), F32),
            pltpu.VMEM((GROUPS, 8, HALF), F32),
            pltpu.VMEM((GROUPS, 8, HALF), F32),
            pltpu.VMEM((SPLITS, BR, TILE), F32),
            pltpu.VMEM((BR, TILE), F32),
            pltpu.VMEM((BR * WIDTH, GROUPS * MOST * WIDTH), BF16),
            pltpu.VMEM((GROUPS * MOST * WIDTH, BR * WIDTH), BF16),
            pltpu.VMEM((BR, WIDTH, TILE), BF16),
            pltpu.VMEM((BR, 2 * PAD + 1, WIDTH, TILE), BF16),
            pltpu.VMEM((GROUPS * MOST, WIDTH, TILE), BF16),
            pltpu.VMEM((ITERS, GROUPS * MOST, WIDTH, TILE), BF16),
            pltpu.VMEM((LT, WIDTH, TILE), BF16),
            pltpu.VMEM((GROUPS * MOST, WIDTH, TILE), BF16),
            pltpu.VMEM((ITERS, GROUPS * MOST, WIDTH, TILE), BF16),
            pltpu.VMEM((STEP, 2 * PAD + 1, WIDTH, TILE), BF16),
            pltpu.VMEM((BR * WIDTH, TILE), F32),
            pltpu.VMEM((ITERS, SPLITS, QROWS, TILE), F32),
            pltpu.VMEM((BR * WIDTH, TILE), F32),
            pltpu.VMEM((BR * WIDTH, TILE), BF16),
            pltpu.VMEM((ITERS, SPLITS, QROWS, TILE), BF16),
            pltpu.VMEM((BR * WIDTH, TILE), F32),
            pltpu.VMEM((BR, len(RIGHT) * WIDTH, TILE), BF16),
            pltpu.VMEM((ITERS, NCORE * SPLITS, 8, HALF), F32),
            pltpu.VMEM((ITERS, NX * NY, 8, HALF), F32),
            dma(((LT + LOC) // CHUNK,)),
            dma((6,)),
            dma((1,)),
            dma((2,)),
            dma((2,)),
            dma((ITERS, 2)),
            dma((ITERS, 2)),
            dma((ITERS, 2)),
            dma((ITERS, 2)),
            dma((2,)),
            dma((ITERS, 2)),
            dma((ITERS, 2)),
        ],
        compiler_params=pltpu.CompilerParams(
            collective_id=0, has_side_effects=True, vmem_limit_bytes=60 << 20
        ),
        name="iterate",
    )(
        remote_groups[0], local_coords[0, 0].T, remote_coords[0, 0].T, local_gains[0, 0], remote_gains[0, 0],
        start_block, local_weights[0, 0], remote_weights[0, 0],
    )


def solution(mesh):
    in_specs = (
        P("rows", "cols", None, None, None),
        P("rows", "cols", None, None, None),
        P("rows", "cols", None, None),
        P("rows", "cols", None, None, None),
        P("rows", "cols", None, None, None),
        P("rows", "cols", None),
        P("rows", "cols", None, None),
        P(None, "rows"),
    )
    out_specs = P(None, ("rows", "cols"))
    return jax.shard_map(
        per_device, mesh=mesh, in_specs=in_specs, out_specs=out_specs, check_vma=False
    )
```

```python
import jax
import jax.numpy as jnp
from jax import lax
from jax.experimental import pallas as pl
from jax.experimental.pallas import tpu as pltpu
from jax.sharding import PartitionSpec as P

TILE = 256
HALF = 128
WIDTH = 16
BR = 16
MOST = 2
ITERS = 2
LOC = 48
LT = 32
GROUPS = 32
SPLITS = 4
QROWS = BR // SPLITS * WIDTH
NX, NY, NCORE = 4, 4, 2
CHUNK = 8
STEP = 4
VERTICES = GROUPS * BR * TILE
PAD = BR - 1
MESH = pl.DeviceIdType.MESH
VMEM = pl.BlockSpec(memory_space=pltpu.VMEM)
F32 = jnp.float32
BF16 = jnp.bfloat16

HBM = pl.BlockSpec(memory_space=pltpu.HBM)
T_REMOTE_ROW, T_REMOTE_COL, T_LOCAL_ROW, T_LOCAL_COL, T_SLOT, T_FIRST = range(6)
LEFT, RIGHT = (0, 0, 1, 0, 1, 2), (0, 1, 0, 2, 1, 0)


def ring(distance, size):
    return min(distance, size - distance)


PLANE = sorted(
    range(1, NX * NY * NCORE), key=lambda o: -ring(o // (NCORE * NY), NX) - ring(o // NCORE % NY, NY)
)
NEAR = sorted(range(1, NCORE * SPLITS), key=lambda o: -ring(o // NCORE, SPLITS))
FAR = sorted(range(1, NX * NY), key=lambda o: -ring(o // NY, NX) - ring(o % NY, NY))
DZ = (2, 1, 3)


def dot(a, b, dims=((1,), (0,))):
    return lax.dot_general(a, b, (dims, ((), ())), preferred_element_type=F32)


def split3(value):
    high = value.astype(BF16)
    rest = value - high.astype(F32)
    middle = rest.astype(BF16)
    return high, middle, (rest - middle.astype(F32)).astype(BF16)


def select_sum(hot, value, dims=((1,), (0,))):
    high, middle, low = split3(value)
    return dot(hot, high, dims) + (dot(hot, middle, dims) + dot(hot, low, dims))


def iota(shape, dim):
    return lax.broadcasted_iota(jnp.int32, shape, dim)


def factor_inverse(gram):
    copies = len(LEFT) * WIDTH
    shape = (WIDTH, HALF)
    row, lane = iota(shape, 0), iota(shape, 1)
    work = jnp.where((lane % WIDTH == row) & (lane < copies), 1.0, 0.0)
    columns = [jnp.broadcast_to(gram[:, k : k + 1], shape) for k in range(WIDTH)]
    roots = jnp.zeros(shape, F32)
    for k in range(WIDTH):
        pivot = jnp.broadcast_to(columns[k][k : k + 1, :], shape)
        roots = jnp.where(row == k, 1.0 / jnp.sqrt(pivot), roots)
        if k == WIDTH - 1:
            break
        factor = jnp.where(row > k, columns[k] * (1.0 / pivot), 0.0)
        for j in range(k + 1, WIDTH):
            columns[j] = columns[j] - factor * jnp.broadcast_to(columns[j][k : k + 1, :], shape)
        work = work - factor * jnp.broadcast_to(work[k : k + 1, :], shape)
    inverse = work * roots
    high, middle, low = (part.astype(F32) for part in split3(inverse))
    part = lane // WIDTH
    chosen = jnp.where((part == 2) | (part == 4), middle, jnp.where(part == 5, low, high))
    return chosen.astype(BF16)[:, 0:copies]


class Place:
    def __init__(self):
        self.me, self.z = lax.axis_index("rows"), lax.axis_index("cols")
        self.core, self.y, self.x = self.me % NCORE, (self.me // NCORE) % NY, self.me // (NCORE * NY)
        self.cores = [(self.core + d) % NCORE for d in range(NCORE)]
        self.ys = [((self.y + d) % NY) * NCORE for d in range(NY)]
        self.xs = [((self.x + d) % NX) * (NY * NCORE) for d in range(NX)]
        self.zs = [(self.z + d) % SPLITS for d in range(SPLITS)]

    def plane(self, offset):
        return self.xs[offset // (NCORE * NY)] + self.ys[(offset // NCORE) % NY] + self.cores[offset % NCORE]

    def split(self, dz):
        return self.zs[dz]

    def near(self, offset):
        return self.xs[0] + self.ys[0] + self.cores[offset % NCORE], self.zs[offset // NCORE]

    def far(self, offset):
        return self.xs[offset // NY] + self.ys[offset % NY] + self.core, self.z


def copy_to(source, target, send_sem, recv_sem, row, split):
    return pltpu.make_async_remote_copy(
        src_ref=source, dst_ref=target, send_sem=send_sem, recv_sem=recv_sem,
        device_id=(row, split), device_id_type=MESH,
    )


def wait_all(ref, send_sem, recv_sem, place):
    copy_to(ref, ref, send_sem, recv_sem, place.me, place.z).wait()


def loop(start, stop, body):
    def step(i, carry):
        body(i)
        return carry

    lax.fori_loop(start, stop, step, 0)


def whole_kernel(
    groups_h, local_coords_h, remote_coords_h, local_gains_h, remote_gains_h, start_h, local_w, remote_w,
    out,
    groups, local_coords, remote_coords, local_gains, remote_gains, start,
    eff, table_v, table, column_sums, sums, deg_out, deg_in, split_part, inv, spread, gather, row_blocks,
    padded, answer_out, answer_in, product, product_out, product_in, fetched, total,
    parts, late, late_out, late_in, image, image_parts, near_gram, far_gram,
    load_sem, small_sem, table_sem, deg_sem, zdeg_sem, answer_sem, product_sem,
    part_sem, late_sem, image_sem, near_sem, far_sem,
):
    at = Place()
    me, z = at.me, at.z
    first = LT // CHUNK
    chunks = (LT + LOC) // CHUNK

    def load(c):
        chunk = pl.ds(c * CHUNK, CHUNK)
        source = remote_w.at[chunk] if c < first else local_w.at[pl.ds((c - first) * CHUNK, CHUNK)]
        return pltpu.make_async_copy(source, eff.at[chunk], load_sem.at[c])

    small = [
        pltpu.make_async_copy(source, target, small_sem.at[i])
        for i, (source, target) in enumerate(
            [
                (groups_h, groups), (remote_coords_h, remote_coords), (local_coords_h, local_coords),
                (remote_gains_h, remote_gains), (local_gains_h, local_gains), (start_h, start),
            ]
        )
    ]
    for copy in small[:4]:
        copy.start()
    for c in range(first):
        load(c).start()

    barrier = pltpu.get_barrier_semaphore()
    greeted = [(at.plane(o), z) for o in PLANE] + [at.near(o) for o in NEAR if o >= NCORE]

    def pair(p):
        return pl.ds(MOST * p, MOST)

    ones = jnp.ones((8, TILE), BF16)

    def scale(tile0, gains, gain0, row_at, keep, col_at):
        row_gains = jnp.concatenate([gains[gain0 + t, 0:1, :] for t in range(CHUNK)], axis=0).T
        for t in range(CHUNK):
            scaled = (
                row_gains[:, t : t + 1] * eff[tile0 + t].astype(F32) * gains[gain0 + t, 1:2, :]
            ).astype(BF16)
            eff[tile0 + t] = scaled
            size = jnp.abs(scaled)
            sums[pl.ds(row_at + t, 1), :] = dot(ones, size, ((1,), (1,)))[0:1, :]
            keep(col_at + t, dot(ones, size))

    def remote_chunk(c):
        chunk = pl.ds(c * CHUNK, CHUNK)
        pltpu.make_async_copy(remote_w.at[chunk], eff.at[chunk], load_sem.at[c]).wait()

        def keep(t, value):
            column_sums[pl.ds(t, 1), :] = value[0:1, :]

        scale(c * CHUNK, remote_gains, c * CHUNK, c * CHUNK, keep, c * CHUNK)

    def local_chunk(c):
        pltpu.make_async_copy(
            local_w.at[pl.ds(c * CHUNK, CHUNK)],
            eff.at[pl.ds(LT + c * CHUNK, CHUNK)],
            load_sem.at[first + c],
        ).wait()

        def keep(t, value):
            sums[pl.ds(t, 1), :] = value[0:1, :]

        scale(LT + c * CHUNK, local_gains, c * CHUNK, LT + c * CHUNK, keep, LT + LOC + c * CHUNK)

    def make_tables():
        for copy in small[:3]:
            copy.wait()
        group = jnp.broadcast_to(groups[...], (GROUPS, LT))
        slot_group, tile_id = iota((GROUPS, LT), 0), iota((GROUPS, LT), 1)
        named = group == slot_group
        lowest = jnp.min(jnp.where(named, tile_id, LT - 1), axis=1, keepdims=True)
        highest = jnp.max(jnp.where(named, tile_id, -1), axis=1, keepdims=True)
        is_first, is_second = named & (tile_id == lowest), named & (tile_id == highest)
        slot = MOST * slot_group + jnp.where(is_second, 1, 0)
        named_t = jnp.transpose(group) == iota((LT, GROUPS), 1)
        tile_t = iota((LT, GROUPS), 0)
        table_v[...] = jnp.zeros_like(table_v)
        table_v[T_REMOTE_ROW : T_REMOTE_ROW + 2, 0:LT] = remote_coords[...]
        table_v[T_LOCAL_ROW : T_LOCAL_ROW + 2, 0:LOC] = local_coords[...]
        table_v[T_SLOT : T_SLOT + 1, 0:LT] = jnp.sum(jnp.where(named, slot, 0), axis=0, keepdims=True)
        table_v[T_FIRST : T_FIRST + 1, 0:GROUPS] = jnp.min(jnp.where(named_t, tile_t, LT - 1), axis=0, keepdims=True)
        table_v[T_FIRST + 1 : T_FIRST + 2, 0:GROUPS] = jnp.max(jnp.where(named_t, tile_t, 0), axis=0, keepdims=True)
        table_copy = pltpu.make_async_copy(table_v, table, table_sem.at[0])
        table_copy.start()
        hot_slots = jnp.concatenate([jnp.where(hot, 1.0, 0.0) for hot in (is_first, is_second)], axis=0)
        target = jnp.broadcast_to(remote_coords[1:2, :].astype(F32) + 1.0, (MOST * GROUPS, LT))
        slot_column = jnp.sum(hot_slots * target, axis=1, keepdims=True) - 1.0
        slot_column = jnp.broadcast_to(slot_column, (MOST * GROUPS, HALF))
        return hot_slots.astype(BF16), slot_column, table_copy

    share = -(-len(greeted) // (first - 1))
    later = [load(c) for c in range(first, chunks)] + small[4:]
    for c in range(first):
        for row, split in greeted[c * share : (c + 1) * share]:
            pl.semaphore_signal(barrier, inc=1, device_id=(row, split), device_id_type=MESH)
        for copy in later[c * 2 : c * 2 + 2]:
            copy.start()
        if c == 0:
            tables = make_tables()
            small[3].wait()
        remote_chunk(c)

    hot_slots, slot_column, table_copy = tables
    pl.semaphore_wait(barrier, GROUPS - 1 + NCORE * SPLITS - 2)

    lanes = iota((1, HALF), 1)
    slot_sums = select_sum(hot_slots, column_sums[...])
    for p in range(GROUPS):
        pieces = []
        for s in range(MOST):
            row = slot_sums[s * GROUPS + p : s * GROUPS + p + 1, :]
            pieces += [row[:, 0:HALF], row[:, HALF:TILE]]
        columns = [slot_column[s * GROUPS + p : s * GROUPS + p + 1, :] for s in range(MOST)]
        by_lane = jnp.where(lanes % 8 < 2, columns[0], jnp.where(lanes % 8 < 4, columns[1], -1.0))
        deg_out[p] = jnp.concatenate(pieces + [by_lane, *columns, jnp.zeros((1, HALF), F32)], axis=0)
    for o in PLANE:
        to = at.plane(o)
        copy_to(deg_out.at[to], deg_in.at[me], deg_sem.at[0], deg_sem.at[1], to, z).start()
    deg_in[me] = deg_out[me]
    small[4].wait()
    for c in range(LOC // CHUNK):
        local_chunk(c)
    small[5].wait()
    table_copy.wait()

    def hot_rows(row):
        return jnp.where(jnp.broadcast_to(row, (BR, row.shape[1])) == iota((BR, row.shape[1]), 0), 1.0, 0.0).astype(BF16)

    own = select_sum(hot_rows(remote_coords[0:1, :]), sums[0:LT, :])
    own += select_sum(hot_rows(local_coords[0:1, :]), sums[LT : LT + LOC, :])
    own += select_sum(hot_rows(local_coords[1:2, :]), sums[LT + LOC : LT + 2 * LOC, :])
    wait_all(deg_in.at[pl.ds(0, GROUPS - 1)], deg_sem.at[0], deg_sem.at[1], at)
    came = deg_in[...].reshape(GROUPS * 8, HALF)
    blocks = []
    for b in range(GROUPS * 8 // HALF):
        column = jnp.full((1, HALF), -1.0, F32)
        for i in range(HALF // 8):
            column = jnp.where(lanes // 8 == i, deg_in[b * (HALF // 8) + i, 4:5, :], column)
        blocks.append(column)
    column = jnp.broadcast_to(jnp.concatenate(blocks, axis=1), (2 * BR, GROUPS * 8))
    row, lane8 = iota(column.shape, 0), iota(column.shape, 1) % 4
    chosen = (column == (row % BR).astype(F32)) & (lane8 % 2 == row // BR)
    added = select_sum(jnp.where(chosen, 1.0, 0.0).astype(BF16), came)
    split_part[z] = own + jnp.concatenate([added[0:BR, :], added[BR : 2 * BR, :]], axis=1)

    for dz in DZ:
        copy_to(split_part.at[z], split_part.at[z], zdeg_sem.at[0], zdeg_sem.at[1], me, at.split(dz)).start()

    padded[...] = jnp.zeros_like(padded)
    fetched[...] = jnp.zeros_like(fetched)
    row = iota((BR * WIDTH, HALF), 0)
    lane = iota((BR * WIDTH, HALF), 1)
    row_tile = (row // WIDTH).astype(F32)
    per = HALF // WIDTH
    for q in range(GROUPS * MOST // per):
        column = jnp.zeros((1, HALF), F32)
        for i in range(per):
            at_slot = deg_in[q * (per // MOST) + i // MOST, 5 + i % MOST : 6 + i % MOST, :]
            column = jnp.where(lanes // WIDTH == i, at_slot, column)
        chosen = (jnp.broadcast_to(column, row.shape) == row_tile) & (lane % WIDTH == row % WIDTH)
        spread[:, q * HALF : (q + 1) * HALF] = jnp.where(chosen, 1.0, 0.0).astype(BF16)
    lane = iota((WIDTH, TILE), 1)
    diagonal = lane % WIDTH == iota((WIDTH, TILE), 0)
    lane_tile = (lane // WIDTH).astype(F32)
    for slot in range(GROUPS * MOST):
        own = deg_in[slot // MOST, 5 + slot % MOST : 6 + slot % MOST, :]
        own = jnp.broadcast_to(jnp.concatenate([own, own], axis=1), (WIDTH, TILE))
        gather[slot * WIDTH : (slot + 1) * WIDTH, :] = jnp.where(diagonal & (own == lane_tile), 1.0, 0.0).astype(BF16)

    wait_all(split_part.at[pl.ds(0, SPLITS - 1)], zdeg_sem.at[0], zdeg_sem.at[1], at)
    inv[...] = 1.0 / jnp.sqrt((split_part[0] + split_part[1]) + (split_part[2] + split_part[3]))

    def set_rows(j, vectors):
        scaled = (vectors * inv[j : j + 1, :]).astype(BF16)
        row_blocks[j] = scaled

    for j in range(BR):
        set_rows(j, start[:, j * TILE : (j + 1) * TILE])

    for it in range(ITERS):
        last = it == ITERS - 1
        a_in, p_in = answer_in.at[it], product_in.at[it]

        answer_out[...] = (
            dot(gather[...], row_blocks[...].reshape(BR * WIDTH, TILE)).astype(BF16).reshape(answer_out.shape)
        )

        for o in PLANE:
            to = at.plane(o)
            copy_to(
                answer_out.at[pair(to)], a_in.at[pair(me)], answer_sem.at[it, 0], answer_sem.at[it, 1], to, z
            ).start()
        a_in[pair(me)] = answer_out[pair(me)]

        def backward(i):
            for u in range(STEP):
                tile = i * STEP + u
                x = row_blocks[table[T_REMOTE_ROW, tile]]
                product[tile] = dot(x, eff[tile]).astype(BF16)

        loop(0, LT // STEP, backward)

        def fill_product(p, ref):
            for s in range(MOST):
                ref[MOST * p + s] = product[table[T_FIRST + s, p]]

        for o in PLANE:
            to = at.plane(o)
            fill_product(to, product_out)
            copy_to(
                product_out.at[pair(to)], p_in.at[pair(me)], product_sem.at[it, 0], product_sem.at[it, 1], to, z
            ).start()
        fill_product(me, p_in)

        for j in range(BR):
            padded[j, PAD] = row_blocks[j]

        total[...] = jnp.zeros_like(total)

        def window(ref, index, row_tile):
            return ref[index, pl.ds(PAD - row_tile, BR)].reshape(BR * WIDTH, TILE)

        def local(i):
            value = total[...]
            for u in range(STEP):
                tile = i * STEP + u
                r, c = table[T_LOCAL_ROW, tile], table[T_LOCAL_COL, tile]
                value += dot(window(padded, c, r), eff[LT + tile], ((1,), (1,)))
                value += dot(window(padded, r, c), eff[LT + tile])
            total[...] = value

        loop(0, LOC // STEP, local)

        for dz in DZ:
            other = at.split(dz)
            copy_to(
                total.at[pl.ds(other * QROWS, QROWS)], parts.at[it, dz], part_sem.at[it, 0], part_sem.at[it, 1], me, other
            ).start()
        late[...] = jnp.zeros_like(late)

        others = pl.ds(0, MOST * (GROUPS - 1))
        wait_all(a_in.at[others], answer_sem.at[it, 0], answer_sem.at[it, 1], at)

        def forward(i):
            value = late[...]
            for u in range(STEP):
                tile = i * STEP + u
                slot = table[T_SLOT, tile]
                fetched[u, PAD] = a_in[slot]
                value += dot(window(fetched, u, table[T_REMOTE_ROW, tile]), eff[tile], ((1,), (1,)))
            late[...] = value

        loop(0, LT // STEP, forward)

        wait_all(p_in.at[others], product_sem.at[it, 0], product_sem.at[it, 1], at)
        came = p_in[...].reshape(GROUPS * MOST * WIDTH, TILE)
        for dz in (*DZ, 0):
            other = at.split(dz)
            rows = pl.ds(pl.multiple_of(other * QROWS, QROWS), QROWS)
            rest = late[rows, :] + dot(spread[rows, :], came)
            if dz:
                late_out[rows, :] = rest.astype(BF16)
                copy_to(
                    late_out.at[rows], late_in.at[it, dz], late_sem.at[it, 0], late_sem.at[it, 1], me, other
                ).start()
        mine = pl.ds(z * QROWS, QROWS)
        wait_all(parts.at[it, pl.ds(1, SPLITS - 1)], part_sem.at[it, 0], part_sem.at[it, 1], at)
        summed = (total[mine, :] + rest) + ((parts[it, 1] + parts[it, 2]) + parts[it, 3])
        wait_all(late_in.at[it, pl.ds(1, SPLITS - 1)], late_sem.at[it, 0], late_sem.at[it, 1], at)
        summed += (late_in[it, 1].astype(F32) + late_in[it, 2].astype(F32)) + late_in[it, 3].astype(F32)
        tiles = [
            summed[j * WIDTH : (j + 1) * WIDTH, :] * inv[pl.ds(z * (BR // SPLITS) + j, 1), :]
            for j in range(BR // SPLITS)
        ]
        wide = jnp.concatenate(tiles, axis=1)
        wide_parts = split3(wide)
        gram = jnp.zeros((WIDTH, WIDTH), F32)
        for i in reversed(range(3)):
            left = jnp.concatenate(wide_parts[: 3 - i], axis=0)
            crossed = dot(left, wide_parts[i], ((1,), (1,)))
            for j in reversed(range(3 - i)):
                gram = gram + crossed[j * WIDTH : (j + 1) * WIDTH, :]
        packed = jnp.concatenate([gram[0:8], gram[8:16], jnp.zeros((8, HALF - 2 * WIDTH), F32)], axis=1)

        own = z * NCORE + at.core
        near_gram[it, own] = packed
        for offset in NEAR:
            row, split = at.near(offset)
            copy_to(
                near_gram.at[it, own], near_gram.at[it, own], near_sem.at[it, 0], near_sem.at[it, 1], row, split
            ).start()
        if not last:
            image[mine, :] = jnp.concatenate(tiles, axis=0)
            for dz in DZ:
                copy_to(image.at[mine], image.at[mine], image_sem.at[0], image_sem.at[1], me, at.split(dz)).start()
        wait_all(near_gram.at[it, pl.ds(0, NCORE * SPLITS - 1)], near_sem.at[it, 0], near_sem.at[it, 1], at)
        near_sum = near_gram[it, 0]
        for i in range(1, NCORE * SPLITS):
            near_sum = near_sum + near_gram[it, i]

        own = at.x * NY + at.y
        far_gram[it, own] = near_sum
        for offset in FAR:
            row, split = at.far(offset)
            copy_to(
                far_gram.at[it, own], far_gram.at[it, own], far_sem.at[it, 0], far_sem.at[it, 1], row, split
            ).start()
        if not last:
            wait_all(image.at[pl.ds(0, (SPLITS - 1) * QROWS)], image_sem.at[0], image_sem.at[1], at)
            for j in range(BR):
                pieces = split3(image[j * WIDTH : (j + 1) * WIDTH, :])
                image_parts[j] = jnp.concatenate([pieces[i] for i in RIGHT], axis=0)
        wait_all(far_gram.at[it, pl.ds(0, NX * NY - 1)], far_sem.at[it, 0], far_sem.at[it, 1], at)
        packed = far_gram[it, 0]
        for i in range(1, NX * NY):
            packed = packed + far_gram[it, i]
        gram = jnp.concatenate([packed[:, 0:WIDTH], packed[:, WIDTH : 2 * WIDTH]], axis=0)
        inverse = factor_inverse(gram / VERTICES)
        if last:
            out[...] = dot(inverse, jnp.concatenate([wide_parts[i] for i in RIGHT], axis=0))
        else:
            for j in range(BR):
                set_rows(j, dot(inverse, image_parts[j]))


def per_device(
    local_weights, local_gains, local_coords, remote_weights, remote_gains, remote_groups, remote_coords, start_block
):
    dma = pltpu.SemaphoreType.DMA
    return pl.pallas_call(
        whole_kernel,
        out_shape=pltpu.VMEM((WIDTH, QROWS // WIDTH * TILE), F32),
        in_specs=[HBM] * 8,
        out_specs=VMEM,
        scratch_shapes=[
            pltpu.VMEM((1, LT), jnp.int32),
            pltpu.VMEM((2, LOC), jnp.int32),
            pltpu.VMEM((2, LT), jnp.int32),
            pltpu.VMEM((LOC, 2, TILE), F32),
            pltpu.VMEM((LT, 2, TILE), F32),
            pltpu.VMEM((WIDTH, BR * TILE), F32),
            pltpu.VMEM((LT + LOC, TILE, TILE), BF16),
            pltpu.VMEM((8, HALF), jnp.int32),
            pltpu.SMEM((8, HALF), jnp.int32),
            pltpu.VMEM((LT, TILE), F32),
            pltpu.VMEM((LT + 2 * LOC, TILE), F32),
            pltpu.VMEM((GROUPS, 8, HALF), F32),
            pltpu.VMEM((GROUPS, 8, HALF), F32),
            pltpu.VMEM((SPLITS, BR, TILE), F32),
            pltpu.VMEM((BR, TILE), F32),
            pltpu.VMEM((BR * WIDTH, GROUPS * MOST * WIDTH), BF16),
            pltpu.VMEM((GROUPS * MOST * WIDTH, BR * WIDTH), BF16),
            pltpu.VMEM((BR, WIDTH, TILE), BF16),
            pltpu.VMEM((BR, 2 * PAD + 1, WIDTH, TILE), BF16),
            pltpu.VMEM((GROUPS * MOST, WIDTH, TILE), BF16),
            pltpu.VMEM((ITERS, GROUPS * MOST, WIDTH, TILE), BF16),
            pltpu.VMEM((LT, WIDTH, TILE), BF16),
            pltpu.VMEM((GROUPS * MOST, WIDTH, TILE), BF16),
            pltpu.VMEM((ITERS, GROUPS * MOST, WIDTH, TILE), BF16),
            pltpu.VMEM((STEP, 2 * PAD + 1, WIDTH, TILE), BF16),
            pltpu.VMEM((BR * WIDTH, TILE), F32),
            pltpu.VMEM((ITERS, SPLITS, QROWS, TILE), F32),
            pltpu.VMEM((BR * WIDTH, TILE), F32),
            pltpu.VMEM((BR * WIDTH, TILE), BF16),
            pltpu.VMEM((ITERS, SPLITS, QROWS, TILE), BF16),
            pltpu.VMEM((BR * WIDTH, TILE), F32),
            pltpu.VMEM((BR, len(RIGHT) * WIDTH, TILE), BF16),
            pltpu.VMEM((ITERS, NCORE * SPLITS, 8, HALF), F32),
            pltpu.VMEM((ITERS, NX * NY, 8, HALF), F32),
            dma(((LT + LOC) // CHUNK,)),
            dma((6,)),
            dma((1,)),
            dma((2,)),
            dma((2,)),
            dma((ITERS, 2)),
            dma((ITERS, 2)),
            dma((ITERS, 2)),
            dma((ITERS, 2)),
            dma((2,)),
            dma((ITERS, 2)),
            dma((ITERS, 2)),
        ],
        compiler_params=pltpu.CompilerParams(
            collective_id=0, has_side_effects=True, vmem_limit_bytes=60 << 20
        ),
        name="iterate",
    )(
        remote_groups[0], local_coords[0, 0].T, remote_coords[0, 0].T, local_gains[0, 0], remote_gains[0, 0],
        start_block, local_weights[0, 0], remote_weights[0, 0],
    )


def solution(mesh):
    in_specs = (
        P("rows", "cols", None, None, None),
        P("rows", "cols", None, None, None),
        P("rows", "cols", None, None),
        P("rows", "cols", None, None, None),
        P("rows", "cols", None, None, None),
        P("rows", "cols", None),
        P("rows", "cols", None, None),
        P(None, "rows"),
    )
    out_specs = P(None, ("rows", "cols"))
    return jax.shard_map(
        per_device, mesh=mesh, in_specs=in_specs, out_specs=out_specs, check_vma=False
    )
```
